128 devices in a mesh: row: 16 (over x, z), col: 8 (over y, core).
Axes of the slice: x: 4, y: 4, z: 4, core: 2. Of those that a mesh axis runs over, the one named last changes fastest.
Arguments:
- sources: float32 [3, 8192, 2048], P(None, 'row', 'col'), may hold values from -1.5 to 1.5
- edge_codes: int32 [2, 8192, 2048], P(None, 'row', 'col'), may hold values from 0 to 15
- seam_labels: int32 [8192, 2048], P('row', 'col'), may hold values from 0 to 4, as said below
Outputs:
- solution: float32 [3, 8192, 2048], P(None, 'row', 'col')
- residual: float32 [3, 8192, 2048], P(None, 'row', 'col')
The draws below stay inside these ranges and needn't reach their ends.
Inputs may be any that keep to these rules, and one draw needn't show every extreme that they name: `seam_labels`: label of the source image from which each pixel was taken.
All inputs are finite; a program needn't handle non-finite values.
Results may differ from the reference program's by a relative error of at most 0.00085.
Values sent between devices are 32-bit elements; how exact they have to be, the bound alone decides.
A program may use at most 192 MiB of HBM per device.

```python
import math
import jax
import jax.numpy as jnp
from jax import lax

CHANNELS = 3
SWEEPS = 4
CYCLES = 2
IMG_ROWS = 8192
IMG_COLS = 2048


def draw_seam_labels(key, part):
    key_rows, key_cols = jax.random.split(jax.random.fold_in(key, 17))
    row_cuts = (jax.random.randint(key_rows, (IMG_ROWS,), 0, 12) == 0).astype(jnp.int32)
    col_cuts = (jax.random.randint(key_cols, (IMG_COLS,), 0, 12) == 0).astype(jnp.int32)
    row_ids = jnp.cumsum(row_cuts)
    col_ids = jnp.cumsum(col_cuts)
    return ((7 * row_ids[:, None] + 3 * col_ids[None, :]) % 5).astype(jnp.int32)


def touch_ends(values, key, low, top_value):
    spot = [jax.random.randint(jax.random.fold_in(key, axis), (), 0, length) for axis, length in enumerate(values.shape)]
    widest = values.shape.index(max(values.shape))
    next_to = spot[:widest] + [(spot[widest] + 1) % values.shape[widest]] + spot[widest + 1:]
    return values.at[tuple(spot)].set(low).at[tuple(next_to)].set(top_value)


def levels(rng, shape, cuts, low, largest):
    loudness = 1.0
    for dim, shards_of in cuts:
        steps = jax.random.uniform(jax.random.fold_in(jax.random.fold_in(rng, 6), dim), (shards_of,), jnp.float32, low / len(cuts), largest / len(cuts))
        loudness = loudness * jnp.repeat(jnp.exp(steps), shape[dim] // shards_of).reshape((-1,) + (1,) * (len(shape) - 1 - dim))
    return loudness


def centred(stream_key, shape, spread, limit, pieces=(), kind=jnp.bfloat16):
    values = spread * jax.random.normal(stream_key, shape, jnp.float32)
    if pieces:
        values = values * levels(stream_key, shape, pieces, -0.22, 0.18)
    return jnp.clip(values, -limit, limit).astype(kind)


def setup_inputs(seed: int = 0) -> dict:
    seeds = jax.random.split(jax.random.key(seed), 4)
    sources = centred(seeds[0], (CHANNELS, IMG_ROWS, IMG_COLS), 0.25, 1.5, ((1, 16), (2, 8)), jnp.float32)
    edge_codes = touch_ends(jax.random.randint(seeds[1], (2, IMG_ROWS, IMG_COLS), 0, 16), jax.random.fold_in(seeds[1], 1), 0, 15).astype(jnp.int32)
    seam_labels = draw_seam_labels(jax.random.fold_in(seeds[3], 71), 0)
    return dict(sources=sources, edge_codes=edge_codes, seam_labels=seam_labels)


screen = 2e-05
seam_factor = 0.2
coarse_scale = 0.0625

def chebyshev_weight(sweep_index):
    return 1.0 / (1.25 + 0.75 * math.cos(math.pi * (2 * sweep_index + 1) / (2 * SWEEPS)))

def edge_weight(code, left_label, right_label):
    strength = jnp.exp2(code.astype(jnp.float32) * 0.25 - 2.0)
    return strength * jnp.where(left_label != right_label, seam_factor, 1.0).astype(jnp.float32)

def fine_faces(edge_codes, seam_labels):
    inner_x = edge_weight(edge_codes[0][:, :-1], seam_labels[:, :-1], seam_labels[:, 1:])
    inner_y = edge_weight(edge_codes[1][:-1, :], seam_labels[:-1, :], seam_labels[1:, :])
    face_x = jnp.pad(inner_x, ((0, 0), (1, 1)), constant_values=1.0)
    face_y = jnp.pad(inner_y, ((1, 1), (0, 0)), constant_values=1.0)
    return (face_x, face_y)

def coarsen_faces(face_x, face_y):
    picked_x = face_x[:, ::4]
    new_x = picked_x.reshape(picked_x.shape[0] // 4, 4, picked_x.shape[1]).sum(axis=1) / 16.0
    picked_y = face_y[::4, :]
    new_y = picked_y.reshape(picked_y.shape[0], picked_y.shape[1] // 4, 4).sum(axis=2) / 16.0
    return (new_x, new_y)

def cell_weights(face_x, face_y):
    weights = jnp.stack([face_x[:, :-1], face_x[:, 1:], face_y[:-1, :], face_y[1:, :]])
    diagonal = screen + weights[0] + weights[1] + weights[2] + weights[3]
    return (weights, diagonal)

def apply_cells(padded, weights, diagonal):
    centre = padded[:, 1:-1, 1:-1]
    result = diagonal * centre - weights[0] * padded[:, 1:-1, :-2] - weights[1] * padded[:, 1:-1, 2:]
    return result - weights[2] * padded[:, :-2, 1:-1] - weights[3] * padded[:, 2:, 1:-1]

def zero_pad(current):
    return jnp.pad(current, ((0, 0), (1, 1), (1, 1)))

def smooth(current, source, weights, diagonal, from_zero):
    for sweep_index in range(SWEEPS):
        omega = chebyshev_weight(sweep_index)
        if sweep_index == 0 and from_zero:
            current = omega * source / diagonal
        else:
            current = current + omega * (source - apply_cells(zero_pad(current), weights, diagonal)) / diagonal
    return current

def block_mean(current):
    shape = current.shape
    return current.reshape(shape[0], shape[1] // 4, 4, shape[2] // 4, 4).mean(axis=(2, 4))

def expand(current):
    return jnp.repeat(jnp.repeat(current, 4, axis=1), 4, axis=2)

def sine_table(first, count, extent):
    rows_idx = first + jnp.arange(count, dtype=jnp.int32) + 1
    cols_idx = jnp.arange(extent, dtype=jnp.int32) + 1
    product = rows_idx[:, None] * cols_idx[None, :] % (2 * (extent + 1))
    return math.sqrt(2.0 / (extent + 1)) * jnp.sin(jnp.pi * product.astype(jnp.float32) / (extent + 1))

def eigen_values(row_first, row_count, row_extent, col_first, col_count, col_extent):
    row_modes = (row_first + jnp.arange(row_count, dtype=jnp.int32) + 1).astype(jnp.float32)
    col_modes = (col_first + jnp.arange(col_count, dtype=jnp.int32) + 1).astype(jnp.float32)
    row_part = 2.0 - 2.0 * jnp.cos(jnp.pi * row_modes / (row_extent + 1))
    col_part = 2.0 - 2.0 * jnp.cos(jnp.pi * col_modes / (col_extent + 1))
    return screen + coarse_scale * (row_part[:, None] + col_part[None, :])

def coarse_solve(source):
    count_rows, count_cols = (source.shape[1], source.shape[2])
    table_rows = sine_table(0, count_rows, count_rows)
    table_cols = sine_table(0, count_cols, count_cols)
    highest = lax.Precision.HIGHEST
    spectrum = jnp.einsum('cij,jl->cil', source, table_cols, precision=highest)
    spectrum = jnp.einsum('ki,cij->ckj', table_rows, spectrum, precision=highest)
    scaled = spectrum / eigen_values(0, count_rows, count_rows, 0, count_cols, count_cols)
    back = jnp.einsum('ki,cij->ckj', table_rows, scaled, precision=highest)
    return jnp.einsum('cij,jl->cil', back, table_cols, precision=highest)

def reference(sources, edge_codes, seam_labels):
    face_x, face_y = fine_faces(edge_codes, seam_labels)
    fine_w, fine_diag = cell_weights(face_x, face_y)
    level_x, level_y = coarsen_faces(face_x, face_y)
    level_w, level_diag = cell_weights(level_x, level_y)
    solution = jnp.zeros_like(sources)
    for cycle_index in range(CYCLES):
        solution = smooth(solution, sources, fine_w, fine_diag, cycle_index == 0)
        fine_res = sources - apply_cells(zero_pad(solution), fine_w, fine_diag)
        level_src = block_mean(fine_res)
        level_field = smooth(jnp.zeros_like(level_src), level_src, level_w, level_diag, True)
        level_res = level_src - apply_cells(zero_pad(level_field), level_w, level_diag)
        correction = coarse_solve(block_mean(level_res))
        level_field = smooth(level_field + expand(correction), level_src, level_w, level_diag, False)
        solution = smooth(solution + expand(level_field), sources, fine_w, fine_diag, False)
    residual = sources - apply_cells(zero_pad(solution), fine_w, fine_diag)
    return (solution, residual)
```

```python
import functools
import math

import jax
import jax.numpy as jnp
import numpy as np
from jax import lax
from jax.experimental import pallas as pl
from jax.experimental.pallas import tpu as pltpu
from jax.sharding import PartitionSpec as P

SWEEPS = 4
SCREEN = 2e-05
SEAM = 0.2
COARSE_SCALE = 0.0625
F32 = jnp.float32
MESH = pl.DeviceIdType.MESH
HIGHEST = lax.Precision.HIGHEST

ROWS, COLS = 512, 256
PAD = 48
HALO = 32
K = (ROWS + 2 * PAD) // 8
NAT = 8 + ROWS + 2 * PAD + 8
LROWS, LCOLS = 128, 64
LPAD = PAD // 4
LHALO = 16
KL = (LROWS + 2 * LPAD) // 8
LNAT = LROWS + 2 * LHALO
CROWS, CCOLS = 32, 16
BROWS = CROWS + 16
VMEM_LIMIT = 62 * 1024 * 1024


def chebyshev_weight(sweep_index):
    return 1.0 / (1.25 + 0.75 * math.cos(math.pi * (2 * sweep_index + 1) / (2 * SWEEPS)))


def lane_iota():
    return lax.broadcasted_iota(jnp.int32, (8, 128), 1)


def sub_iota():
    return lax.broadcasted_iota(jnp.int32, (8, 128), 0)


def lroll(x, shift):
    shift = shift % 128
    return x if shift == 0 else pltpu.roll(x, shift, 1)


def rows8(k):
    return pl.ds(pl.multiple_of(k * 8, 8), 8)


def lanes_take(x, idx):
    return jnp.take_along_axis(x, idx, axis=1)


def left_of(tiles, lane):
    rolled = [lroll(x, 1) for x in tiles]
    return [jnp.where(lane == 0, rolled[(t + 2) % 3], rolled[t]) for t in range(3)]


def right_of(tiles, lane):
    rolled = [lroll(x, 127) for x in tiles]
    return [jnp.where(lane == 127, rolled[(t + 1) % 3], rolled[t]) for t in range(3)]


def set_pads(ref, lead, count):
    last = ref[lead + (rows8(count), slice(None))]
    first = ref[lead + (rows8(1), slice(None))]
    ref[lead + (rows8(0), slice(None))] = pltpu.roll(last, 1, 0)
    ref[lead + (rows8(count + 1), slice(None))] = pltpu.roll(first, 7, 0)


def pack_fine(tile_of, n_arrays, right, left, lane, rows):
    def body(i, carry):
        r = rows8(i)
        for first in range(0, n_arrays, 4):
            out_r = out_l = jnp.zeros((8, 128), F32)
            for a in range(first, min(first + 4, n_arrays)):
                g = a - first
                here = (lane >= 32 * g) & (lane < 32 * g + 32)
                out_r = jnp.where(here, lroll(tile_of(a, 1, r), 32 * g - 96), out_r)
                out_l = jnp.where(here, lroll(tile_of(a, 0, r), 32 * g), out_l)
            right[first // 4, r, :] = out_r
            left[first // 4, r, :] = out_l
        return carry

    lax.fori_loop(0, rows // 8, body, 0)


def unpack_fine(nat, n_arrays, at, count, from_left, from_right, lane):
    def body(i, carry):
        src = rows8(i)
        dst = pl.ds(pl.multiple_of(at + i * 8, 8), 8)
        for a in range(n_arrays):
            g = a % 4
            l = lroll(from_left[a // 4, src, :], 96 - 32 * g)
            r = lroll(from_right[a // 4, src, :], -32 * g)
            nat[a, 2, dst, :] = jnp.where(lane < 32, r, jnp.where(lane >= 96, l, 0.0))
        return carry

    lax.fori_loop(0, count, body, 0)


def zero_ends(nat, n_arrays):
    zero = jnp.zeros((8, 128), F32)
    for a in range(n_arrays):
        for t in range(3):
            for r in (0, 8, 16, NAT - 24, NAT - 16, NAT - 8):
                nat[a, t, r : r + 8, :] = zero


def unpack_columns(nat, n_arrays, cols, corners, lane):
    unpack_fine(nat, n_arrays, 8 + PAD, ROWS // 8, cols.at[0], cols.at[1], lane)
    unpack_fine(nat, n_arrays, 8 + PAD - HALO, HALO // 8, corners.at[0], corners.at[1], lane)
    unpack_fine(nat, n_arrays, 8 + PAD + ROWS, HALO // 8, corners.at[2], corners.at[3], lane)


def fine_inside(k, t, lane, sub, row0, col0, n_rows, n_cols):
    row = row0 - PAD + sub * K + k
    if t < 2:
        col = lane + (col0 + 128 * t)
    else:
        col = jnp.where(lane < 64, lane + (col0 + 256), lane + (col0 - 128))
    return (row >= 0) & (row < n_rows) & (col >= 0) & (col < n_cols), row, col


def level_inside(k, lane, sub, row0, col0, n_rows, n_cols):
    row = row0 - LPAD + sub * KL + k
    col = jnp.where(lane < 96, lane, lane - 128) + col0
    return (row >= 0) & (row < n_rows) & (col >= 0) & (col < n_cols)


def fine_neighbours(v, w, k, lane, ch):
    here = [v[ch, t, rows8(k + 1), :] for t in range(3)]
    left, right = left_of(here, lane), right_of(here, lane)
    total = []
    for t in range(3):
        up, down = v[ch, t, rows8(k), :], v[ch, t, rows8(k + 2), :]
        total.append(w[0][t] * left[t] + w[1][t] * right[t] + w[2][t] * up + w[3][t] * down)
    return here, total


def fine_weights_at(wt, k):
    return [[wt[n, t, rows8(k), :] for t in range(3)] for n in range(4)]


def fine_pads(v):
    for ch in range(3):
        for t in range(3):
            set_pads(v, (ch, t), K)


def fine_sweep(vin, vout, sp, wt, omega):
    lane = lane_iota()

    def body(k, carry):
        w = fine_weights_at(wt, k)
        for ch in range(3):
            here, total = fine_neighbours(vin, w, k, lane, ch)
            for t in range(3):
                new = sp[ch, t, rows8(k), :] + total[t]
                vout[ch, t, rows8(k + 1), :] = (1.0 - omega) * here[t] + omega * new
        return carry

    lax.fori_loop(0, K, body, 0, unroll=2)
    fine_pads(vout)


def fine_first(vout, sp):
    omega = chebyshev_weight(0)

    def body(k, carry):
        for ch in range(3):
            for t in range(3):
                vout[ch, t, rows8(k + 1), :] = omega * sp[ch, t, rows8(k), :]
        return carry

    lax.fori_loop(0, K, body, 0)
    fine_pads(vout)


def fine_smooth(va, vb, sp, wt, from_zero):
    bufs = [va, vb]
    at = 0
    for i in range(SWEEPS):
        if i == 0 and from_zero:
            fine_first(va, sp)
            continue
        fine_sweep(bufs[at], bufs[1 - at], sp, wt, chebyshev_weight(i))
        at = 1 - at
    return bufs[at], bufs[1 - at]


def to_level(x, lane, idx):
    got = []
    for y in x:
        y = y + lroll(y, 127)
        y = y + lroll(y, 126)
        got.append(lanes_take(y, idx))
    return jnp.where(lane < 32, got[0], jnp.where(lane < 64, got[1], got[2]))


def fine_residual_to_level(v, sp, wt, dg, lsrc):
    lane = lane_iota()
    idx = (4 * lane) % 128

    def body(kl, carry):
        acc = [[None] * 3 for _ in range(3)]
        for q in range(4):
            k = kl * 4 + q
            w = fine_weights_at(wt, k)
            for ch in range(3):
                here, total = fine_neighbours(v, w, k, lane, ch)
                for t in range(3):
                    res = dg[t, rows8(k), :] * (sp[ch, t, rows8(k), :] - here[t] + total[t])
                    acc[ch][t] = res if q == 0 else acc[ch][t] + res
        for ch in range(3):
            lsrc[ch, rows8(kl), :] = to_level(acc[ch], lane, idx) * 0.0625
        return carry

    lax.fori_loop(0, KL, body, 0)


def level_weights(fx, fy, lw, ld, li, where):
    lane, sub = lane_iota(), sub_iota()
    fy[rows8(KL), :] = pltpu.roll(fy[rows8(0), :], 7, 0)

    def body(k, carry):
        left, up, down = fx[rows8(k), :], fy[rows8(k), :], fy[rows8(k + 1), :]
        right = lroll(left, 127)
        diag = SCREEN + left + right + up + down
        inv = jnp.where(level_inside(k, lane, sub, *where), 1.0 / diag, 0.0)
        ld[rows8(k), :] = diag
        li[rows8(k), :] = inv
        for n, face in enumerate((left, right, up, down)):
            lw[n, rows8(k), :] = face * inv
        return carry

    lax.fori_loop(0, KL, body, 0)


def level_neighbours(f, lw, k, ch):
    here = f[ch, rows8(k + 1), :]
    total = lw[0, rows8(k), :] * lroll(here, 1) + lw[1, rows8(k), :] * lroll(here, 127)
    return here, total + lw[2, rows8(k), :] * f[ch, rows8(k), :] + lw[3, rows8(k), :] * f[ch, rows8(k + 2), :]


def level_pads(f):
    for ch in range(3):
        set_pads(f, (ch,), KL)


def level_smooth(fa, fb, lsp, lw, from_zero):
    bufs = [fa, fb]
    at = 0
    for i in range(SWEEPS):
        omega = chebyshev_weight(i)
        src, dst = bufs[at], bufs[1 - at]
        if i == 0 and from_zero:

            def first(k, carry):
                for ch in range(3):
                    src[ch, rows8(k + 1), :] = omega * lsp[ch, rows8(k), :]
                return carry

            lax.fori_loop(0, KL, first, 0)
            level_pads(src)
            continue

        def body(k, carry):
            for ch in range(3):
                here, total = level_neighbours(src, lw, k, ch)
                dst[ch, rows8(k + 1), :] = (1.0 - omega) * here + omega * (lsp[ch, rows8(k), :] + total)
            return carry

        lax.fori_loop(0, KL, body, 0)
        level_pads(dst)
        at = 1 - at
    return bufs[at]


def level_down(lsrc, li, ld, lw, lsp, fa, fb, lnat, lev, lpr, lpl, g):
    lane = lane_iota()

    def scale(k, carry):
        for ch in range(3):
            lsp[ch, rows8(k), :] = lsrc[ch, rows8(k), :] * li[rows8(k), :]
        return carry

    lax.fori_loop(0, KL, scale, 0)
    f = level_smooth(fa, fb, lsp, lw, True)

    def out(k, carry):
        at = pl.ds(LHALO - LPAD + k, 8, stride=KL)
        for ch in range(3):
            here, total = level_neighbours(f, lw, k, ch)
            lnat[8 + ch, at, :] = ld[rows8(k), :] * (lsp[ch, rows8(k), :] - here + total)
            lnat[ch, at, :] = here
            lnat[3 + ch, at, :] = lsrc[ch, rows8(k), :]
        return carry

    lax.fori_loop(0, KL, out, 0)

    def copy(i, carry):
        src = pl.ds(pl.multiple_of(LHALO + i * 8, 8), 8)
        right = left = jnp.zeros((8, 128), F32)
        for a in range(8):
            x = lnat[a, src, :]
            lev[a, rows8(i), :] = x
            here = (lane >= 16 * a) & (lane < 16 * a + 16)
            right = jnp.where(here, lroll(x, 16 * a - 48), right)
            left = jnp.where(here, lroll(x, 16 * a), left)
        lpr[rows8(i), :] = right
        lpl[rows8(i), :] = left
        return carry

    lax.fori_loop(0, LROWS // 8, copy, 0)
    idx = (4 * lane) % 128
    for i in range(CROWS // 8):
        total = jnp.zeros((8, 128), F32)
        for ch in range(3):
            x = sum(lnat[8 + ch, pl.ds(LHALO + 32 * i + q, 8, stride=4), :] for q in range(4))
            x = x + lroll(x, 127)
            x = x + lroll(x, 126)
            x = jnp.where(lane < CCOLS, lanes_take(x, idx), 0.0) * 0.0625
            total = total + lroll(x, CCOLS * ch)
        g[i * 8 : i * 8 + 8, :] = total


def level_up(lev, lrows, lcols, lcorn, corr, lnat, lnc, fx, fy, lw, ld, li, lsp, fa, fb, where):
    lane, sub = lane_iota(), sub_iota()

    def place(dst_row, count, own, left, right):
        def body(i, carry):
            dst = pl.ds(pl.multiple_of(dst_row + i * 8, 8), 8)
            l, r = left(rows8(i)), right(rows8(i))
            for a in range(8):
                x = jnp.where(lane < 64, own(a, rows8(i)), 0.0)
                x = jnp.where((lane >= 64) & (lane < 80), lroll(r, 64 - 16 * a), x)
                lnat[a, dst, :] = jnp.where(lane >= 112, lroll(l, 112 - 16 * a), x)
            return carry

        lax.fori_loop(0, count, body, 0)

    place(0, LHALO // 8, lambda a, r: lrows[0, a, r, :], lambda r: lcorn[0, r, :], lambda r: lcorn[1, r, :])
    place(LHALO, LROWS // 8, lambda a, r: lev[a, r, :], lambda r: lcols[0, r, :], lambda r: lcols[1, r, :])
    place(LHALO + LROWS, LHALO // 8, lambda a, r: lrows[1, a, r, :], lambda r: lcorn[2, r, :], lambda r: lcorn[3, r, :])
    for ch in range(3):
        for h in range(LNAT // 32):
            x = corr[ch, 4 + 8 * h : 12 + 8 * h, :]
            for q in range(4):
                lnc[ch, pl.ds(32 * h + q, 8, stride=4), :] = x

    def faces(k, carry):
        at = pl.ds(LHALO - LPAD + k, 8, stride=KL)
        fx[rows8(k), :] = lnat[6, at, :]
        fy[rows8(k), :] = lnat[7, at, :]
        return carry

    lax.fori_loop(0, KL, faces, 0)
    level_weights(fx, fy, lw, ld, li, where)

    def fields(k, carry):
        at = pl.ds(LHALO - LPAD + k, 8, stride=KL)
        inside = level_inside(k, lane, sub, *where)
        inv = li[rows8(k), :]
        for ch in range(3):
            fa[ch, rows8(k + 1), :] = jnp.where(inside, lnat[ch, at, :] + lnc[ch, at, :], 0.0)
            lsp[ch, rows8(k), :] = lnat[3 + ch, at, :] * inv
        return carry

    lax.fori_loop(0, KL, fields, 0)
    level_pads(fa)
    return level_smooth(fa, fb, lsp, lw, False)


def fine_up(v, vrows, vcols, vcorn, field, nat, va, where):
    lane, sub = lane_iota(), sub_iota()
    zero_ends(nat, 3)
    for ch in range(3):
        for t in range(2):
            nat[ch, t, 8 + PAD : 8 + PAD + ROWS, :] = v[ch, t]
            nat[ch, t, 8 + PAD - HALO : 8 + PAD, :] = vrows[0, ch, t]
            nat[ch, t, 8 + PAD + ROWS : 8 + PAD + ROWS + HALO, :] = vrows[1, ch, t]
    unpack_columns(nat, 3, vcols, vcorn, lane)
    quarter = lane // 4
    idx = [quarter, 32 + quarter, jnp.where(lane < 64, 64 + quarter, 96 + quarter)]

    def body(kl, carry):
        for ch in range(3):
            level = field[ch, rows8(kl + 1), :]
            for t in range(3):
                add = lanes_take(level, idx[t])
                for q in range(4):
                    k = kl * 4 + q
                    inside = fine_inside(k, t, lane, sub, *where)[0]
                    x = nat[ch, t, pl.ds(8 + k, 8, stride=K), :] + add
                    va[ch, t, rows8(k + 1), :] = jnp.where(inside, x, 0.0)
        return carry

    lax.fori_loop(0, KL, body, 0)
    fine_pads(va)


def field_out(field, nat, v, vpr, vpl):
    lane = lane_iota()

    def body(k, carry):
        for ch in range(3):
            for t in range(2):
                nat[ch, t, pl.ds(8 + k, 8, stride=K), :] = field[ch, t, rows8(k + 1), :]
        return carry

    lax.fori_loop(0, K, body, 0)
    for ch in range(3):
        for t in range(2):
            v[ch, t] = nat[ch, t, 8 + PAD : 8 + PAD + ROWS, :]
    pack_fine(lambda a, t, r: v[a, t, r, :], 3, vpr, vpl, lane, ROWS)


def positions(n_row, n_col):
    i, j = lax.axis_index("row"), lax.axis_index("col")
    fine = (i * ROWS, j * COLS, n_row * ROWS, n_col * COLS)
    level = (i * LROWS, j * LCOLS, n_row * LROWS, n_col * LCOLS)
    return fine, level


def start_kernel(
    n_row, n_col,
    src, codes, labels, srows, crows, lrows, cols, corners,
    sp, wt, dg, v, vpr, vpl, lev, lpr, lpl, g,
    nat, fxp, fyp, va, vb, lsrc, lfx, lfy, lw, ld, li, lsp, fa, fb, lnat,
):
    where, lwhere = positions(n_row, n_col)
    lane, sub = lane_iota(), sub_iota()
    zero_ends(nat, 6)
    mid, top, low = (
        pl.ds(8 + PAD, ROWS),
        pl.ds(8 + PAD - HALO, HALO),
        pl.ds(8 + PAD + ROWS, HALO),
    )
    for t in range(2):
        c = slice(128 * t, 128 * t + 128)
        for a in range(3):
            nat[a, t, mid, :] = src[a, :, c]
            nat[a, t, top, :] = srows[0, a, :, c]
            nat[a, t, low, :] = srows[1, a, :, c]
        for a in range(2):
            nat[3 + a, t, mid, :] = codes[a, :, c].astype(F32)
            nat[3 + a, t, top, :] = crows[0, a, :, c].astype(F32)
            nat[3 + a, t, low, :] = crows[1, a, :, c].astype(F32)
        nat[5, t, mid, :] = labels[:, c].astype(F32)
        nat[5, t, top, :] = lrows[0, :, c].astype(F32)
        nat[5, t, low, :] = lrows[1, :, c].astype(F32)
    unpack_columns(nat, 6, cols, corners, lane)

    def edge(code, a, b):
        return jnp.exp2(code * 0.25 - 2.0) * jnp.where(a != b, SEAM, 1.0)

    def faces(k, carry):
        at, above = pl.ds(8 + k, 8, stride=K), pl.ds(7 + k, 8, stride=K)
        code = left_of([nat[3, t, at, :] for t in range(3)], lane)
        label = [nat[5, t, at, :] for t in range(3)]
        beside = left_of(label, lane)
        for t in range(3):
            _, row, col = fine_inside(k, t, lane, sub, *where)
            inner = edge(code[t], beside[t], label[t])
            fxp[t, rows8(k), :] = jnp.where((col >= 1) & (col < where[3]), inner, 1.0)
            inner = edge(nat[4, t, above, :], nat[5, t, above, :], label[t])
            fyp[t, rows8(k), :] = jnp.where((row >= 1) & (row < where[2]), inner, 1.0)
        return carry

    lax.fori_loop(0, K, faces, 0)
    for t in range(3):
        fyp[t, rows8(K), :] = pltpu.roll(fyp[t, rows8(0), :], 7, 0)

    def weights(k, carry):
        left = [fxp[t, rows8(k), :] for t in range(3)]
        right = right_of(left, lane)
        at = pl.ds(8 + k, 8, stride=K)
        for t in range(3):
            up, down = fyp[t, rows8(k), :], fyp[t, rows8(k + 1), :]
            diag = SCREEN + left[t] + right[t] + up + down
            inside = fine_inside(k, t, lane, sub, *where)[0]
            inv = jnp.where(inside, 1.0 / diag, 0.0)
            dg[t, rows8(k), :] = diag
            for n, face in enumerate((left[t], right[t], up, down)):
                wt[n, t, rows8(k), :] = face * inv
            for ch in range(3):
                sp[ch, t, rows8(k), :] = nat[ch, t, at, :] * inv
        return carry

    lax.fori_loop(0, K, weights, 0)
    idx = (4 * lane) % 128

    def level_faces(kl, carry):
        got = [
            lanes_take(sum(fxp[t, rows8(kl * 4 + q), :] for q in range(4)), idx) for t in range(3)
        ]
        x = jnp.where(lane < 32, got[0], jnp.where(lane < 64, got[1], got[2])) * 0.0625
        y = to_level([fyp[t, rows8(kl * 4), :] for t in range(3)], lane, idx) * 0.0625
        at = pl.ds(LHALO - LPAD + kl, 8, stride=KL)
        lfx[rows8(kl), :] = x
        lfy[rows8(kl), :] = y
        lnat[6, at, :] = x
        lnat[7, at, :] = y
        return carry

    lax.fori_loop(0, KL, level_faces, 0)
    level_weights(lfx, lfy, lw, ld, li, lwhere)
    field, _ = fine_smooth(va, vb, sp, wt, True)
    fine_residual_to_level(field, sp, wt, dg, lsrc)
    level_down(lsrc, li, ld, lw, lsp, fa, fb, lnat, lev, lpr, lpl, g)
    field_out(field, nat, v, vpr, vpl)


def cycle_kernel(
    n_row, n_col,
    sp, wt, dg, v_in, vrows, vcols, vcorn, lev_in, lrows, lcols, lcorn, corr,
    v, vpr, vpl, lev, lpr, lpl, g,
    nat, va, vb, lsrc, lfx, lfy, lw, ld, li, lsp, fa, fb, lnat, lnc,
):
    where, lwhere = positions(n_row, n_col)
    level = level_up(
        lev_in, lrows, lcols, lcorn, corr, lnat, lnc, lfx, lfy, lw, ld, li, lsp, fa, fb, lwhere
    )
    fine_up(v_in, vrows, vcols, vcorn, level, nat, va, where)
    field, other = fine_smooth(va, vb, sp, wt, False)
    field, other = fine_smooth(field, other, sp, wt, False)
    fine_residual_to_level(field, sp, wt, dg, lsrc)
    level_down(lsrc, li, ld, lw, lsp, fa, fb, lnat, lev, lpr, lpl, g)
    field_out(field, nat, v, vpr, vpl)


def end_kernel(
    n_row, n_col,
    sp, wt, dg, v_in, vrows, vcols, vcorn, lev_in, lrows, lcols, lcorn, corr,
    solution_out, residual_out,
    nat, va, vb, lfx, lfy, lw, ld, li, lsp, fa, fb, lnat, lnc,
):
    where, lwhere = positions(n_row, n_col)
    lane = lane_iota()
    level = level_up(
        lev_in, lrows, lcols, lcorn, corr, lnat, lnc, lfx, lfy, lw, ld, li, lsp, fa, fb, lwhere
    )
    fine_up(v_in, vrows, vcols, vcorn, level, nat, va, where)
    field, _ = fine_smooth(va, vb, sp, wt, False)

    def body(k, carry):
        at = pl.ds(8 + k, 8, stride=K)
        w = fine_weights_at(wt, k)
        for ch in range(3):
            here, total = fine_neighbours(field, w, k, lane, ch)
            for t in range(2):
                nat[ch, t, at, :] = here[t]
                res = dg[t, rows8(k), :] * (sp[ch, t, rows8(k), :] - here[t] + total[t])
                nat[3 + ch, t, at, :] = res
        return carry

    lax.fori_loop(0, K, body, 0)
    for ch in range(3):
        for t in range(2):
            c = slice(128 * t, 128 * t + 128)
            solution_out[ch, :, c] = nat[ch, t, 8 + PAD : 8 + PAD + ROWS, :]
            residual_out[ch, :, c] = nat[3 + ch, t, 8 + PAD : 8 + PAD + ROWS, :]


def around(n_row, n_col):
    i, j = lax.axis_index("row"), lax.axis_index("col")
    up, down = lax.rem(i + n_row - 1, n_row), lax.rem(i + 1, n_row)
    left, right = lax.rem(j + n_col - 1, n_col), lax.rem(j + 1, n_col)
    return i, j, up, down, left, right


def send(copies, src, dst, sems, device):
    n = len(copies)
    copy = pltpu.make_async_remote_copy(
        src_ref=src, dst_ref=dst, send_sem=sems[0].at[n], recv_sem=sems[1].at[n],
        device_id=device, device_id_type=MESH,
    )
    copy.start()
    copies.append(copy)
    return copy


def exchange_kernel(
    n_row, n_col,
    src, codes, labels, src_v, codes_v, labels_v,
    srows, crows, lrows, cols, corners,
    right_pack, left_pack, send_sems, recv_sems,
):
    i, j, up, down, left, right = around(n_row, n_col)
    barrier = pltpu.get_barrier_semaphore()
    for r in (up, i, down):
        for c in (left, j, right):
            if r is not i or c is not j:
                pl.semaphore_signal(barrier, inc=1, device_id=(r, c), device_id_type=MESH)
    lane = lane_iota()

    def tile_of(a, t, r):
        c = slice(128 * t, 128 * t + 128)
        if a < 3:
            return src_v[a, r, c]
        if a < 5:
            return codes_v[a - 3, r, c].astype(F32)
        return labels_v[r, c].astype(F32)

    pack_fine(tile_of, 6, right_pack, left_pack, lane, ROWS)
    pl.semaphore_wait(barrier, 8)
    copies, sems = [], (send_sems, recv_sems)
    top, low = pl.ds(0, HALO), pl.ds(ROWS - HALO, HALO)
    send(copies, right_pack, cols.at[0], sems, (i, right))
    send(copies, left_pack, cols.at[1], sems, (i, left))
    for slot, rows, device in ((1, top, up), (0, low, down)):
        send(copies, src.at[:, rows, :], srows.at[slot], sems, (device, j))
        send(copies, codes.at[:, rows, :], crows.at[slot], sems, (device, j))
        send(copies, labels.at[rows, :], lrows.at[slot], sems, (device, j))
    send(copies, right_pack.at[:, low, :], corners.at[0], sems, (down, right))
    send(copies, left_pack.at[:, low, :], corners.at[1], sems, (down, left))
    send(copies, right_pack.at[:, top, :], corners.at[2], sems, (up, right))
    send(copies, left_pack.at[:, top, :], corners.at[3], sems, (up, left))
    for copy in copies:
        copy.wait()


def coarse_kernel(
    n_row, n_col,
    g, s_cols, s_rows, t_back, row_eig, col_eig, s_ext, v, vpr, vpl, lev, lpr, lpl,
    vrows, vcols, vcorn, lrows, lcols, lcorn, corr,
    one, two, three, mine, spec, back, send_sems, recv_sems,
):
    i, j, up, down, left, right = around(n_row, n_col)
    n_modes = n_row * CROWS
    barrier = pltpu.get_barrier_semaphore()
    for d in range(1, n_col):
        pl.semaphore_signal(barrier, inc=1, device_id=(i, lax.rem(j + d, n_col)), device_id_type=MESH)
    for d in range(1, n_row):
        pl.semaphore_signal(barrier, inc=1, device_id=(lax.rem(i + d, n_row), j), device_id_type=MESH)
    for r in (up, down):
        for c in (left, right):
            pl.semaphore_signal(barrier, inc=1, device_id=(r, c), device_id_type=MESH)
    pl.semaphore_wait(barrier, n_col + n_row + 2)
    copies, sems = [], (send_sems, recv_sems)
    lane = lane_iota()

    first = [
        send(copies, g, one.at[j], sems, (i, lax.rem(j + d, n_col))) for d in range(1, n_col)
    ]
    one[j] = g[...]
    halos = []
    top, low = pl.ds(0, HALO), pl.ds(ROWS - HALO, HALO)
    ltop, llow = pl.ds(0, LHALO), pl.ds(LROWS - LHALO, LHALO)

    def halo(*args):
        halos.append(send(copies, *args[:2], sems, args[2]))

    halo(lpr, lcols.at[0], (i, right))
    halo(lpl, lcols.at[1], (i, left))
    halo(lev.at[:, ltop, :], lrows.at[1], (up, j))
    halo(lev.at[:, llow, :], lrows.at[0], (down, j))
    halo(lpr.at[llow, :], lcorn.at[0], (down, right))
    halo(lpl.at[llow, :], lcorn.at[1], (down, left))
    halo(lpr.at[ltop, :], lcorn.at[2], (up, right))
    halo(lpl.at[ltop, :], lcorn.at[3], (up, left))
    for copy in first:
        copy.wait()

    def placed(ref, n_rows):
        out = []
        for ch in range(3):
            parts = []
            for r in range(n_rows // 8):
                x = jnp.zeros((8, 128), F32)
                for p in range(n_col):
                    here = (lane >= CCOLS * p) & (lane < CCOLS * p + CCOLS)
                    y = lroll(ref[p, r * 8 : r * 8 + 8, :], CCOLS * (p - ch))
                    x = jnp.where(here, y, x)
                parts.append(x)
            out.append(jnp.concatenate(parts, axis=0))
        return out

    x = jnp.concatenate(placed(one, CROWS), axis=0)
    x = jnp.dot(x, s_cols[j], precision=HIGHEST, preferred_element_type=F32)
    total = lax.slice_in_dim(x, 0, CROWS)
    for ch in (1, 2):
        total = total + pltpu.roll(lax.slice_in_dim(x, CROWS * ch, CROWS * ch + CROWS), CCOLS * ch, 1)
    mine[...] = total
    own = pl.ds(pl.multiple_of(i * CROWS, CROWS), CROWS)
    second = [
        send(copies, mine, two.at[own, :], sems, (lax.rem(i + d, n_row), j)) for d in range(1, n_row)
    ]
    two[own, :] = total
    halo(vpr, vcols.at[0], (i, right))
    halo(vpl, vcols.at[1], (i, left))
    halo(vpr.at[:, low, :], vcorn.at[0], (down, right))
    halo(vpl.at[:, low, :], vcorn.at[1], (down, left))
    halo(vpr.at[:, top, :], vcorn.at[2], (up, right))
    halo(vpl.at[:, top, :], vcorn.at[3], (up, left))
    for copy in second:
        copy.wait()
    halo(v.at[:, :, top, :], vrows.at[1], (up, j))
    halo(v.at[:, :, low, :], vrows.at[0], (down, j))
    y = jnp.dot(s_rows[...], two[...], precision=HIGHEST, preferred_element_type=F32)
    eig = SCREEN + COARSE_SCALE * (row_eig[...] + col_eig[pl.ds(j, 1), :])
    spec[...] = y / eig
    rows = s_ext[pl.ds(pl.multiple_of(i * CROWS, CROWS), BROWS), :]
    z = jnp.dot(rows, spec[...], precision=HIGHEST, preferred_element_type=F32)
    back[...] = z
    third = [
        send(copies, back, three.at[j], sems, (i, lax.rem(j + d, n_col))) for d in range(1, n_col)
    ]
    three[j] = z
    for copy in third:
        copy.wait()
    z = jnp.concatenate(placed(three, BROWS), axis=0)
    z = jnp.dot(z, t_back[j], precision=HIGHEST, preferred_element_type=F32)
    for ch in range(3):
        corr[ch] = lax.slice_in_dim(z, BROWS * ch, BROWS * ch + BROWS)
    for copy in halos:
        copy.wait()


@functools.lru_cache(maxsize=None)
def tables(n_row, n_col):
    def sines(n):
        k = np.arange(1, n + 1)
        return math.sqrt(2.0 / (n + 1)) * np.sin(np.pi * ((k[:, None] * k[None, :]) % (2 * (n + 1))) / (n + 1))

    def eig(n):
        return 2.0 - 2.0 * np.cos(np.pi * np.arange(1, n + 1) / (n + 1))

    nr, nc = n_row * CROWS, n_col * CCOLS
    rows, cols = sines(nr), sines(nc)
    s_cols = np.zeros((n_col, 128, 128))
    t_back = np.zeros((n_col, 128, 128))
    col_eig = np.ones((n_col, 128))
    lane = np.arange(128)
    for j in range(n_col):
        own = slice(CCOLS * j, CCOLS * j + CCOLS)
        s_cols[j, :nc, :CCOLS] = cols[:, own]
        col_eig[j, : 3 * CCOLS] = np.tile(eig(nc)[own], 3)
        c = LCOLS * j + np.where(lane < 96, lane, lane - 128)
        ok = (c >= 0) & (c < n_col * LCOLS) & ((lane < 80) | (lane >= 112))
        t_back[j, :nc, ok] = cols[:, c[ok] // 4].T
    s_ext = np.zeros((nr + 16, nr))
    s_ext[8 : 8 + nr] = rows
    row_eig = np.repeat(eig(nr)[:, None], 128, axis=1)
    return tuple(x.astype(np.float32) for x in (s_cols, rows, t_back, row_eig, col_eig, s_ext))


def shape(*dims, dtype=F32):
    return jax.ShapeDtypeStruct(dims, dtype)


IN_VMEM = pl.BlockSpec(memory_space=pltpu.VMEM)
IN_ANY = pl.BlockSpec(memory_space=pl.ANY)


def solution(mesh):
    n_row, n_col = mesh.shape["row"], mesh.shape["col"]
    fine = functools.partial(pltpu.VMEM, dtype=F32)
    params = pltpu.CompilerParams(vmem_limit_bytes=VMEM_LIMIT)

    def level_scratch():
        flat = pltpu.VMEM((KL * 8, 128), F32)
        padded = pltpu.VMEM((3, (KL + 2) * 8, 128), F32)
        return [
            flat, pltpu.VMEM(((KL + 1) * 8, 128), F32), pltpu.VMEM((4, KL * 8, 128), F32), flat, flat,
            pltpu.VMEM((3, KL * 8, 128), F32), padded, padded, pltpu.VMEM((11, LNAT, 128), F32),
        ]

    padded = pltpu.VMEM((3, 3, (K + 2) * 8, 128), F32)
    lsrc = pltpu.VMEM((3, KL * 8, 128), F32)
    lnc = pltpu.VMEM((3, LNAT, 128), F32)
    nat = lambda n: pltpu.VMEM((n, 3, NAT, 128), F32)
    down_shapes = [
        shape(3, 2, ROWS, 128), shape(1, ROWS, 128), shape(1, ROWS, 128), shape(8, LROWS, 128),
        shape(LROWS, 128), shape(LROWS, 128), shape(CROWS, 128),
    ]
    n_coarse = 2 * (n_col - 1) + (n_row - 1) + 16

    def call(kernel, n_in, outs, scratch):
        return pl.pallas_call(
            functools.partial(kernel, n_row, n_col), out_shape=outs, in_specs=[IN_VMEM] * n_in,
            out_specs=[IN_VMEM] * len(outs), scratch_shapes=scratch, compiler_params=params,
        )

    exchange = pl.pallas_call(
        functools.partial(exchange_kernel, n_row, n_col),
        out_shape=[
            shape(2, 3, HALO, COLS), shape(2, 2, HALO, COLS, dtype=jnp.int32), shape(2, HALO, COLS, dtype=jnp.int32),
            shape(2, 2, ROWS, 128), shape(4, 2, HALO, 128),
        ],
        in_specs=[IN_ANY] * 3 + [IN_VMEM] * 3,
        out_specs=[IN_VMEM] * 5,
        scratch_shapes=[pltpu.VMEM((2, ROWS, 128), F32)] * 2 + [pltpu.SemaphoreType.DMA((12,))] * 2,
        compiler_params=pltpu.CompilerParams(collective_id=0, has_side_effects=True, vmem_limit_bytes=VMEM_LIMIT),
    )
    start = call(
        start_kernel, 8,
        [shape(3, 3, K * 8, 128), shape(4, 3, K * 8, 128), shape(3, K * 8, 128)] + down_shapes,
        [nat(6), pltpu.VMEM((3, K * 8, 128), F32), pltpu.VMEM((3, (K + 1) * 8, 128), F32), padded, padded, lsrc]
        + level_scratch(),
    )
    coarse = pl.pallas_call(
        functools.partial(coarse_kernel, n_row, n_col),
        out_shape=[
            shape(2, 3, 2, HALO, 128), shape(2, 1, ROWS, 128), shape(4, 1, HALO, 128),
            shape(2, 8, LHALO, 128), shape(2, LROWS, 128), shape(4, LHALO, 128), shape(3, BROWS, 128),
        ],
        in_specs=[IN_VMEM] * 7 + [IN_ANY] * 6,
        out_specs=[IN_VMEM] * 7,
        scratch_shapes=[
            pltpu.VMEM((n_col, CROWS, 128), F32), pltpu.VMEM((n_row * CROWS, 128), F32),
            pltpu.VMEM((n_col, BROWS, 128), F32), pltpu.VMEM((CROWS, 128), F32),
            pltpu.VMEM((n_row * CROWS, 128), F32), pltpu.VMEM((BROWS, 128), F32),
            pltpu.SemaphoreType.DMA((n_coarse,)), pltpu.SemaphoreType.DMA((n_coarse,)),
        ],
        compiler_params=pltpu.CompilerParams(collective_id=1, has_side_effects=True, vmem_limit_bytes=VMEM_LIMIT),
    )
    cycle = call(cycle_kernel, 12, down_shapes, [nat(3), padded, padded, lsrc] + level_scratch() + [lnc])
    end = call(
        end_kernel, 12, [shape(3, ROWS, COLS)] * 2, [nat(6), padded, padded] + level_scratch() + [lnc]
    )
    consts = tables(n_row, n_col)

    def local(sources, edge_codes, seam_labels):
        halos = exchange(sources, edge_codes, seam_labels, sources, edge_codes, seam_labels)
        sp, wt, dg, *down = start(sources, edge_codes, seam_labels, *halos)
        for step in (cycle, end):
            v, vpr, vpl, lev, lpr, lpl, g = down
            vrows, vcols, vcorn, lrows, lcols, lcorn, corr = coarse(g, *consts, v, vpr, vpl, lev, lpr, lpl)
            down = step(sp, wt, dg, v, vrows, vcols, vcorn, lev, lrows, lcols, lcorn, corr)
        return tuple(down)

    spec = P(None, "row", "col")
    return jax.shard_map(
        local, mesh=mesh, in_specs=(spec, spec, P("row", "col")), out_specs=(spec, spec), check_vma=False
    )
```

```python
import functools
import math

import jax
import jax.numpy as jnp
import numpy as np
from jax import lax
from jax.experimental import pallas as pl
from jax.experimental.pallas import tpu as pltpu
from jax.sharding import PartitionSpec as P

SWEEPS = 4
SCREEN = 2e-05
SEAM = 0.2
COARSE_SCALE = 0.0625
F32 = jnp.float32
MESH = pl.DeviceIdType.MESH
HIGHEST = lax.Precision.HIGHEST

ROWS, COLS = 512, 256
PAD = 48
HALO = 32
K = (ROWS + 2 * PAD) // 8
NAT = 8 + ROWS + 2 * PAD + 8
LROWS, LCOLS = 128, 64
LPAD = PAD // 4
LHALO = 16
KL = (LROWS + 2 * LPAD) // 8
LNAT = LROWS + 2 * LHALO
CROWS, CCOLS = 32, 16
BROWS = CROWS + 16
VMEM_LIMIT = 62 * 1024 * 1024


def chebyshev_weight(sweep_index):
    return 1.0 / (1.25 + 0.75 * math.cos(math.pi * (2 * sweep_index + 1) / (2 * SWEEPS)))


def lane_iota():
    return lax.broadcasted_iota(jnp.int32, (8, 128), 1)


def sub_iota():
    return lax.broadcasted_iota(jnp.int32, (8, 128), 0)


def lroll(x, shift):
    shift = shift % 128
    return x if shift == 0 else pltpu.roll(x, shift, 1)


def rows8(k):
    return pl.ds(pl.multiple_of(k * 8, 8), 8)


def lanes_take(x, idx):
    return jnp.take_along_axis(x, idx, axis=1)


def left_of(tiles, lane):
    rolled = [lroll(x, 1) for x in tiles]
    return [jnp.where(lane == 0, rolled[(t + 2) % 3], rolled[t]) for t in range(3)]


def right_of(tiles, lane):
    rolled = [lroll(x, 127) for x in tiles]
    return [jnp.where(lane == 127, rolled[(t + 1) % 3], rolled[t]) for t in range(3)]


def set_pads(ref, lead, count):
    last = ref[lead + (rows8(count), slice(None))]
    first = ref[lead + (rows8(1), slice(None))]
    ref[lead + (rows8(0), slice(None))] = pltpu.roll(last, 1, 0)
    ref[lead + (rows8(count + 1), slice(None))] = pltpu.roll(first, 7, 0)


def pack_fine(tile_of, n_arrays, right, left, lane, rows):
    def body(i, carry):
        r = rows8(i)
        for first in range(0, n_arrays, 4):
            out_r = out_l = jnp.zeros((8, 128), F32)
            for a in range(first, min(first + 4, n_arrays)):
                g = a - first
                here = (lane >= 32 * g) & (lane < 32 * g + 32)
                out_r = jnp.where(here, lroll(tile_of(a, 1, r), 32 * g - 96), out_r)
                out_l = jnp.where(here, lroll(tile_of(a, 0, r), 32 * g), out_l)
            right[first // 4, r, :] = out_r
            left[first // 4, r, :] = out_l
        return carry

    lax.fori_loop(0, rows // 8, body, 0)


def unpack_fine(nat, n_arrays, at, count, from_left, from_right, lane):
    def body(i, carry):
        src = rows8(i)
        dst = pl.ds(pl.multiple_of(at + i * 8, 8), 8)
        for a in range(n_arrays):
            g = a % 4
            l = lroll(from_left[a // 4, src, :], 96 - 32 * g)
            r = lroll(from_right[a // 4, src, :], -32 * g)
            nat[a, 2, dst, :] = jnp.where(lane < 32, r, jnp.where(lane >= 96, l, 0.0))
        return carry

    lax.fori_loop(0, count, body, 0)


def zero_ends(nat, n_arrays):
    zero = jnp.zeros((8, 128), F32)
    for a in range(n_arrays):
        for t in range(3):
            for r in (0, 8, 16, NAT - 24, NAT - 16, NAT - 8):
                nat[a, t, r : r + 8, :] = zero


def unpack_columns(nat, n_arrays, cols, corners, lane):
    unpack_fine(nat, n_arrays, 8 + PAD, ROWS // 8, cols.at[0], cols.at[1], lane)
    unpack_fine(nat, n_arrays, 8 + PAD - HALO, HALO // 8, corners.at[0], corners.at[1], lane)
    unpack_fine(nat, n_arrays, 8 + PAD + ROWS, HALO // 8, corners.at[2], corners.at[3], lane)


def fine_inside(k, t, lane, sub, row0, col0, n_rows, n_cols):
    row = row0 - PAD + sub * K + k
    if t < 2:
        col = lane + (col0 + 128 * t)
    else:
        col = jnp.where(lane < 64, lane + (col0 + 256), lane + (col0 - 128))
    return (row >= 0) & (row < n_rows) & (col >= 0) & (col < n_cols), row, col


def level_inside(k, lane, sub, row0, col0, n_rows, n_cols):
    row = row0 - LPAD + sub * KL + k
    col = jnp.where(lane < 96, lane, lane - 128) + col0
    return (row >= 0) & (row < n_rows) & (col >= 0) & (col < n_cols)


def stencil_pass(v, wt, sl, emit, tiles=3, begin=None, end=None):
    lane = lane_iota()

    def shift(k, slot):
        for ch in range(3):
            here = [v[ch, t, rows8(k + 1), :] for t in range(3)]
            left, right = left_of(here, lane), right_of(here, lane)
            for t in range(3):
                sl[slot, 0, ch, t] = left[t]
                sl[slot, 1, ch, t] = right[t]

    def compute(k, slot):
        for t in range(tiles):
            w = [wt[n, t, rows8(k), :] for n in range(4)]
            for ch in range(3):
                total = w[0] * sl[slot, 0, ch, t] + w[1] * sl[slot, 1, ch, t]
                total = total + w[2] * v[ch, t, rows8(k), :] + w[3] * v[ch, t, rows8(k + 2), :]
                emit(k, ch, t, v[ch, t, rows8(k + 1), :], total)

    def body(m, carry):
        k = 4 * m
        if begin is not None:
            begin()
        shift(k + 2, 2)
        shift(k + 3, 3)
        compute(k, 0)
        compute(k + 1, 1)
        shift(k + 4, 0)
        shift(k + 5, 1)
        compute(k + 2, 2)
        compute(k + 3, 3)
        if end is not None:
            end(m)
        return carry

    shift(0, 0)
    shift(1, 1)
    lax.fori_loop(0, K // 4, body, 0)


def fine_pads(v):
    for ch in range(3):
        for t in range(3):
            set_pads(v, (ch, t), K)


def fine_sweep(vin, vout, sp, wt, sl, omega):
    def emit(k, ch, t, here, total):
        new = sp[ch, t, rows8(k), :] + total
        vout[ch, t, rows8(k + 1), :] = (1.0 - omega) * here + omega * new

    stencil_pass(vin, wt, sl, emit)
    fine_pads(vout)


def fine_first(vout, sp):
    omega = chebyshev_weight(0)

    def body(k, carry):
        for ch in range(3):
            for t in range(3):
                vout[ch, t, rows8(k + 1), :] = omega * sp[ch, t, rows8(k), :]
        return carry

    lax.fori_loop(0, K, body, 0)
    fine_pads(vout)


def fine_smooth(va, vb, sp, wt, sl, from_zero):
    bufs = [va, vb]
    at = 0
    for i in range(SWEEPS):
        if i == 0 and from_zero:
            fine_first(va, sp)
            continue
        fine_sweep(bufs[at], bufs[1 - at], sp, wt, sl, chebyshev_weight(i))
        at = 1 - at
    return bufs[at], bufs[1 - at]


def to_level(x, lane, idx):
    got = []
    for y in x:
        y = y + lroll(y, 127)
        y = y + lroll(y, 126)
        got.append(lanes_take(y, idx))
    return jnp.where(lane < 32, got[0], jnp.where(lane < 64, got[1], got[2]))


def fine_residual_to_level(v, sp, wt, dg, sl, lsrc):
    lane = lane_iota()
    idx = (4 * lane) % 128
    acc = {}

    def emit(k, ch, t, here, total):
        res = dg[t, rows8(k), :] * (sp[ch, t, rows8(k), :] - here + total)
        acc[ch, t] = acc[ch, t] + res if (ch, t) in acc else res

    def end(m):
        for ch in range(3):
            lsrc[ch, rows8(m), :] = to_level([acc[ch, t] for t in range(3)], lane, idx) * 0.0625

    stencil_pass(v, wt, sl, emit, begin=acc.clear, end=end)


def level_weights(fx, fy, lw, ld, li, where):
    lane, sub = lane_iota(), sub_iota()
    fy[rows8(KL), :] = pltpu.roll(fy[rows8(0), :], 7, 0)

    def body(k, carry):
        left, up, down = fx[rows8(k), :], fy[rows8(k), :], fy[rows8(k + 1), :]
        right = lroll(left, 127)
        diag = SCREEN + left + right + up + down
        inv = jnp.where(level_inside(k, lane, sub, *where), 1.0 / diag, 0.0)
        ld[rows8(k), :] = diag
        li[rows8(k), :] = inv
        for n, face in enumerate((left, right, up, down)):
            lw[n, rows8(k), :] = face * inv
        return carry

    lax.fori_loop(0, KL, body, 0)


def level_neighbours(f, lw, k, ch):
    here = f[ch, rows8(k + 1), :]
    total = lw[0, rows8(k), :] * lroll(here, 1) + lw[1, rows8(k), :] * lroll(here, 127)
    return here, total + lw[2, rows8(k), :] * f[ch, rows8(k), :] + lw[3, rows8(k), :] * f[ch, rows8(k + 2), :]


def level_pads(f):
    for ch in range(3):
        set_pads(f, (ch,), KL)


def level_smooth(fa, fb, lsp, lw, from_zero):
    bufs = [fa, fb]
    at = 0
    for i in range(SWEEPS):
        omega = chebyshev_weight(i)
        src, dst = bufs[at], bufs[1 - at]
        if i == 0 and from_zero:

            def first(k, carry):
                for ch in range(3):
                    src[ch, rows8(k + 1), :] = omega * lsp[ch, rows8(k), :]
                return carry

            lax.fori_loop(0, KL, first, 0)
            level_pads(src)
            continue

        def body(k, carry):
            for ch in range(3):
                here, total = level_neighbours(src, lw, k, ch)
                dst[ch, rows8(k + 1), :] = (1.0 - omega) * here + omega * (lsp[ch, rows8(k), :] + total)
            return carry

        lax.fori_loop(0, KL, body, 0)
        level_pads(dst)
        at = 1 - at
    return bufs[at]


def level_down(lsrc, li, ld, lw, lsp, fa, fb, lnat, lev, lpr, lpl, g):
    lane = lane_iota()

    def scale(k, carry):
        for ch in range(3):
            lsp[ch, rows8(k), :] = lsrc[ch, rows8(k), :] * li[rows8(k), :]
        return carry

    lax.fori_loop(0, KL, scale, 0)
    f = level_smooth(fa, fb, lsp, lw, True)

    def out(k, carry):
        at = pl.ds(LHALO - LPAD + k, 8, stride=KL)
        for ch in range(3):
            here, total = level_neighbours(f, lw, k, ch)
            lnat[8 + ch, at, :] = ld[rows8(k), :] * (lsp[ch, rows8(k), :] - here + total)
            lnat[ch, at, :] = here
            lnat[3 + ch, at, :] = lsrc[ch, rows8(k), :]
        return carry

    lax.fori_loop(0, KL, out, 0)

    def copy(i, carry):
        src = pl.ds(pl.multiple_of(LHALO + i * 8, 8), 8)
        right = left = jnp.zeros((8, 128), F32)
        for a in range(8):
            x = lnat[a, src, :]
            lev[a, rows8(i), :] = x
            here = (lane >= 16 * a) & (lane < 16 * a + 16)
            right = jnp.where(here, lroll(x, 16 * a - 48), right)
            left = jnp.where(here, lroll(x, 16 * a), left)
        lpr[rows8(i), :] = right
        lpl[rows8(i), :] = left
        return carry

    lax.fori_loop(0, LROWS // 8, copy, 0)
    idx = (4 * lane) % 128
    for i in range(CROWS // 8):
        total = jnp.zeros((8, 128), F32)
        for ch in range(3):
            x = sum(lnat[8 + ch, pl.ds(LHALO + 32 * i + q, 8, stride=4), :] for q in range(4))
            x = x + lroll(x, 127)
            x = x + lroll(x, 126)
            x = jnp.where(lane < CCOLS, lanes_take(x, idx), 0.0) * 0.0625
            total = total + lroll(x, CCOLS * ch)
        g[i * 8 : i * 8 + 8, :] = total


def level_up(lev, lrows, lcols, lcorn, corr, lnat, lnc, fx, fy, lw, ld, li, lsp, fa, fb, where):
    lane, sub = lane_iota(), sub_iota()

    def place(dst_row, count, own, left, right):
        def body(i, carry):
            dst = pl.ds(pl.multiple_of(dst_row + i * 8, 8), 8)
            l, r = left(rows8(i)), right(rows8(i))
            for a in range(8):
                x = jnp.where(lane < 64, own(a, rows8(i)), 0.0)
                x = jnp.where((lane >= 64) & (lane < 80), lroll(r, 64 - 16 * a), x)
                lnat[a, dst, :] = jnp.where(lane >= 112, lroll(l, 112 - 16 * a), x)
            return carry

        lax.fori_loop(0, count, body, 0)

    place(0, LHALO // 8, lambda a, r: lrows[0, a, r, :], lambda r: lcorn[0, r, :], lambda r: lcorn[1, r, :])
    place(LHALO, LROWS // 8, lambda a, r: lev[a, r, :], lambda r: lcols[0, r, :], lambda r: lcols[1, r, :])
    place(LHALO + LROWS, LHALO // 8, lambda a, r: lrows[1, a, r, :], lambda r: lcorn[2, r, :], lambda r: lcorn[3, r, :])
    for ch in range(3):
        for h in range(LNAT // 32):
            x = corr[ch, 4 + 8 * h : 12 + 8 * h, :]
            for q in range(4):
                lnc[ch, pl.ds(32 * h + q, 8, stride=4), :] = x

    def faces(k, carry):
        at = pl.ds(LHALO - LPAD + k, 8, stride=KL)
        fx[rows8(k), :] = lnat[6, at, :]
        fy[rows8(k), :] = lnat[7, at, :]
        return carry

    lax.fori_loop(0, KL, faces, 0)
    level_weights(fx, fy, lw, ld, li, where)

    def fields(k, carry):
        at = pl.ds(LHALO - LPAD + k, 8, stride=KL)
        inside = level_inside(k, lane, sub, *where)
        inv = li[rows8(k), :]
        for ch in range(3):
            fa[ch, rows8(k + 1), :] = jnp.where(inside, lnat[ch, at, :] + lnc[ch, at, :], 0.0)
            lsp[ch, rows8(k), :] = lnat[3 + ch, at, :] * inv
        return carry

    lax.fori_loop(0, KL, fields, 0)
    level_pads(fa)
    return level_smooth(fa, fb, lsp, lw, False)


def fine_up(v, vrows, vcols, vcorn, field, nat, va, where):
    lane, sub = lane_iota(), sub_iota()
    zero_ends(nat, 3)
    for ch in range(3):
        for t in range(2):
            nat[ch, t, 8 + PAD : 8 + PAD + ROWS, :] = v[ch, t]
            nat[ch, t, 8 + PAD - HALO : 8 + PAD, :] = vrows[0, ch, t]
            nat[ch, t, 8 + PAD + ROWS : 8 + PAD + ROWS + HALO, :] = vrows[1, ch, t]
    unpack_columns(nat, 3, vcols, vcorn, lane)
    quarter = lane // 4
    idx = [quarter, 32 + quarter, jnp.where(lane < 64, 64 + quarter, 96 + quarter)]

    def body(kl, carry):
        for ch in range(3):
            level = field[ch, rows8(kl + 1), :]
            for t in range(3):
                add = lanes_take(level, idx[t])
                for q in range(4):
                    k = kl * 4 + q
                    inside = fine_inside(k, t, lane, sub, *where)[0]
                    x = nat[ch, t, pl.ds(8 + k, 8, stride=K), :] + add
                    va[ch, t, rows8(k + 1), :] = jnp.where(inside, x, 0.0)
        return carry

    lax.fori_loop(0, KL, body, 0)
    fine_pads(va)


def field_out(field, nat, v, vpr, vpl):
    lane = lane_iota()

    def body(k, carry):
        for ch in range(3):
            for t in range(2):
                nat[ch, t, pl.ds(8 + k, 8, stride=K), :] = field[ch, t, rows8(k + 1), :]
        return carry

    lax.fori_loop(0, K, body, 0)
    for ch in range(3):
        for t in range(2):
            v[ch, t] = nat[ch, t, 8 + PAD : 8 + PAD + ROWS, :]
    pack_fine(lambda a, t, r: v[a, t, r, :], 3, vpr, vpl, lane, ROWS)


def positions(n_row, n_col):
    i, j = lax.axis_index("row"), lax.axis_index("col")
    fine = (i * ROWS, j * COLS, n_row * ROWS, n_col * COLS)
    level = (i * LROWS, j * LCOLS, n_row * LROWS, n_col * LCOLS)
    return fine, level


TOP, LOW = pl.ds(0, HALO), pl.ds(ROWS - HALO, HALO)
LTOP, LLOW = pl.ds(0, LHALO), pl.ds(LROWS - LHALO, LHALO)
MID = pl.ds(8 + PAD, ROWS)
ABOVE, BELOW = pl.ds(8 + PAD - HALO, HALO), pl.ds(8 + PAD + ROWS, HALO)


class Sender:
    def __init__(self, send_sems, recv_sems):
        self.send_sems, self.recv_sems, self.count = send_sems, recv_sems, 0

    def __call__(self, src, dst, device):
        n = self.count
        self.count += 1
        copy = pltpu.make_async_remote_copy(
            src_ref=src, dst_ref=dst, send_sem=self.send_sems.at[n], recv_sem=self.recv_sems.at[n],
            device_id=device, device_id_type=MESH,
        )
        copy.start()
        return copy


def fine_operator(nat, fxp, fyp, sp, wt, dg, lfx, lfy, lnat, where):
    lane, sub = lane_iota(), sub_iota()

    def edge(code, a, b):
        return jnp.exp2(code * 0.25 - 2.0) * jnp.where(a != b, SEAM, 1.0)

    def faces(k, carry):
        at, above = pl.ds(8 + k, 8, stride=K), pl.ds(7 + k, 8, stride=K)
        code = left_of([nat[3, t, at, :] for t in range(3)], lane)
        label = [nat[5, t, at, :] for t in range(3)]
        beside = left_of(label, lane)
        for t in range(3):
            _, row, col = fine_inside(k, t, lane, sub, *where)
            inner = edge(code[t], beside[t], label[t])
            fxp[t, rows8(k), :] = jnp.where((col >= 1) & (col < where[3]), inner, 1.0)
            inner = edge(nat[4, t, above, :], nat[5, t, above, :], label[t])
            fyp[t, rows8(k), :] = jnp.where((row >= 1) & (row < where[2]), inner, 1.0)
        return carry

    lax.fori_loop(0, K, faces, 0, unroll=2)
    for t in range(3):
        fyp[t, rows8(K), :] = pltpu.roll(fyp[t, rows8(0), :], 7, 0)

    def weights(k, carry):
        left = [fxp[t, rows8(k), :] for t in range(3)]
        right = right_of(left, lane)
        at = pl.ds(8 + k, 8, stride=K)
        for t in range(3):
            up, down = fyp[t, rows8(k), :], fyp[t, rows8(k + 1), :]
            diag = SCREEN + left[t] + right[t] + up + down
            inside = fine_inside(k, t, lane, sub, *where)[0]
            inv = jnp.where(inside, 1.0 / diag, 0.0)
            dg[t, rows8(k), :] = diag
            for n, face in enumerate((left[t], right[t], up, down)):
                wt[n, t, rows8(k), :] = face * inv
            for ch in range(3):
                sp[ch, t, rows8(k), :] = nat[ch, t, at, :] * inv
        return carry

    lax.fori_loop(0, K, weights, 0, unroll=2)
    idx = (4 * lane) % 128

    def level_faces(kl, carry):
        got = [
            lanes_take(sum(fxp[t, rows8(kl * 4 + q), :] for q in range(4)), idx) for t in range(3)
        ]
        x = jnp.where(lane < 32, got[0], jnp.where(lane < 64, got[1], got[2])) * 0.0625
        y = to_level([fyp[t, rows8(kl * 4), :] for t in range(3)], lane, idx) * 0.0625
        at = pl.ds(LHALO - LPAD + kl, 8, stride=KL)
        lfx[rows8(kl), :] = x
        lfy[rows8(kl), :] = y
        lnat[6, at, :] = x
        lnat[7, at, :] = y
        return carry

    lax.fori_loop(0, KL, level_faces, 0)


def coarse_solve(
    n_row, n_col, place, send, g, s_cols, s_ext, t_back, row_eig, col_eig, v, vpr, vpl, lev, lpr, lpl,
    vrows, vcols, vcorn, lrows, lcols, lcorn, one, two, three, mine, spec, back, corr,
):
    i, j, up, down, left, right = place
    n_modes = n_row * CROWS
    lane = lane_iota()

    first = [send(g, one.at[j], (i, lax.rem(j + d, n_col))) for d in range(1, n_col)]
    one[j] = g[...]
    halos = [
        send(lpr, lcols.at[0], (i, right)),
        send(lpl, lcols.at[1], (i, left)),
        send(lev.at[:, LTOP, :], lrows.at[1], (up, j)),
        send(lev.at[:, LLOW, :], lrows.at[0], (down, j)),
        send(lpr.at[LLOW, :], lcorn.at[0], (down, right)),
        send(lpl.at[LLOW, :], lcorn.at[1], (down, left)),
        send(lpr.at[LTOP, :], lcorn.at[2], (up, right)),
        send(lpl.at[LTOP, :], lcorn.at[3], (up, left)),
    ]
    for copy in first:
        copy.wait()

    def placed(ref, n_rows):
        out = []
        for ch in range(3):
            parts = []
            for r in range(n_rows // 8):
                x = jnp.zeros((8, 128), F32)
                for p in range(n_col):
                    here = (lane >= CCOLS * p) & (lane < CCOLS * p + CCOLS)
                    y = lroll(ref[p, r * 8 : r * 8 + 8, :], CCOLS * (p - ch))
                    x = jnp.where(here, y, x)
                parts.append(x)
            out.append(jnp.concatenate(parts, axis=0))
        return out

    x = jnp.concatenate(placed(one, CROWS), axis=0)
    x = jnp.dot(x, s_cols[j], precision=HIGHEST, preferred_element_type=F32)
    total = lax.slice_in_dim(x, 0, CROWS)
    for ch in (1, 2):
        total = total + pltpu.roll(lax.slice_in_dim(x, CROWS * ch, CROWS * ch + CROWS), CCOLS * ch, 1)
    mine[...] = total
    own = pl.ds(pl.multiple_of(i * CROWS, CROWS), CROWS)
    second = [send(mine, two.at[own, :], (lax.rem(i + d, n_row), j)) for d in range(1, n_row)]
    two[own, :] = total
    halos += [
        send(vpr, vcols.at[0], (i, right)),
        send(vpl, vcols.at[1], (i, left)),
        send(vpr.at[:, LOW, :], vcorn.at[0], (down, right)),
        send(vpl.at[:, LOW, :], vcorn.at[1], (down, left)),
        send(vpr.at[:, TOP, :], vcorn.at[2], (up, right)),
        send(vpl.at[:, TOP, :], vcorn.at[3], (up, left)),
    ]
    for copy in second:
        copy.wait()
    halos += [
        send(v.at[:, :, TOP, :], vrows.at[1], (up, j)),
        send(v.at[:, :, LOW, :], vrows.at[0], (down, j)),
    ]
    y = jnp.dot(s_ext[8 : 8 + n_modes, :], two[...], precision=HIGHEST, preferred_element_type=F32)
    eig = SCREEN + COARSE_SCALE * (row_eig[...] + col_eig[pl.ds(j, 1), :])
    spec[...] = y / eig
    rows = s_ext[pl.ds(pl.multiple_of(i * CROWS, CROWS), BROWS), :]
    z = jnp.dot(rows, spec[...], precision=HIGHEST, preferred_element_type=F32)
    back[...] = z
    third = [send(back, three.at[j], (i, lax.rem(j + d, n_col))) for d in range(1, n_col)]
    three[j] = z
    for copy in third:
        copy.wait()
    z = jnp.concatenate(placed(three, BROWS), axis=0)
    z = jnp.dot(z, t_back[j], precision=HIGHEST, preferred_element_type=F32)
    for ch in range(3):
        corr[ch] = lax.slice_in_dim(z, BROWS * ch, BROWS * ch + BROWS)
    for copy in halos:
        copy.wait()


def kernel(n_row, n_col, src, codes, labels, *refs):
    s_cols, s_ext, t_back, row_eig, col_eig, solution_out, residual_out = refs[:7]
    (
        codes_v, labels_v, right_pack, left_pack, srows, crows, labrows, cols, corners,
        nat, fxp, fyp, sp, wt, dg, va, vb, sl, v, vpr, vpl,
        lsrc, lfx, lfy, lw, ld, li, lsp, fa, fb, lnat, lnc, lev, lpr, lpl, g,
        one, two, three, mine, spec, back, corr,
        vrows, vcols, vcorn, lrows, lcols, lcorn,
        copy_sems, send_sems, recv_sems,
    ) = refs[7:]
    i, j = lax.axis_index("row"), lax.axis_index("col")
    up, down = lax.rem(i + n_row - 1, n_row), lax.rem(i + 1, n_row)
    left, right = lax.rem(j + n_col - 1, n_col), lax.rem(j + 1, n_col)
    where, lwhere = positions(n_row, n_col)
    lane = lane_iota()

    barrier = pltpu.get_barrier_semaphore()
    peers = [(i, lax.rem(j + d, n_col)) for d in range(1, n_col)]
    peers += [(lax.rem(i + d, n_row), j) for d in range(1, n_row)]
    peers += [(r, c) for r in (up, down) for c in (left, right)]
    for peer in peers:
        pl.semaphore_signal(barrier, inc=1, device_id=peer, device_id_type=MESH)

    loads = [pltpu.make_async_copy(codes, codes_v, copy_sems.at[0])]
    loads.append(pltpu.make_async_copy(labels, labels_v, copy_sems.at[1]))
    for a in range(3):
        for t in range(2):
            part = src.at[a, :, pl.ds(128 * t, 128)]
            loads.append(pltpu.make_async_copy(part, nat.at[a, t, MID, :], copy_sems.at[len(loads)]))
    for copy in loads:
        copy.start()
    zero_ends(nat, 6)
    for copy in loads:
        copy.wait()

    def convert(n, carry):
        r = rows8(n)
        at = pl.ds(pl.multiple_of(8 + PAD + 8 * n, 8), 8)
        for t in range(2):
            c = slice(128 * t, 128 * t + 128)
            nat[3, t, at, :] = codes_v[0, r, c].astype(F32)
            nat[4, t, at, :] = codes_v[1, r, c].astype(F32)
            nat[5, t, at, :] = labels_v[r, c].astype(F32)
        return carry

    lax.fori_loop(0, ROWS // 8, convert, 0, unroll=2)

    def natural(a, t, r):
        return nat[a, t, pl.ds(pl.multiple_of(8 + PAD + r.start, 8), 8), :]

    pack_fine(natural, 6, right_pack, left_pack, lane, ROWS)
    pl.semaphore_wait(barrier, n_col + n_row + 2)
    send = Sender(send_sems, recv_sems)
    copies = [
        send(right_pack, cols.at[0], (i, right)),
        send(left_pack, cols.at[1], (i, left)),
    ]
    for slot, rows, device in ((1, TOP, up), (0, LOW, down)):
        copies.append(send(src.at[:, rows, :], srows.at[slot], (device, j)))
        copies.append(send(codes.at[:, rows, :], crows.at[slot], (device, j)))
        copies.append(send(labels.at[rows, :], labrows.at[slot], (device, j)))
    copies.append(send(right_pack.at[:, LOW, :], corners.at[0], (down, right)))
    copies.append(send(left_pack.at[:, LOW, :], corners.at[1], (down, left)))
    copies.append(send(right_pack.at[:, TOP, :], corners.at[2], (up, right)))
    copies.append(send(left_pack.at[:, TOP, :], corners.at[3], (up, left)))
    for copy in copies:
        copy.wait()

    for t in range(2):
        c = slice(128 * t, 128 * t + 128)
        for slot, rows in ((0, ABOVE), (1, BELOW)):
            for a in range(3):
                nat[a, t, rows, :] = srows[slot, a, :, c]
            for a in range(2):
                nat[3 + a, t, rows, :] = crows[slot, a, :, c].astype(F32)
            nat[5, t, rows, :] = labrows[slot, :, c].astype(F32)
    unpack_columns(nat, 6, cols, corners, lane)
    fine_operator(nat, fxp, fyp, sp, wt, dg, lfx, lfy, lnat, where)
    level_weights(lfx, lfy, lw, ld, li, lwhere)

    field, other = fine_smooth(va, vb, sp, wt, sl, True)
    for cycle in range(2):
        fine_residual_to_level(field, sp, wt, dg, sl, lsrc)
        level_down(lsrc, li, ld, lw, lsp, fa, fb, lnat, lev, lpr, lpl, g)
        field_out(field, nat, v, vpr, vpl)
        got = [ref.at[cycle] for ref in (vrows, vcols, vcorn, lrows, lcols, lcorn, one, two, three)]
        coarse_solve(
            n_row, n_col, (i, j, up, down, left, right), send, g, s_cols, s_ext, t_back, row_eig, col_eig,
            v, vpr, vpl, lev, lpr, lpl, *got, mine, spec, back, corr,
        )
        level = level_up(
            lev, got[3], got[4], got[5], corr, lnat, lnc, lfx, lfy, lw, ld, li, lsp, fa, fb, lwhere
        )
        fine_up(v, got[0], got[1], got[2], level, nat, va, where)
        field, other = fine_smooth(va, vb, sp, wt, sl, False)
        if cycle == 0:
            field, other = fine_smooth(field, other, sp, wt, sl, False)

    def emit(k, ch, t, here, total):
        at = pl.ds(8 + k, 8, stride=K)
        nat[ch, t, at, :] = here
        nat[3 + ch, t, at, :] = dg[t, rows8(k), :] * (sp[ch, t, rows8(k), :] - here + total)

    stencil_pass(field, wt, sl, emit, tiles=2)
    stores = []
    for a in range(6):
        for t in range(2):
            out = (solution_out if a < 3 else residual_out).at[a % 3, :, pl.ds(128 * t, 128)]
            stores.append(pltpu.make_async_copy(nat.at[a, t, MID, :], out, copy_sems.at[len(stores)]))
    for copy in stores:
        copy.start()
    for copy in stores:
        copy.wait()


@functools.lru_cache(maxsize=None)
def tables(n_row, n_col):
    def sines(n):
        k = np.arange(1, n + 1)
        return math.sqrt(2.0 / (n + 1)) * np.sin(np.pi * ((k[:, None] * k[None, :]) % (2 * (n + 1))) / (n + 1))

    def eig(n):
        return 2.0 - 2.0 * np.cos(np.pi * np.arange(1, n + 1) / (n + 1))

    nr, nc = n_row * CROWS, n_col * CCOLS
    rows, cols = sines(nr), sines(nc)
    s_cols = np.zeros((n_col, 128, 128))
    t_back = np.zeros((n_col, 128, 128))
    col_eig = np.ones((n_col, 128))
    lane = np.arange(128)
    for j in range(n_col):
        own = slice(CCOLS * j, CCOLS * j + CCOLS)
        s_cols[j, :nc, :CCOLS] = cols[:, own]
        col_eig[j, : 3 * CCOLS] = np.tile(eig(nc)[own], 3)
        c = LCOLS * j + np.where(lane < 96, lane, lane - 128)
        ok = (c >= 0) & (c < n_col * LCOLS) & ((lane < 80) | (lane >= 112))
        t_back[j, :nc, ok] = cols[:, c[ok] // 4].T
    s_ext = np.zeros((nr + 16, nr))
    s_ext[8 : 8 + nr] = rows
    row_eig = np.repeat(eig(nr)[:, None], 128, axis=1)
    return tuple(x.astype(np.float32) for x in (s_cols, s_ext, t_back, row_eig, col_eig))


def shape(*dims, dtype=F32):
    return jax.ShapeDtypeStruct(dims, dtype)


IN_VMEM = pl.BlockSpec(memory_space=pltpu.VMEM)
IN_ANY = pl.BlockSpec(memory_space=pl.ANY)


def solution(mesh):
    n_row, n_col = mesh.shape["row"], mesh.shape["col"]

    def vmem(*dims, dtype=F32):
        return pltpu.VMEM(dims, dtype)

    n_copies = 12 + 2 * (2 * (n_col - 1) + (n_row - 1) + 16)
    scratch = [
        vmem(2, ROWS, COLS, dtype=jnp.int32), vmem(ROWS, COLS, dtype=jnp.int32),
        vmem(2, ROWS, 128), vmem(2, ROWS, 128),
        vmem(2, 3, HALO, COLS), vmem(2, 2, HALO, COLS, dtype=jnp.int32), vmem(2, HALO, COLS, dtype=jnp.int32),
        vmem(2, 2, ROWS, 128), vmem(4, 2, HALO, 128),
        vmem(6, 3, NAT, 128), vmem(3, K * 8, 128), vmem(3, (K + 1) * 8, 128),
        vmem(3, 3, K * 8, 128), vmem(4, 3, K * 8, 128), vmem(3, K * 8, 128),
        vmem(3, 3, (K + 4) * 8, 128), vmem(3, 3, (K + 4) * 8, 128), vmem(4, 2, 3, 3, 8, 128),
        vmem(3, 2, ROWS, 128), vmem(1, ROWS, 128), vmem(1, ROWS, 128),
        vmem(3, KL * 8, 128), vmem(KL * 8, 128), vmem((KL + 1) * 8, 128),
        vmem(4, KL * 8, 128), vmem(KL * 8, 128), vmem(KL * 8, 128), vmem(3, KL * 8, 128),
        vmem(3, (KL + 2) * 8, 128), vmem(3, (KL + 2) * 8, 128),
        vmem(11, LNAT, 128), vmem(3, LNAT, 128), vmem(8, LROWS, 128),
        vmem(LROWS, 128), vmem(LROWS, 128), vmem(CROWS, 128),
        vmem(2, n_col, CROWS, 128), vmem(2, n_row * CROWS, 128), vmem(2, n_col, BROWS, 128),
        vmem(CROWS, 128), vmem(n_row * CROWS, 128), vmem(BROWS, 128), vmem(3, BROWS, 128),
        vmem(2, 2, 3, 2, HALO, 128), vmem(2, 2, 1, ROWS, 128), vmem(2, 4, 1, HALO, 128),
        vmem(2, 2, 8, LHALO, 128), vmem(2, 2, LROWS, 128), vmem(2, 4, LHALO, 128),
        pltpu.SemaphoreType.DMA((12,)),
        pltpu.SemaphoreType.DMA((n_copies,)), pltpu.SemaphoreType.DMA((n_copies,)),
    ]
    call = pl.pallas_call(
        functools.partial(kernel, n_row, n_col),
        out_shape=[shape(3, ROWS, COLS)] * 2,
        in_specs=[IN_ANY] * 3 + [IN_VMEM] * 5,
        out_specs=[IN_ANY] * 2,
        scratch_shapes=scratch,
        compiler_params=pltpu.CompilerParams(collective_id=0, has_side_effects=True, vmem_limit_bytes=VMEM_LIMIT),
    )
    consts = tables(n_row, n_col)

    def local(sources, edge_codes, seam_labels):
        return tuple(call(sources, edge_codes, seam_labels, *consts))

    spec = P(None, "row", "col")
    return jax.shard_map(
        local, mesh=mesh, in_specs=(spec, spec, P("row", "col")), out_specs=(spec, spec), check_vma=False
    )
```

```python
import functools
import math

import jax
import jax.numpy as jnp
import numpy as np
from jax import lax
from jax.experimental import pallas as pl
from jax.experimental.pallas import tpu as pltpu
from jax.sharding import PartitionSpec as P

SWEEPS = 4
SCREEN = 2e-05
SEAM = 0.2
COARSE_SCALE = 0.0625
F32 = jnp.float32
MESH = pl.DeviceIdType.MESH
HIGHEST = lax.Precision.HIGHEST

ROWS, COLS = 512, 256
PAD = 48
HALO = 32
K = (ROWS + 2 * PAD) // 8
NAT = 8 + ROWS + 2 * PAD + 8
LROWS, LCOLS = 128, 64
LPAD = PAD // 4
LHALO = 16
KL = (LROWS + 2 * LPAD) // 8
LNAT = LROWS + 2 * LHALO
CROWS, CCOLS = 32, 16
BROWS = CROWS + 16
VMEM_LIMIT = 62 * 1024 * 1024


def chebyshev_weight(sweep_index):
    return 1.0 / (1.25 + 0.75 * math.cos(math.pi * (2 * sweep_index + 1) / (2 * SWEEPS)))


def lane_iota():
    return lax.broadcasted_iota(jnp.int32, (8, 128), 1)


def sub_iota():
    return lax.broadcasted_iota(jnp.int32, (8, 128), 0)


def lroll(x, shift):
    shift = shift % 128
    return x if shift == 0 else pltpu.roll(x, shift, 1)


def rows8(k):
    return pl.ds(pl.multiple_of(k * 8, 8), 8)


def lanes_take(x, idx):
    return jnp.take_along_axis(x, idx, axis=1)


def left_of(tiles, lane):
    rolled = [lroll(x, 1) for x in tiles]
    return [jnp.where(lane == 0, rolled[(t + 2) % 3], rolled[t]) for t in range(3)]


def set_pads(ref, lead, count):
    last = ref[lead + (rows8(count), slice(None))]
    first = ref[lead + (rows8(1), slice(None))]
    ref[lead + (rows8(0), slice(None))] = pltpu.roll(last, 1, 0)
    ref[lead + (rows8(count + 1), slice(None))] = pltpu.roll(first, 7, 0)


def pack_fine(tile_of, n_arrays, right, left, lane, rows):
    def body(i, carry):
        r = rows8(i)
        for first in range(0, n_arrays, 4):
            out_r = out_l = jnp.zeros((8, 128), F32)
            for a in range(first, min(first + 4, n_arrays)):
                g = a - first
                here = (lane >= 32 * g) & (lane < 32 * g + 32)
                out_r = jnp.where(here, lroll(tile_of(a, 1, r), 32 * g - 96), out_r)
                out_l = jnp.where(here, lroll(tile_of(a, 0, r), 32 * g), out_l)
            right[first // 4, r, :] = out_r
            left[first // 4, r, :] = out_l
        return carry

    lax.fori_loop(0, rows // 8, body, 0)


def unpack_fine(nat, n_arrays, at, count, from_left, from_right, lane):
    def body(i, carry):
        src = rows8(i)
        dst = pl.ds(pl.multiple_of(at + i * 8, 8), 8)
        for a in range(n_arrays):
            g = a % 4
            l = lroll(from_left[a // 4, src, :], 96 - 32 * g)
            r = lroll(from_right[a // 4, src, :], -32 * g)
            nat[a, 2, dst, :] = jnp.where(lane < 32, r, jnp.where(lane >= 96, l, 0.0))
        return carry

    lax.fori_loop(0, count, body, 0)


def zero_ends(nat, n_arrays):
    zero = jnp.zeros((8, 128), F32)
    for a in range(n_arrays):
        for t in range(3):
            for r in (0, 8, 16, NAT - 24, NAT - 16, NAT - 8):
                nat[a, t, r : r + 8, :] = zero


def unpack_columns(nat, n_arrays, cols, corners, lane):
    unpack_fine(nat, n_arrays, 8 + PAD, ROWS // 8, cols.at[0], cols.at[1], lane)
    unpack_fine(nat, n_arrays, 8 + PAD - HALO, HALO // 8, corners.at[0], corners.at[1], lane)
    unpack_fine(nat, n_arrays, 8 + PAD + ROWS, HALO // 8, corners.at[2], corners.at[3], lane)


CPAD = 64
EDGE, EDGE_RIGHT, EDGE_LEFT = 11, 96, 21


def pack_field(nat, right, left):
    lane = lane_iota()

    def body(i, carry):
        r = pl.ds(pl.multiple_of(8 + PAD + i * 8, 8), 8)
        out_r = out_l = jnp.zeros((8, 128), F32)
        for q in range(9):
            x = nat[q // 3, q % 3, r, :]
            here = (lane >= EDGE * q) & (lane < EDGE * q + EDGE)
            out_r = jnp.where(here, lroll(x, EDGE * q - EDGE_RIGHT), out_r)
            out_l = jnp.where(here, lroll(x, EDGE * q - EDGE_LEFT), out_l)
        right[rows8(i), :] = out_r
        left[rows8(i), :] = out_l
        return carry

    lax.fori_loop(0, ROWS // 8, body, 0, unroll=2)


def unpack_field(nat, at, count, own, from_left, from_right):
    lane = lane_iota()

    def body(i, carry):
        dst = pl.ds(pl.multiple_of(at + i * 8, 8), 8)
        l, r = from_left[rows8(i), :], from_right[rows8(i), :]
        for ch in range(3):
            for t in range(3):
                p = 3 * lane + t
                u = (t + 1) % 3
                a = lroll(l, EDGE_RIGHT - (86 if u == 0 else 85) - EDGE * (3 * ch + u))
                u = (t + 2) % 3
                b = lroll(r, EDGE_LEFT + (86 if u == 2 else 85) - EDGE * (3 * ch + u))
                x = jnp.where((p >= CPAD - HALO) & (p < CPAD), a, own(ch, t, i, dst))
                x = jnp.where((p >= CPAD + COLS) & (p < CPAD + COLS + HALO), b, x)
                nat[ch, t, dst, :] = x
        return carry

    lax.fori_loop(0, count, body, 0)


def dealt(x, lane):
    out = []
    for t in range(3):
        p = 3 * lane + t
        got = [lanes_take(y, (p - CPAD) % 128) for y in x]
        out.append(jnp.where((p < 64) | (p >= 320), got[2], jnp.where(p < 192, got[0], got[1])))
    return out


def undealt(x, lane):
    out = []
    for t in range(2):
        p = lane + (128 * t + CPAD)
        got = [lanes_take(y, p // 3) for y in x]
        out.append(jnp.where(p % 3 == 0, got[0], jnp.where(p % 3 == 1, got[1], got[2])))
    return out


def natural_place(k, t, lane, sub, row0, col0):
    row = row0 - PAD + sub * K + k
    if t < 2:
        return row, lane + (col0 + 128 * t)
    return row, jnp.where(lane < 64, lane + (col0 + 256), lane + (col0 - 128))


def fine_inside(k, t, lane, sub, row0, col0, n_rows, n_cols):
    row = row0 - PAD + sub * K + k
    col = 3 * lane + (t - CPAD + col0)
    return (row >= 0) & (row < n_rows) & (col >= 0) & (col < n_cols)


def level_inside(k, lane, sub, row0, col0, n_rows, n_cols):
    row = row0 - LPAD + sub * KL + k
    col = lane - LHALO + col0
    return (row >= 0) & (row < n_rows) & (col >= 0) & (col < n_cols) & (lane < 96)


def stencil_pass(v, wt, emit, unroll, end=None):
    def row(k):
        w = [[wt[n, t, rows8(k), :] for t in range(3)] for n in range(4)]
        for ch in range(3):
            here = [v[ch, t, rows8(k + 1), :] for t in range(3)]
            left = [lroll(here[2], 1), here[0], here[1]]
            right = [here[1], here[2], lroll(here[0], 127)]
            total = []
            for t in range(3):
                x = w[2][t] * v[ch, t, rows8(k), :] + w[3][t] * v[ch, t, rows8(k + 2), :]
                total.append(x + (w[0][t] * left[t] + w[1][t] * right[t]))
            emit(k, ch, here, total)

    def body(m, carry):
        for q in range(unroll):
            row(unroll * m + q)
        if end is not None:
            end(m)
        return carry

    lax.fori_loop(0, K // unroll, body, 0)


def fine_pads(v):
    for ch in range(3):
        for t in range(3):
            set_pads(v, (ch, t), K)


def fine_sweep(vin, vout, sp, wt, omega):
    def emit(k, ch, here, total):
        for t in range(3):
            new = sp[ch, t, rows8(k), :] + total[t]
            vout[ch, t, rows8(k + 1), :] = (1.0 - omega) * here[t] + omega * new

    stencil_pass(vin, wt, emit, 4)
    fine_pads(vout)


def fine_first(vout, sp):
    omega = chebyshev_weight(0)

    def body(k, carry):
        for ch in range(3):
            for t in range(3):
                vout[ch, t, rows8(k + 1), :] = omega * sp[ch, t, rows8(k), :]
        return carry

    lax.fori_loop(0, K, body, 0)
    fine_pads(vout)


def fine_smooth(va, vb, sp, wt, from_zero):
    bufs = [va, vb]
    at = 0
    for i in range(SWEEPS):
        if i == 0 and from_zero:
            fine_first(va, sp)
            continue
        fine_sweep(bufs[at], bufs[1 - at], sp, wt, chebyshev_weight(i))
        at = 1 - at
    return bufs[at], bufs[1 - at]


def pick(x, lane):
    got = [lanes_take(y, jnp.minimum((4 * lane) // 3, 127)) for y in x]
    return jnp.where(lane % 3 == 0, got[0], jnp.where(lane % 3 == 1, got[1], got[2]))


def to_level(x, lane):
    after = [lroll(y, 127) for y in x]
    mid, first = x[1] + x[2], after[0] + after[1]
    sums = [x[0] + mid + after[0], mid + first, x[2] + first + after[2]]
    return pick(sums, lane)


def fine_residual_to_level(v, sp, wt, dg, lsrc):
    lane = lane_iota()
    acc = {}

    def emit(k, ch, here, total):
        res = [dg[t, rows8(k), :] * (sp[ch, t, rows8(k), :] - here[t] + total[t]) for t in range(3)]
        acc[ch] = [a + b for a, b in zip(acc[ch], res)] if ch in acc else res

    def end(m):
        for ch in range(3):
            lsrc[ch, rows8(m), :] = to_level(acc.pop(ch), lane) * 0.0625

    stencil_pass(v, wt, emit, 4, end)


def level_weights(fx, fy, lw, ld, li, where):
    lane, sub = lane_iota(), sub_iota()
    fy[rows8(KL), :] = pltpu.roll(fy[rows8(0), :], 7, 0)

    def body(k, carry):
        left, up, down = fx[rows8(k), :], fy[rows8(k), :], fy[rows8(k + 1), :]
        right = lroll(left, 127)
        diag = SCREEN + left + right + up + down
        inv = jnp.where(level_inside(k, lane, sub, *where), 1.0 / diag, 0.0)
        ld[rows8(k), :] = diag
        li[rows8(k), :] = inv
        for n, face in enumerate((left, right, up, down)):
            lw[n, rows8(k), :] = face * inv
        return carry

    lax.fori_loop(0, KL, body, 0)


def level_neighbours(f, lw, k, ch):
    here = f[ch, rows8(k + 1), :]
    total = lw[0, rows8(k), :] * lroll(here, 1) + lw[1, rows8(k), :] * lroll(here, 127)
    return here, total + lw[2, rows8(k), :] * f[ch, rows8(k), :] + lw[3, rows8(k), :] * f[ch, rows8(k + 2), :]


def level_pads(f):
    for ch in range(3):
        set_pads(f, (ch,), KL)


def level_smooth(fa, fb, lsp, lw, from_zero):
    bufs = [fa, fb]
    at = 0
    for i in range(SWEEPS):
        omega = chebyshev_weight(i)
        src, dst = bufs[at], bufs[1 - at]
        if i == 0 and from_zero:

            def first(k, carry):
                for ch in range(3):
                    src[ch, rows8(k + 1), :] = omega * lsp[ch, rows8(k), :]
                return carry

            lax.fori_loop(0, KL, first, 0, unroll=True)
            level_pads(src)
            continue

        def body(k, carry):
            for ch in range(3):
                here, total = level_neighbours(src, lw, k, ch)
                dst[ch, rows8(k + 1), :] = (1.0 - omega) * here + omega * (lsp[ch, rows8(k), :] + total)
            return carry

        lax.fori_loop(0, KL, body, 0, unroll=True)
        level_pads(dst)
        at = 1 - at
    return bufs[at]


def level_down(lsrc, li, ld, lw, lsp, fa, fb, lnat, lev, lpr, lpl, g):
    lane = lane_iota()

    def scale(k, carry):
        for ch in range(3):
            lsp[ch, rows8(k), :] = lsrc[ch, rows8(k), :] * li[rows8(k), :]
        return carry

    lax.fori_loop(0, KL, scale, 0, unroll=True)
    f = level_smooth(fa, fb, lsp, lw, True)

    def out(k, carry):
        at = pl.ds(LHALO - LPAD + k, 8, stride=KL)
        for ch in range(3):
            here, total = level_neighbours(f, lw, k, ch)
            lnat[8 + ch, at, :] = ld[rows8(k), :] * (lsp[ch, rows8(k), :] - here + total)
            lnat[ch, at, :] = here
            lnat[3 + ch, at, :] = lsrc[ch, rows8(k), :]
        return carry

    lax.fori_loop(0, KL, out, 0, unroll=True)

    def copy(i, carry):
        src = pl.ds(pl.multiple_of(LHALO + i * 8, 8), 8)
        right = left = jnp.zeros((8, 128), F32)
        for a in range(8):
            x = lnat[a, src, :]
            lev[a, rows8(i), :] = x
            here = (lane >= 16 * a) & (lane < 16 * a + 16)
            right = jnp.where(here, lroll(x, 16 * a - 64), right)
            left = jnp.where(here, lroll(x, 16 * a - 16), left)
        lpr[rows8(i), :] = right
        lpl[rows8(i), :] = left
        return carry

    lax.fori_loop(0, LROWS // 8, copy, 0)
    idx = (LHALO + 4 * lane) % 128
    for i in range(CROWS // 8):
        total = jnp.zeros((8, 128), F32)
        for ch in range(3):
            x = sum(lnat[8 + ch, pl.ds(LHALO + 32 * i + q, 8, stride=4), :] for q in range(4))
            x = x + lroll(x, 127)
            x = x + lroll(x, 126)
            x = jnp.where(lane < CCOLS, lanes_take(x, idx), 0.0) * 0.0625
            total = total + lroll(x, CCOLS * ch)
        g[i * 8 : i * 8 + 8, :] = total


def level_up(lev, lrows, lcols, lcorn, corr, lnat, lnc, fx, fy, lw, ld, li, lsp, fa, fb, where):
    lane, sub = lane_iota(), sub_iota()

    def place(dst_row, count, own, left, right):
        def body(i, carry):
            dst = pl.ds(pl.multiple_of(dst_row + i * 8, 8), 8)
            l, r = left(rows8(i)), right(rows8(i))
            for a in range(8):
                x = jnp.where((lane >= 80) & (lane < 96), lroll(r, 80 - 16 * a), 0.0)
                x = jnp.where((lane >= 16) & (lane < 80), own(a, rows8(i)), x)
                lnat[a, dst, :] = jnp.where(lane < 16, lroll(l, -16 * a), x)
            return carry

        lax.fori_loop(0, count, body, 0)

    place(0, LHALO // 8, lambda a, r: lrows[0, a, r, :], lambda r: lcorn[0, r, :], lambda r: lcorn[1, r, :])
    place(LHALO, LROWS // 8, lambda a, r: lev[a, r, :], lambda r: lcols[0, r, :], lambda r: lcols[1, r, :])
    place(LHALO + LROWS, LHALO // 8, lambda a, r: lrows[1, a, r, :], lambda r: lcorn[2, r, :], lambda r: lcorn[3, r, :])
    for ch in range(3):
        for h in range(LNAT // 32):
            x = corr[ch, 4 + 8 * h : 12 + 8 * h, :]
            for q in range(4):
                lnc[ch, pl.ds(32 * h + q, 8, stride=4), :] = x

    def faces(k, carry):
        at = pl.ds(LHALO - LPAD + k, 8, stride=KL)
        fx[rows8(k), :] = lnat[6, at, :]
        fy[rows8(k), :] = lnat[7, at, :]
        return carry

    lax.fori_loop(0, KL, faces, 0)
    level_weights(fx, fy, lw, ld, li, where)

    def fields(k, carry):
        at = pl.ds(LHALO - LPAD + k, 8, stride=KL)
        inside = level_inside(k, lane, sub, *where)
        inv = li[rows8(k), :]
        for ch in range(3):
            fa[ch, rows8(k + 1), :] = jnp.where(inside, lnat[ch, at, :] + lnc[ch, at, :], 0.0)
            lsp[ch, rows8(k), :] = lnat[3 + ch, at, :] * inv
        return carry

    lax.fori_loop(0, KL, fields, 0, unroll=True)
    level_pads(fa)
    return level_smooth(fa, fb, lsp, lw, False)


def fine_up(vrows, vcols, vcorn, field, nat, va, where):
    lane, sub = lane_iota(), sub_iota()
    unpack_field(nat, 8 + PAD, ROWS // 8, lambda ch, t, i, r: nat[ch, t, r, :], vcols.at[0], vcols.at[1])
    for slot, at in ((0, 8 + PAD - HALO), (1, 8 + PAD + ROWS)):
        own = lambda ch, t, i, r, slot=slot: vrows[slot, ch, t, rows8(i), :]
        unpack_field(nat, at, HALO // 8, own, vcorn.at[2 * slot], vcorn.at[2 * slot + 1])

    def body(kl, carry):
        for t in range(3):
            idx = jnp.minimum((3 * lane + t) // 4, 127)
            inside = [fine_inside(kl * 4 + q, t, lane, sub, *where) for q in range(4)]
            for ch in range(3):
                add = lanes_take(field[ch, rows8(kl + 1), :], idx)
                for q in range(4):
                    x = nat[ch, t, pl.ds(8 + kl * 4 + q, 8, stride=K), :] + add
                    va[ch, t, rows8(kl * 4 + q + 1), :] = jnp.where(inside[q], x, 0.0)
        return carry

    lax.fori_loop(0, KL, body, 0)
    fine_pads(va)


def field_out(field, nat, vpr, vpl):
    def body(m, carry):
        for q in range(2):
            k = 2 * m + q
            for ch in range(3):
                for t in range(3):
                    nat[ch, t, pl.ds(8 + k, 8, stride=K), :] = field[ch, t, rows8(k + 1), :]
        return carry

    lax.fori_loop(0, K // 2, body, 0)
    pack_field(nat, vpr, vpl)


def positions(n_row, n_col):
    i, j = lax.axis_index("row"), lax.axis_index("col")
    fine = (i * ROWS, j * COLS, n_row * ROWS, n_col * COLS)
    level = (i * LROWS, j * LCOLS, n_row * LROWS, n_col * LCOLS)
    return fine, level


TOP, LOW = pl.ds(0, HALO), pl.ds(ROWS - HALO, HALO)
LTOP, LLOW = pl.ds(0, LHALO), pl.ds(LROWS - LHALO, LHALO)
MID = pl.ds(8 + PAD, ROWS)
FIRST, LAST = pl.ds(8 + PAD, HALO), pl.ds(8 + PAD + ROWS - HALO, HALO)
ABOVE, BELOW = pl.ds(8 + PAD - HALO, HALO), pl.ds(8 + PAD + ROWS, HALO)


class Sender:
    def __init__(self, send_sems, recv_sems):
        self.send_sems, self.recv_sems, self.count = send_sems, recv_sems, 0

    def __call__(self, src, dst, device):
        n = self.count
        self.count += 1
        copy = pltpu.make_async_remote_copy(
            src_ref=src, dst_ref=dst, send_sem=self.send_sems.at[n], recv_sem=self.recv_sems.at[n],
            device_id=device, device_id_type=MESH,
        )
        copy.start()
        return copy


def fine_operator(nat, fxp, fyp, sp, wt, dg, lfx, lfy, lnat, where):
    lane, sub = lane_iota(), sub_iota()

    def edge(code, a, b):
        return jnp.exp2(code * 0.25 - 2.0) * jnp.where(a != b, SEAM, 1.0)

    def faces(k, carry):
        at, above = pl.ds(8 + k, 8, stride=K), pl.ds(7 + k, 8, stride=K)
        code = left_of([nat[3, t, at, :] for t in range(3)], lane)
        label = [nat[5, t, at, :] for t in range(3)]
        beside = left_of(label, lane)
        fx, fy = [], []
        for t in range(3):
            row, col = natural_place(k, t, lane, sub, where[0], where[1])
            inner = edge(code[t], beside[t], label[t])
            fx.append(jnp.where((col >= 1) & (col < where[3]), inner, 1.0))
            inner = edge(nat[4, t, above, :], nat[5, t, above, :], label[t])
            fy.append(jnp.where((row >= 1) & (row < where[2]), inner, 1.0))
        for t, x in enumerate(dealt(fx, lane)):
            fxp[t, rows8(k), :] = x
        for t, x in enumerate(dealt(fy, lane)):
            fyp[t, rows8(k), :] = x
        return carry

    lax.fori_loop(0, K, faces, 0, unroll=2)
    for t in range(3):
        fyp[t, rows8(K), :] = pltpu.roll(fyp[t, rows8(0), :], 7, 0)

    def weights(k, carry):
        left = [fxp[t, rows8(k), :] for t in range(3)]
        right = [left[1], left[2], lroll(left[0], 127)]
        at = pl.ds(8 + k, 8, stride=K)
        scale = []
        for t in range(3):
            up, down = fyp[t, rows8(k), :], fyp[t, rows8(k + 1), :]
            diag = SCREEN + left[t] + right[t] + up + down
            inv = jnp.where(fine_inside(k, t, lane, sub, *where), 1.0 / diag, 0.0)
            scale.append(inv)
            dg[t, rows8(k), :] = diag
            for n, face in enumerate((left[t], right[t], up, down)):
                wt[n, t, rows8(k), :] = face * inv
        for ch in range(3):
            for t, x in enumerate(dealt([nat[ch, t, at, :] for t in range(3)], lane)):
                sp[ch, t, rows8(k), :] = x * scale[t]
        return carry

    lax.fori_loop(0, K, weights, 0, unroll=2)

    def level_faces(kl, carry):
        rows = [sum(fxp[t, rows8(kl * 4 + q), :] for q in range(4)) for t in range(3)]
        x = pick(rows, lane) * 0.0625
        y = to_level([fyp[t, rows8(kl * 4), :] for t in range(3)], lane) * 0.0625
        at = pl.ds(LHALO - LPAD + kl, 8, stride=KL)
        lfx[rows8(kl), :] = x
        lfy[rows8(kl), :] = y
        lnat[6, at, :] = x
        lnat[7, at, :] = y
        return carry

    lax.fori_loop(0, KL, level_faces, 0)


def coarse_solve(
    n_row, n_col, place, send, g, s_cols, s_ext, t_back, row_eig, col_eig, nat, vpr, vpl, lev, lpr, lpl,
    vrows, vcols, vcorn, lrows, lcols, lcorn, one, two, three, mine, spec, back, corr,
):
    i, j, up, down, left, right = place
    n_modes = n_row * CROWS
    lane = lane_iota()

    first = [send(g, one.at[j], (i, lax.rem(j + d, n_col))) for d in range(1, n_col)]
    one[j] = g[...]
    halos = [
        send(lpr, lcols.at[0], (i, right)),
        send(lpl, lcols.at[1], (i, left)),
        send(lev.at[:, LTOP, :], lrows.at[1], (up, j)),
        send(lev.at[:, LLOW, :], lrows.at[0], (down, j)),
        send(lpr.at[LLOW, :], lcorn.at[0], (down, right)),
        send(lpl.at[LLOW, :], lcorn.at[1], (down, left)),
        send(lpr.at[LTOP, :], lcorn.at[2], (up, right)),
        send(lpl.at[LTOP, :], lcorn.at[3], (up, left)),
    ]
    for copy in first:
        copy.wait()

    def placed(ref, n_rows):
        out = []
        for ch in range(3):
            parts = []
            for r in range(n_rows // 8):
                x = jnp.zeros((8, 128), F32)
                for p in range(n_col):
                    here = (lane >= CCOLS * p) & (lane < CCOLS * p + CCOLS)
                    y = lroll(ref[p, r * 8 : r * 8 + 8, :], CCOLS * (p - ch))
                    x = jnp.where(here, y, x)
                parts.append(x)
            out.append(jnp.concatenate(parts, axis=0))
        return out

    x = jnp.concatenate(placed(one, CROWS), axis=0)
    x = jnp.dot(x, s_cols[j], precision=HIGHEST, preferred_element_type=F32)
    total = lax.slice_in_dim(x, 0, CROWS)
    for ch in (1, 2):
        total = total + pltpu.roll(lax.slice_in_dim(x, CROWS * ch, CROWS * ch + CROWS), CCOLS * ch, 1)
    mine[...] = total
    own = pl.ds(pl.multiple_of(i * CROWS, CROWS), CROWS)
    second = [send(mine, two.at[own, :], (lax.rem(i + d, n_row), j)) for d in range(1, n_row)]
    two[own, :] = total
    halos += [
        send(vpr, vcols.at[0], (i, right)),
        send(vpl, vcols.at[1], (i, left)),
        send(vpr.at[LOW, :], vcorn.at[0], (down, right)),
        send(vpl.at[LOW, :], vcorn.at[1], (down, left)),
        send(vpr.at[TOP, :], vcorn.at[2], (up, right)),
        send(vpl.at[TOP, :], vcorn.at[3], (up, left)),
    ]
    for copy in second:
        copy.wait()
    halos += [
        send(nat.at[pl.ds(0, 3), :, FIRST, :], vrows.at[1], (up, j)),
        send(nat.at[pl.ds(0, 3), :, LAST, :], vrows.at[0], (down, j)),
    ]
    y = jnp.dot(s_ext[8 : 8 + n_modes, :], two[...], precision=HIGHEST, preferred_element_type=F32)
    eig = SCREEN + COARSE_SCALE * (row_eig[...] + col_eig[pl.ds(j, 1), :])
    spec[...] = y / eig
    rows = s_ext[pl.ds(pl.multiple_of(i * CROWS, CROWS), BROWS), :]
    z = jnp.dot(rows, spec[...], precision=HIGHEST, preferred_element_type=F32)
    back[...] = z
    third = [send(back, three.at[j], (i, lax.rem(j + d, n_col))) for d in range(1, n_col)]
    three[j] = z
    for copy in third:
        copy.wait()
    z = jnp.concatenate(placed(three, BROWS), axis=0)
    z = jnp.dot(z, t_back[j], precision=HIGHEST, preferred_element_type=F32)
    for ch in range(3):
        corr[ch] = lax.slice_in_dim(z, BROWS * ch, BROWS * ch + BROWS)
    for copy in halos:
        copy.wait()


def kernel(n_row, n_col, src, codes, labels, *refs):
    s_cols, s_ext, t_back, row_eig, col_eig, solution_out, residual_out = refs[:7]
    (
        codes_v, labels_v, right_pack, left_pack, srows, crows, labrows, cols, corners,
        nat, fxp, fyp, sp, wt, dg, va, vb, vpr, vpl,
        lsrc, lfx, lfy, lw, ld, li, lsp, fa, fb, lnat, lnc, lev, lpr, lpl, g,
        one, two, three, mine, spec, back, corr,
        vrows, vcols, vcorn, lrows, lcols, lcorn,
        copy_sems, send_sems, recv_sems,
    ) = refs[7:]
    i, j = lax.axis_index("row"), lax.axis_index("col")
    up, down = lax.rem(i + n_row - 1, n_row), lax.rem(i + 1, n_row)
    left, right = lax.rem(j + n_col - 1, n_col), lax.rem(j + 1, n_col)
    where, lwhere = positions(n_row, n_col)
    lane = lane_iota()

    barrier = pltpu.get_barrier_semaphore()
    peers = [(i, lax.rem(j + d, n_col)) for d in range(1, n_col)]
    peers += [(lax.rem(i + d, n_row), j) for d in range(1, n_row)]
    peers += [(r, c) for r in (up, down) for c in (left, right)]
    for peer in peers:
        pl.semaphore_signal(barrier, inc=1, device_id=peer, device_id_type=MESH)

    loads = [pltpu.make_async_copy(codes, codes_v, copy_sems.at[0])]
    loads.append(pltpu.make_async_copy(labels, labels_v, copy_sems.at[1]))
    for a in range(3):
        for t in range(2):
            part = src.at[a, :, pl.ds(128 * t, 128)]
            loads.append(pltpu.make_async_copy(part, nat.at[a, t, MID, :], copy_sems.at[len(loads)]))
    for copy in loads:
        copy.start()
    zero_ends(nat, 6)
    for copy in loads:
        copy.wait()

    def convert(n, carry):
        r = rows8(n)
        at = pl.ds(pl.multiple_of(8 + PAD + 8 * n, 8), 8)
        for t in range(2):
            c = slice(128 * t, 128 * t + 128)
            nat[3, t, at, :] = codes_v[0, r, c].astype(F32)
            nat[4, t, at, :] = codes_v[1, r, c].astype(F32)
            nat[5, t, at, :] = labels_v[r, c].astype(F32)
        return carry

    lax.fori_loop(0, ROWS // 8, convert, 0, unroll=2)

    def natural(a, t, r):
        return nat[a, t, pl.ds(pl.multiple_of(8 + PAD + r.start, 8), 8), :]

    pack_fine(natural, 6, right_pack, left_pack, lane, ROWS)
    pl.semaphore_wait(barrier, n_col + n_row + 2)
    send = Sender(send_sems, recv_sems)
    copies = [
        send(right_pack, cols.at[0], (i, right)),
        send(left_pack, cols.at[1], (i, left)),
    ]
    for slot, rows, device in ((1, TOP, up), (0, LOW, down)):
        copies.append(send(src.at[:, rows, :], srows.at[slot], (device, j)))
        copies.append(send(codes.at[:, rows, :], crows.at[slot], (device, j)))
        copies.append(send(labels.at[rows, :], labrows.at[slot], (device, j)))
    copies.append(send(right_pack.at[:, LOW, :], corners.at[0], (down, right)))
    copies.append(send(left_pack.at[:, LOW, :], corners.at[1], (down, left)))
    copies.append(send(right_pack.at[:, TOP, :], corners.at[2], (up, right)))
    copies.append(send(left_pack.at[:, TOP, :], corners.at[3], (up, left)))
    for copy in copies:
        copy.wait()

    for t in range(2):
        c = slice(128 * t, 128 * t + 128)
        for slot, rows in ((0, ABOVE), (1, BELOW)):
            for a in range(3):
                nat[a, t, rows, :] = srows[slot, a, :, c]
            for a in range(2):
                nat[3 + a, t, rows, :] = crows[slot, a, :, c].astype(F32)
            nat[5, t, rows, :] = labrows[slot, :, c].astype(F32)
    unpack_columns(nat, 6, cols, corners, lane)
    fine_operator(nat, fxp, fyp, sp, wt, dg, lfx, lfy, lnat, where)
    level_weights(lfx, lfy, lw, ld, li, lwhere)

    field, other = fine_smooth(va, vb, sp, wt, True)
    for cycle in range(2):
        fine_residual_to_level(field, sp, wt, dg, lsrc)
        level_down(lsrc, li, ld, lw, lsp, fa, fb, lnat, lev, lpr, lpl, g)
        field_out(field, nat, vpr, vpl)
        got = [ref.at[cycle] for ref in (vrows, vcols, vcorn, lrows, lcols, lcorn, one, two, three)]
        coarse_solve(
            n_row, n_col, (i, j, up, down, left, right), send, g, s_cols, s_ext, t_back, row_eig, col_eig,
            nat, vpr, vpl, lev, lpr, lpl, *got, mine, spec, back, corr,
        )
        level = level_up(
            lev, got[3], got[4], got[5], corr, lnat, lnc, lfx, lfy, lw, ld, li, lsp, fa, fb, lwhere
        )
        fine_up(got[0], got[1], got[2], level, nat, va, where)
        field, other = fine_smooth(va, vb, sp, wt, False)
        if cycle == 0:
            field, other = fine_smooth(field, other, sp, wt, False)

    def emit(k, ch, here, total):
        at = pl.ds(8 + k, 8, stride=K)
        res = [dg[t, rows8(k), :] * (sp[ch, t, rows8(k), :] - here[t] + total[t]) for t in range(3)]
        for t, x in enumerate(undealt(here, lane)):
            nat[ch, t, at, :] = x
        for t, x in enumerate(undealt(res, lane)):
            nat[3 + ch, t, at, :] = x

    stencil_pass(field, wt, emit, 2)
    stores = []
    for a in range(6):
        for t in range(2):
            out = (solution_out if a < 3 else residual_out).at[a % 3, :, pl.ds(128 * t, 128)]
            stores.append(pltpu.make_async_copy(nat.at[a, t, MID, :], out, copy_sems.at[len(stores)]))
    for copy in stores:
        copy.start()
    for copy in stores:
        copy.wait()


@functools.lru_cache(maxsize=None)
def tables(n_row, n_col):
    def sines(n):
        k = np.arange(1, n + 1)
        return math.sqrt(2.0 / (n + 1)) * np.sin(np.pi * ((k[:, None] * k[None, :]) % (2 * (n + 1))) / (n + 1))

    def eig(n):
        return 2.0 - 2.0 * np.cos(np.pi * np.arange(1, n + 1) / (n + 1))

    nr, nc = n_row * CROWS, n_col * CCOLS
    rows, cols = sines(nr), sines(nc)
    s_cols = np.zeros((n_col, 128, 128))
    t_back = np.zeros((n_col, 128, 128))
    col_eig = np.ones((n_col, 128))
    lane = np.arange(128)
    for j in range(n_col):
        own = slice(CCOLS * j, CCOLS * j + CCOLS)
        s_cols[j, :nc, :CCOLS] = cols[:, own]
        col_eig[j, : 3 * CCOLS] = np.tile(eig(nc)[own], 3)
        c = LCOLS * j + lane - LHALO
        ok = (c >= 0) & (c < n_col * LCOLS) & (lane < 96)
        t_back[j, :nc, ok] = cols[:, c[ok] // 4].T
    s_ext = np.zeros((nr + 16, nr))
    s_ext[8 : 8 + nr] = rows
    row_eig = np.repeat(eig(nr)[:, None], 128, axis=1)
    return tuple(x.astype(np.float32) for x in (s_cols, s_ext, t_back, row_eig, col_eig))


def shape(*dims, dtype=F32):
    return jax.ShapeDtypeStruct(dims, dtype)


IN_VMEM = pl.BlockSpec(memory_space=pltpu.VMEM)
IN_ANY = pl.BlockSpec(memory_space=pl.ANY)


def solution(mesh):
    n_row, n_col = mesh.shape["row"], mesh.shape["col"]

    def vmem(*dims, dtype=F32):
        return pltpu.VMEM(dims, dtype)

    n_copies = 12 + 2 * (2 * (n_col - 1) + (n_row - 1) + 16)
    scratch = [
        vmem(2, ROWS, COLS, dtype=jnp.int32), vmem(ROWS, COLS, dtype=jnp.int32),
        vmem(2, ROWS, 128), vmem(2, ROWS, 128),
        vmem(2, 3, HALO, COLS), vmem(2, 2, HALO, COLS, dtype=jnp.int32), vmem(2, HALO, COLS, dtype=jnp.int32),
        vmem(2, 2, ROWS, 128), vmem(4, 2, HALO, 128),
        vmem(6, 3, NAT, 128), vmem(3, K * 8, 128), vmem(3, (K + 1) * 8, 128),
        vmem(3, 3, K * 8, 128), vmem(4, 3, K * 8, 128), vmem(3, K * 8, 128),
        vmem(3, 3, (K + 2) * 8, 128), vmem(3, 3, (K + 2) * 8, 128),
        vmem(ROWS, 128), vmem(ROWS, 128),
        vmem(3, KL * 8, 128), vmem(KL * 8, 128), vmem((KL + 1) * 8, 128),
        vmem(4, KL * 8, 128), vmem(KL * 8, 128), vmem(KL * 8, 128), vmem(3, KL * 8, 128),
        vmem(3, (KL + 2) * 8, 128), vmem(3, (KL + 2) * 8, 128),
        vmem(11, LNAT, 128), vmem(3, LNAT, 128), vmem(8, LROWS, 128),
        vmem(LROWS, 128), vmem(LROWS, 128), vmem(CROWS, 128),
        vmem(2, n_col, CROWS, 128), vmem(2, n_row * CROWS, 128), vmem(2, n_col, BROWS, 128),
        vmem(CROWS, 128), vmem(n_row * CROWS, 128), vmem(BROWS, 128), vmem(3, BROWS, 128),
        vmem(2, 2, 3, 3, HALO, 128), vmem(2, 2, ROWS, 128), vmem(2, 4, HALO, 128),
        vmem(2, 2, 8, LHALO, 128), vmem(2, 2, LROWS, 128), vmem(2, 4, LHALO, 128),
        pltpu.SemaphoreType.DMA((12,)),
        pltpu.SemaphoreType.DMA((n_copies,)), pltpu.SemaphoreType.DMA((n_copies,)),
    ]
    call = pl.pallas_call(
        functools.partial(kernel, n_row, n_col),
        out_shape=[shape(3, ROWS, COLS)] * 2,
        in_specs=[IN_ANY] * 3 + [IN_VMEM] * 5,
        out_specs=[IN_ANY] * 2,
        scratch_shapes=scratch,
        compiler_params=pltpu.CompilerParams(collective_id=0, has_side_effects=True, vmem_limit_bytes=VMEM_LIMIT),
    )
    consts = tables(n_row, n_col)

    def local(sources, edge_codes, seam_labels):
        return tuple(call(sources, edge_codes, seam_labels, *consts))

    spec = P(None, "row", "col")
    return jax.shard_map(
        local, mesh=mesh, in_specs=(spec, spec, P("row", "col")), out_specs=(spec, spec), check_vma=False
    )
```

```python
import functools
import math

import jax
import jax.numpy as jnp
import numpy as np
from jax import lax
from jax.experimental import pallas as pl
from jax.experimental.pallas import tpu as pltpu
from jax.sharding import PartitionSpec as P

SWEEPS = 4
SCREEN = 2e-05
SEAM = 0.2
COARSE_SCALE = 0.0625
F32 = jnp.float32
MESH = pl.DeviceIdType.MESH
HIGHEST = lax.Precision.HIGHEST

ROWS, COLS = 512, 256
PAD = 48
HALO = 32
K = (ROWS + 2 * PAD) // 8
NAT = 8 + ROWS + 2 * PAD + 8
LROWS, LCOLS = 128, 64
LPAD = PAD // 4
LHALO = 16
KL = (LROWS + 2 * LPAD) // 8
LNAT = LROWS + 2 * LHALO
CROWS, CCOLS = 32, 16
BROWS = CROWS + 16
VMEM_LIMIT = 62 * 1024 * 1024


def chebyshev_weight(sweep_index):
    return 1.0 / (1.25 + 0.75 * math.cos(math.pi * (2 * sweep_index + 1) / (2 * SWEEPS)))


def lane_iota():
    return lax.broadcasted_iota(jnp.int32, (8, 128), 1)


def sub_iota():
    return lax.broadcasted_iota(jnp.int32, (8, 128), 0)


def lroll(x, shift):
    shift = shift % 128
    return x if shift == 0 else pltpu.roll(x, shift, 1)


def rows8(k):
    return pl.ds(pl.multiple_of(k * 8, 8), 8)


def lanes_take(x, idx):
    return jnp.take_along_axis(x, idx, axis=1)


def left_of(tiles, lane):
    rolled = [lroll(x, 1) for x in tiles]
    return [jnp.where(lane == 0, rolled[(t + 2) % 3], rolled[t]) for t in range(3)]


def set_pads(ref, lead, count):
    last = ref[lead + (rows8(count), slice(None))]
    first = ref[lead + (rows8(1), slice(None))]
    ref[lead + (rows8(0), slice(None))] = pltpu.roll(last, 1, 0)
    ref[lead + (rows8(count + 1), slice(None))] = pltpu.roll(first, 7, 0)


def pack_fine(tile_of, n_arrays, right, left, lane, rows):
    def body(i, carry):
        r = rows8(i)
        for first in range(0, n_arrays, 4):
            out_r = out_l = jnp.zeros((8, 128), F32)
            for a in range(first, min(first + 4, n_arrays)):
                g = a - first
                here = (lane >= 32 * g) & (lane < 32 * g + 32)
                out_r = jnp.where(here, lroll(tile_of(a, 1, r), 32 * g - 96), out_r)
                out_l = jnp.where(here, lroll(tile_of(a, 0, r), 32 * g), out_l)
            right[first // 4, r, :] = out_r
            left[first // 4, r, :] = out_l
        return carry

    lax.fori_loop(0, rows // 8, body, 0)


def unpack_fine(nat, n_arrays, at, count, from_left, from_right, lane):
    def body(i, carry):
        src = rows8(i)
        dst = pl.ds(pl.multiple_of(at + i * 8, 8), 8)
        for a in range(n_arrays):
            g = a % 4
            l = lroll(from_left[a // 4, src, :], 96 - 32 * g)
            r = lroll(from_right[a // 4, src, :], -32 * g)
            nat[a, 2, dst, :] = jnp.where(lane < 32, r, jnp.where(lane >= 96, l, 0.0))
        return carry

    lax.fori_loop(0, count, body, 0)


def zero_ends(nat, n_arrays):
    zero = jnp.zeros((8, 128), F32)
    for a in range(n_arrays):
        for t in range(3):
            for r in (0, 8, 16, NAT - 24, NAT - 16, NAT - 8):
                nat[a, t, r : r + 8, :] = zero


def unpack_columns(nat, n_arrays, cols, corners, lane):
    unpack_fine(nat, n_arrays, 8 + PAD, ROWS // 8, cols.at[0], cols.at[1], lane)
    unpack_fine(nat, n_arrays, 8 + PAD - HALO, HALO // 8, corners.at[0], corners.at[1], lane)
    unpack_fine(nat, n_arrays, 8 + PAD + ROWS, HALO // 8, corners.at[2], corners.at[3], lane)


CPAD = 64
EDGE, EDGE_RIGHT, EDGE_LEFT = 11, 96, 21


def pack_field(nat, right, left):
    lane = lane_iota()

    def body(i, carry):
        r = pl.ds(pl.multiple_of(8 + PAD + i * 8, 8), 8)
        out_r = out_l = jnp.zeros((8, 128), F32)
        for q in range(9):
            x = nat[q // 3, q % 3, r, :]
            here = (lane >= EDGE * q) & (lane < EDGE * q + EDGE)
            out_r = jnp.where(here, lroll(x, EDGE * q - EDGE_RIGHT), out_r)
            out_l = jnp.where(here, lroll(x, EDGE * q - EDGE_LEFT), out_l)
        right[rows8(i), :] = out_r
        left[rows8(i), :] = out_l
        return carry

    lax.fori_loop(0, ROWS // 8, body, 0, unroll=2)


def unpack_field(nat, at, count, own, from_left, from_right):
    lane = lane_iota()

    def body(i, carry):
        dst = pl.ds(pl.multiple_of(at + i * 8, 8), 8)
        l, r = from_left[rows8(i), :], from_right[rows8(i), :]
        for ch in range(3):
            for t in range(3):
                p = 3 * lane + t
                u = (t + 1) % 3
                a = lroll(l, EDGE_RIGHT - (86 if u == 0 else 85) - EDGE * (3 * ch + u))
                u = (t + 2) % 3
                b = lroll(r, EDGE_LEFT + (86 if u == 2 else 85) - EDGE * (3 * ch + u))
                x = jnp.where((p >= CPAD - HALO) & (p < CPAD), a, own(ch, t, i, dst))
                x = jnp.where((p >= CPAD + COLS) & (p < CPAD + COLS + HALO), b, x)
                nat[ch, t, dst, :] = x
        return carry

    lax.fori_loop(0, count, body, 0)


def dealt(fields, lane):
    out = [[] for _ in fields]
    for t in range(3):
        p = 3 * lane + t
        idx = (p - CPAD) % 128
        for x, y in zip(fields, out):
            got = [lanes_take(part, idx) for part in x]
            y.append(jnp.where((p < 64) | (p >= 320), got[2], jnp.where(p < 192, got[0], got[1])))
    return out


def undealt(fields, lane):
    out = [[] for _ in fields]
    for t in range(2):
        p = lane + (128 * t + CPAD)
        idx = p // 3
        for x, y in zip(fields, out):
            got = [lanes_take(part, idx) for part in x]
            y.append(jnp.where(p % 3 == 0, got[0], jnp.where(p % 3 == 1, got[1], got[2])))
    return out


def natural_place(k, t, lane, sub, row0, col0):
    row = row0 - PAD + sub * K + k
    if t < 2:
        return row, lane + (col0 + 128 * t)
    return row, jnp.where(lane < 64, lane + (col0 + 256), lane + (col0 - 128))


def fine_inside(k, t, lane, sub, row0, col0, n_rows, n_cols):
    row = row0 - PAD + sub * K + k
    col = 3 * lane + (t - CPAD + col0)
    return (row >= 0) & (row < n_rows) & (col >= 0) & (col < n_cols)


def level_inside(k, lane, sub, row0, col0, n_rows, n_cols):
    row = row0 - LPAD + sub * KL + k
    col = lane - LHALO + col0
    return (row >= 0) & (row < n_rows) & (col >= 0) & (col < n_cols) & (lane < 96)


def stencil_pass(v, wt, emit, unroll, end=None):
    def row(k):
        w = [[wt[n, t, rows8(k), :] for t in range(3)] for n in range(4)]
        for ch in range(3):
            here = [v[ch, t, rows8(k + 1), :] for t in range(3)]
            left = [lroll(here[2], 1), here[0], here[1]]
            right = [here[1], here[2], lroll(here[0], 127)]
            total = []
            for t in range(3):
                x = w[2][t] * v[ch, t, rows8(k), :] + w[3][t] * v[ch, t, rows8(k + 2), :]
                total.append(x + (w[0][t] * left[t] + w[1][t] * right[t]))
            emit(k, ch, here, total)

    def body(m, carry):
        for q in range(unroll):
            row(unroll * m + q)
        if end is not None:
            end(m)
        return carry

    lax.fori_loop(0, K // unroll, body, 0)


def fine_pads(v):
    for ch in range(3):
        for t in range(3):
            set_pads(v, (ch, t), K)


def fine_sweep(vin, vout, sp, wt, omega):
    def emit(k, ch, here, total):
        for t in range(3):
            new = sp[ch, t, rows8(k), :] + total[t]
            vout[ch, t, rows8(k + 1), :] = (1.0 - omega) * here[t] + omega * new

    stencil_pass(vin, wt, emit, 4)
    fine_pads(vout)


def fine_first(vout, sp):
    omega = chebyshev_weight(0)

    def body(k, carry):
        for ch in range(3):
            for t in range(3):
                vout[ch, t, rows8(k + 1), :] = omega * sp[ch, t, rows8(k), :]
        return carry

    lax.fori_loop(0, K, body, 0)
    fine_pads(vout)


def fine_smooth(va, vb, sp, wt, from_zero):
    bufs = [va, vb]
    at = 0
    for i in range(SWEEPS):
        if i == 0 and from_zero:
            fine_first(va, sp)
            continue
        fine_sweep(bufs[at], bufs[1 - at], sp, wt, chebyshev_weight(i))
        at = 1 - at
    return bufs[at], bufs[1 - at]


def pick(x, lane):
    got = [lanes_take(y, jnp.minimum((4 * lane) // 3, 127)) for y in x]
    return jnp.where(lane % 3 == 0, got[0], jnp.where(lane % 3 == 1, got[1], got[2]))


def to_level(x, lane):
    after = [lroll(y, 127) for y in x]
    mid, first = x[1] + x[2], after[0] + after[1]
    sums = [x[0] + mid + after[0], mid + first, x[2] + first + after[2]]
    return pick(sums, lane)


def fine_residual_to_level(v, sp, wt, dg, lsrc):
    lane = lane_iota()
    acc = {}

    def emit(k, ch, here, total):
        res = [dg[t, rows8(k), :] * (sp[ch, t, rows8(k), :] - here[t] + total[t]) for t in range(3)]
        acc[ch] = [a + b for a, b in zip(acc[ch], res)] if ch in acc else res

    def end(m):
        for ch in range(3):
            lsrc[ch, rows8(m), :] = to_level(acc.pop(ch), lane) * 0.0625

    stencil_pass(v, wt, emit, 4, end)


def level_weights(fx, fy, lw, ld, li, where):
    lane, sub = lane_iota(), sub_iota()
    fy[rows8(KL), :] = pltpu.roll(fy[rows8(0), :], 7, 0)

    def body(k, carry):
        left, up, down = fx[rows8(k), :], fy[rows8(k), :], fy[rows8(k + 1), :]
        right = lroll(left, 127)
        diag = SCREEN + left + right + up + down
        inv = jnp.where(level_inside(k, lane, sub, *where), 1.0 / diag, 0.0)
        ld[rows8(k), :] = diag
        li[rows8(k), :] = inv
        for n, face in enumerate((left, right, up, down)):
            lw[n, rows8(k), :] = face * inv
        return carry

    lax.fori_loop(0, KL, body, 0)


def level_neighbours(f, lw, k, ch):
    here = f[ch, rows8(k + 1), :]
    total = lw[0, rows8(k), :] * lroll(here, 1) + lw[1, rows8(k), :] * lroll(here, 127)
    return here, total + lw[2, rows8(k), :] * f[ch, rows8(k), :] + lw[3, rows8(k), :] * f[ch, rows8(k + 2), :]


def level_pads(f):
    for ch in range(3):
        set_pads(f, (ch,), KL)


def level_smooth(fa, fb, lsp, lw, from_zero):
    bufs = [fa, fb]
    at = 0
    for i in range(SWEEPS):
        omega = chebyshev_weight(i)
        src, dst = bufs[at], bufs[1 - at]
        if i == 0 and from_zero:

            def first(k, carry):
                for ch in range(3):
                    src[ch, rows8(k + 1), :] = omega * lsp[ch, rows8(k), :]
                return carry

            lax.fori_loop(0, KL, first, 0, unroll=True)
            level_pads(src)
            continue

        def body(k, carry):
            for ch in range(3):
                here, total = level_neighbours(src, lw, k, ch)
                dst[ch, rows8(k + 1), :] = (1.0 - omega) * here + omega * (lsp[ch, rows8(k), :] + total)
            return carry

        lax.fori_loop(0, KL, body, 0, unroll=True)
        level_pads(dst)
        at = 1 - at
    return bufs[at]


def level_down(lsrc, li, ld, lw, lsp, fa, fb, lnat, lev, lpr, lpl, g):
    lane = lane_iota()

    def scale(k, carry):
        for ch in range(3):
            lsp[ch, rows8(k), :] = lsrc[ch, rows8(k), :] * li[rows8(k), :]
        return carry

    lax.fori_loop(0, KL, scale, 0, unroll=True)
    f = level_smooth(fa, fb, lsp, lw, True)

    def out(k, carry):
        at = pl.ds(LHALO - LPAD + k, 8, stride=KL)
        for ch in range(3):
            here, total = level_neighbours(f, lw, k, ch)
            lnat[8 + ch, at, :] = ld[rows8(k), :] * (lsp[ch, rows8(k), :] - here + total)
            lnat[ch, at, :] = here
            lnat[3 + ch, at, :] = lsrc[ch, rows8(k), :]
        return carry

    lax.fori_loop(0, KL, out, 0, unroll=True)

    def copy(i, carry):
        src = pl.ds(pl.multiple_of(LHALO + i * 8, 8), 8)
        right = left = jnp.zeros((8, 128), F32)
        for a in range(8):
            x = lnat[a, src, :]
            lev[a, rows8(i), :] = x
            here = (lane >= 16 * a) & (lane < 16 * a + 16)
            right = jnp.where(here, lroll(x, 16 * a - 64), right)
            left = jnp.where(here, lroll(x, 16 * a - 16), left)
        lpr[rows8(i), :] = right
        lpl[rows8(i), :] = left
        return carry

    lax.fori_loop(0, LROWS // 8, copy, 0)
    idx = (LHALO + 4 * lane) % 128
    parts = []
    for i in range(CROWS // 8):
        total = jnp.zeros((8, 128), F32)
        for ch in range(3):
            x = sum(lnat[8 + ch, pl.ds(LHALO + 32 * i + q, 8, stride=4), :] for q in range(4))
            x = x + lroll(x, 127)
            x = x + lroll(x, 126)
            x = jnp.where(lane < CCOLS, lanes_take(x, idx), 0.0) * 0.0625
            total = total + lroll(x, CCOLS * ch)
        parts.append(total)
    half = len(parts) // 2
    for i in range(half):
        g[i * 8 : i * 8 + 8, :] = parts[i] + lroll(parts[half + i], 64)


def level_up(lev, lrows, lcols, lcorn, corr, lnat, lnc, fx, fy, lw, ld, li, lsp, fa, fb, where):
    lane, sub = lane_iota(), sub_iota()

    def place(dst_row, count, own, left, right):
        def body(i, carry):
            dst = pl.ds(pl.multiple_of(dst_row + i * 8, 8), 8)
            l, r = left(rows8(i)), right(rows8(i))
            for a in range(8):
                x = jnp.where((lane >= 80) & (lane < 96), lroll(r, 80 - 16 * a), 0.0)
                x = jnp.where((lane >= 16) & (lane < 80), own(a, rows8(i)), x)
                lnat[a, dst, :] = jnp.where(lane < 16, lroll(l, -16 * a), x)
            return carry

        lax.fori_loop(0, count, body, 0)

    place(0, LHALO // 8, lambda a, r: lrows[0, a, r, :], lambda r: lcorn[0, r, :], lambda r: lcorn[1, r, :])
    place(LHALO, LROWS // 8, lambda a, r: lev[a, r, :], lambda r: lcols[0, r, :], lambda r: lcols[1, r, :])
    place(LHALO + LROWS, LHALO // 8, lambda a, r: lrows[1, a, r, :], lambda r: lcorn[2, r, :], lambda r: lcorn[3, r, :])
    for ch in range(3):
        for h in range(LNAT // 32):
            x = corr[ch, 4 + 8 * h : 12 + 8 * h, :]
            for q in range(4):
                lnc[ch, pl.ds(32 * h + q, 8, stride=4), :] = x

    def faces(k, carry):
        at = pl.ds(LHALO - LPAD + k, 8, stride=KL)
        fx[rows8(k), :] = lnat[6, at, :]
        fy[rows8(k), :] = lnat[7, at, :]
        return carry

    lax.fori_loop(0, KL, faces, 0)
    level_weights(fx, fy, lw, ld, li, where)

    def fields(k, carry):
        at = pl.ds(LHALO - LPAD + k, 8, stride=KL)
        inside = level_inside(k, lane, sub, *where)
        inv = li[rows8(k), :]
        for ch in range(3):
            fa[ch, rows8(k + 1), :] = jnp.where(inside, lnat[ch, at, :] + lnc[ch, at, :], 0.0)
            lsp[ch, rows8(k), :] = lnat[3 + ch, at, :] * inv
        return carry

    lax.fori_loop(0, KL, fields, 0, unroll=True)
    level_pads(fa)
    return level_smooth(fa, fb, lsp, lw, False)


def fine_up(vrows, vcols, vcorn, field, nat, va, where):
    lane, sub = lane_iota(), sub_iota()
    unpack_field(nat, 8 + PAD, ROWS // 8, lambda ch, t, i, r: nat[ch, t, r, :], vcols.at[0], vcols.at[1])
    for slot, at in ((0, 8 + PAD - HALO), (1, 8 + PAD + ROWS)):
        own = lambda ch, t, i, r, slot=slot: vrows[slot, ch, t, rows8(i), :]
        unpack_field(nat, at, HALO // 8, own, vcorn.at[2 * slot], vcorn.at[2 * slot + 1])

    def body(kl, carry):
        for t in range(3):
            idx = jnp.minimum((3 * lane + t) // 4, 127)
            inside = [fine_inside(kl * 4 + q, t, lane, sub, *where) for q in range(4)]
            for ch in range(3):
                add = lanes_take(field[ch, rows8(kl + 1), :], idx)
                for q in range(4):
                    x = nat[ch, t, pl.ds(8 + kl * 4 + q, 8, stride=K), :] + add
                    va[ch, t, rows8(kl * 4 + q + 1), :] = jnp.where(inside[q], x, 0.0)
        return carry

    lax.fori_loop(0, KL, body, 0)
    fine_pads(va)


def field_out(field, nat, vpr, vpl):
    def body(m, carry):
        for q in range(2):
            k = 2 * m + q
            for ch in range(3):
                for t in range(3):
                    nat[ch, t, pl.ds(8 + k, 8, stride=K), :] = field[ch, t, rows8(k + 1), :]
        return carry

    lax.fori_loop(0, K // 2, body, 0)
    pack_field(nat, vpr, vpl)


def positions(n_row, n_col):
    i, j = lax.axis_index("row"), lax.axis_index("col")
    fine = (i * ROWS, j * COLS, n_row * ROWS, n_col * COLS)
    level = (i * LROWS, j * LCOLS, n_row * LROWS, n_col * LCOLS)
    return fine, level


TOP, LOW = pl.ds(0, HALO), pl.ds(ROWS - HALO, HALO)
LTOP, LLOW = pl.ds(0, LHALO), pl.ds(LROWS - LHALO, LHALO)
MID = pl.ds(8 + PAD, ROWS)
FIRST, LAST = pl.ds(8 + PAD, HALO), pl.ds(8 + PAD + ROWS - HALO, HALO)
ABOVE, BELOW = pl.ds(8 + PAD - HALO, HALO), pl.ds(8 + PAD + ROWS, HALO)


class Sender:
    def __init__(self, send_sems, recv_sems):
        self.send_sems, self.recv_sems, self.count = send_sems, recv_sems, 0

    def __call__(self, src, dst, device):
        n = self.count
        self.count += 1
        copy = pltpu.make_async_remote_copy(
            src_ref=src, dst_ref=dst, send_sem=self.send_sems.at[n], recv_sem=self.recv_sems.at[n],
            device_id=device, device_id_type=MESH,
        )
        copy.start()
        return copy


def fine_operator(nat, fxp, fyp, sp, wt, dg, lfx, lfy, lnat, where):
    lane, sub = lane_iota(), sub_iota()

    def edge(code, a, b):
        return jnp.exp2(code * 0.25 - 2.0) * jnp.where(a != b, SEAM, 1.0)

    def faces(k, carry):
        at, above = pl.ds(8 + k, 8, stride=K), pl.ds(7 + k, 8, stride=K)
        code = left_of([nat[3, t, at, :] for t in range(3)], lane)
        label = [nat[5, t, at, :] for t in range(3)]
        beside = left_of(label, lane)
        fx, fy = [], []
        for t in range(3):
            row, col = natural_place(k, t, lane, sub, where[0], where[1])
            inner = edge(code[t], beside[t], label[t])
            fx.append(jnp.where((col >= 1) & (col < where[3]), inner, 1.0))
            inner = edge(nat[4, t, above, :], nat[5, t, above, :], label[t])
            fy.append(jnp.where((row >= 1) & (row < where[2]), inner, 1.0))
        for ref, tiles in zip((fxp, fyp), dealt([fx, fy], lane)):
            for t, x in enumerate(tiles):
                ref[t, rows8(k), :] = x
        return carry

    lax.fori_loop(0, K, faces, 0, unroll=2)
    for t in range(3):
        fyp[t, rows8(K), :] = pltpu.roll(fyp[t, rows8(0), :], 7, 0)

    def weights(k, carry):
        left = [fxp[t, rows8(k), :] for t in range(3)]
        right = [left[1], left[2], lroll(left[0], 127)]
        at = pl.ds(8 + k, 8, stride=K)
        scale = []
        for t in range(3):
            up, down = fyp[t, rows8(k), :], fyp[t, rows8(k + 1), :]
            diag = SCREEN + left[t] + right[t] + up + down
            inv = jnp.where(fine_inside(k, t, lane, sub, *where), 1.0 / diag, 0.0)
            scale.append(inv)
            dg[t, rows8(k), :] = diag
            for n, face in enumerate((left[t], right[t], up, down)):
                wt[n, t, rows8(k), :] = face * inv
        natural = [[nat[ch, t, at, :] for t in range(3)] for ch in range(3)]
        for ch, tiles in enumerate(dealt(natural, lane)):
            for t, x in enumerate(tiles):
                sp[ch, t, rows8(k), :] = x * scale[t]
        return carry

    lax.fori_loop(0, K, weights, 0, unroll=2)

    def level_faces(kl, carry):
        rows = [sum(fxp[t, rows8(kl * 4 + q), :] for q in range(4)) for t in range(3)]
        x = pick(rows, lane) * 0.0625
        y = to_level([fyp[t, rows8(kl * 4), :] for t in range(3)], lane) * 0.0625
        at = pl.ds(LHALO - LPAD + kl, 8, stride=KL)
        lfx[rows8(kl), :] = x
        lfy[rows8(kl), :] = y
        lnat[6, at, :] = x
        lnat[7, at, :] = y
        return carry

    lax.fori_loop(0, KL, level_faces, 0)


def coarse_solve(
    n_row, n_col, place, send, g, s_cols, s_ext, t_back, row_eig, col_eig, nat, vpr, vpl, lev, lpr, lpl,
    vrows, vcols, vcorn, lrows, lcols, lcorn, one, two, three, mine, full, spec, back, corr,
):
    i, j, up, down, left, right = place
    n_modes = n_row * CROWS
    lane = lane_iota()

    first = [send(g, one.at[j], (i, lax.rem(j + d, n_col))) for d in range(1, n_col)]
    one[j] = g[...]
    halos = [
        send(lpr, lcols.at[0], (i, right)),
        send(lpl, lcols.at[1], (i, left)),
        send(lev.at[:, LTOP, :], lrows.at[1], (up, j)),
        send(lev.at[:, LLOW, :], lrows.at[0], (down, j)),
        send(lpr.at[LLOW, :], lcorn.at[0], (down, right)),
        send(lpl.at[LLOW, :], lcorn.at[1], (down, left)),
        send(lpr.at[LTOP, :], lcorn.at[2], (up, right)),
        send(lpl.at[LTOP, :], lcorn.at[3], (up, left)),
    ]
    for copy in first:
        copy.wait()

    def placed(ref, n_rows):
        out = []
        for ch in range(3):
            parts = []
            for r in range(n_rows // 8):
                x = jnp.zeros((8, 128), F32)
                for p in range(n_col):
                    here = (lane >= CCOLS * p) & (lane < CCOLS * p + CCOLS)
                    low_half = r * 16 >= n_rows
                    row = r * 8 - n_rows // 2 if low_half else r * 8
                    y = lroll(ref[p, row : row + 8, :], CCOLS * (p - ch) - (64 if low_half else 0))
                    x = jnp.where(here, y, x)
                parts.append(x)
            out.append(jnp.concatenate(parts, axis=0))
        return out

    x = jnp.concatenate(placed(one, CROWS), axis=0)
    x = jnp.dot(x, s_cols[j], precision=HIGHEST, preferred_element_type=F32)
    total = lax.slice_in_dim(x, 0, CROWS)
    for ch in (1, 2):
        total = total + pltpu.roll(lax.slice_in_dim(x, CROWS * ch, CROWS * ch + CROWS), CCOLS * ch, 1)
    half = CROWS // 2
    total = lax.slice_in_dim(total, 0, half) + pltpu.roll(lax.slice_in_dim(total, half, CROWS), 64, 1)
    mine[...] = total
    second = [send(mine, two.at[i], (lax.rem(i + d, n_row), j)) for d in range(1, n_row)]
    two[i] = total
    halos += [
        send(vpr, vcols.at[0], (i, right)),
        send(vpl, vcols.at[1], (i, left)),
        send(vpr.at[LOW, :], vcorn.at[0], (down, right)),
        send(vpl.at[LOW, :], vcorn.at[1], (down, left)),
        send(vpr.at[TOP, :], vcorn.at[2], (up, right)),
        send(vpl.at[TOP, :], vcorn.at[3], (up, left)),
    ]
    for copy in second:
        copy.wait()
    halos += [
        send(nat.at[pl.ds(0, 3), :, FIRST, :], vrows.at[1], (up, j)),
        send(nat.at[pl.ds(0, 3), :, LAST, :], vrows.at[0], (down, j)),
    ]
    for p in range(n_row):
        for r in range(0, half, 8):
            x = two[p, r : r + 8, :]
            full[p * CROWS + r : p * CROWS + r + 8, :] = x
            full[p * CROWS + half + r : p * CROWS + half + r + 8, :] = lroll(x, 64)
    y = jnp.dot(s_ext[8 : 8 + n_modes, :], full[...], precision=HIGHEST, preferred_element_type=F32)
    eig = SCREEN + COARSE_SCALE * (row_eig[...] + col_eig[pl.ds(j, 1), :])
    spec[...] = y / eig
    rows = s_ext[pl.ds(pl.multiple_of(i * CROWS, CROWS), BROWS), :]
    z = jnp.dot(rows, spec[...], precision=HIGHEST, preferred_element_type=F32)
    half = BROWS // 2
    z = jnp.where(
        lax.broadcasted_iota(jnp.int32, (half, 128), 1) < 64,
        lax.slice_in_dim(z, 0, half), pltpu.roll(lax.slice_in_dim(z, half, BROWS), 64, 1),
    )
    back[...] = z
    third = [send(back, three.at[j], (i, lax.rem(j + d, n_col))) for d in range(1, n_col)]
    three[j] = z
    for copy in third:
        copy.wait()
    z = jnp.concatenate(placed(three, BROWS), axis=0)
    z = jnp.dot(z, t_back[j], precision=HIGHEST, preferred_element_type=F32)
    for ch in range(3):
        corr[ch] = lax.slice_in_dim(z, BROWS * ch, BROWS * ch + BROWS)
    for copy in halos:
        copy.wait()


def kernel(n_row, n_col, src, codes, labels, *refs):
    s_cols, s_ext, t_back, row_eig, col_eig, solution_out, residual_out = refs[:7]
    (
        codes_v, labels_v, right_pack, left_pack, srows, crows, labrows, cols, corners,
        nat, fxp, fyp, sp, wt, dg, va, vb, vpr, vpl,
        lsrc, lfx, lfy, lw, ld, li, lsp, fa, fb, lnat, lnc, lev, lpr, lpl, g,
        one, two, three, mine, full, spec, back, corr,
        vrows, vcols, vcorn, lrows, lcols, lcorn,
        copy_sems, send_sems, recv_sems,
    ) = refs[7:]
    i, j = lax.axis_index("row"), lax.axis_index("col")
    up, down = lax.rem(i + n_row - 1, n_row), lax.rem(i + 1, n_row)
    left, right = lax.rem(j + n_col - 1, n_col), lax.rem(j + 1, n_col)
    where, lwhere = positions(n_row, n_col)
    lane = lane_iota()

    barrier = pltpu.get_barrier_semaphore()
    peers = [(i, lax.rem(j + d, n_col)) for d in range(1, n_col)]
    peers += [(lax.rem(i + d, n_row), j) for d in range(1, n_row)]
    peers += [(r, c) for r in (up, down) for c in (left, right)]
    for peer in peers:
        pl.semaphore_signal(barrier, inc=1, device_id=peer, device_id_type=MESH)

    loads = [pltpu.make_async_copy(codes, codes_v, copy_sems.at[0])]
    loads.append(pltpu.make_async_copy(labels, labels_v, copy_sems.at[1]))
    for a in range(3):
        for t in range(2):
            part = src.at[a, :, pl.ds(128 * t, 128)]
            loads.append(pltpu.make_async_copy(part, nat.at[a, t, MID, :], copy_sems.at[len(loads)]))
    for copy in loads:
        copy.start()
    zero_ends(nat, 6)
    pl.semaphore_wait(barrier, n_col + n_row + 2)
    send = Sender(send_sems, recv_sems)
    copies = []
    for slot, rows, device in ((1, TOP, up), (0, LOW, down)):
        copies.append(send(src.at[:, rows, :], srows.at[slot], (device, j)))
        copies.append(send(codes.at[:, rows, :], crows.at[slot], (device, j)))
        copies.append(send(labels.at[rows, :], labrows.at[slot], (device, j)))
    for copy in loads:
        copy.wait()

    def convert(n, carry):
        r = rows8(n)
        at = pl.ds(pl.multiple_of(8 + PAD + 8 * n, 8), 8)
        for t in range(2):
            c = slice(128 * t, 128 * t + 128)
            nat[3, t, at, :] = codes_v[0, r, c].astype(F32)
            nat[4, t, at, :] = codes_v[1, r, c].astype(F32)
            nat[5, t, at, :] = labels_v[r, c].astype(F32)
        return carry

    lax.fori_loop(0, ROWS // 8, convert, 0, unroll=2)

    def natural(a, t, r):
        return nat[a, t, pl.ds(pl.multiple_of(8 + PAD + r.start, 8), 8), :]

    pack_fine(natural, 6, right_pack, left_pack, lane, ROWS)
    copies.append(send(right_pack, cols.at[0], (i, right)))
    copies.append(send(left_pack, cols.at[1], (i, left)))
    copies.append(send(right_pack.at[:, LOW, :], corners.at[0], (down, right)))
    copies.append(send(left_pack.at[:, LOW, :], corners.at[1], (down, left)))
    copies.append(send(right_pack.at[:, TOP, :], corners.at[2], (up, right)))
    copies.append(send(left_pack.at[:, TOP, :], corners.at[3], (up, left)))
    for copy in copies:
        copy.wait()

    for t in range(2):
        c = slice(128 * t, 128 * t + 128)
        for slot, rows in ((0, ABOVE), (1, BELOW)):
            for a in range(3):
                nat[a, t, rows, :] = srows[slot, a, :, c]
            for a in range(2):
                nat[3 + a, t, rows, :] = crows[slot, a, :, c].astype(F32)
            nat[5, t, rows, :] = labrows[slot, :, c].astype(F32)
    unpack_columns(nat, 6, cols, corners, lane)
    fine_operator(nat, fxp, fyp, sp, wt, dg, lfx, lfy, lnat, where)
    level_weights(lfx, lfy, lw, ld, li, lwhere)

    field, other = fine_smooth(va, vb, sp, wt, True)
    for cycle in range(2):
        fine_residual_to_level(field, sp, wt, dg, lsrc)
        level_down(lsrc, li, ld, lw, lsp, fa, fb, lnat, lev, lpr, lpl, g)
        field_out(field, nat, vpr, vpl)
        got = [ref.at[cycle] for ref in (vrows, vcols, vcorn, lrows, lcols, lcorn, one, two, three)]
        coarse_solve(
            n_row, n_col, (i, j, up, down, left, right), send, g, s_cols, s_ext, t_back, row_eig, col_eig,
            nat, vpr, vpl, lev, lpr, lpl, *got, mine, full, spec, back, corr,
        )
        level = level_up(
            lev, got[3], got[4], got[5], corr, lnat, lnc, lfx, lfy, lw, ld, li, lsp, fa, fb, lwhere
        )
        fine_up(got[0], got[1], got[2], level, nat, va, where)
        field, other = fine_smooth(va, vb, sp, wt, False)
        if cycle == 0:
            field, other = fine_smooth(field, other, sp, wt, False)

    fields = []

    def emit(k, ch, here, total):
        fields.append(here)
        fields.append(
            [dg[t, rows8(k), :] * (sp[ch, t, rows8(k), :] - here[t] + total[t]) for t in range(3)]
        )

    def finish(k):
        at = pl.ds(8 + k, 8, stride=K)
        for n, tiles in enumerate(undealt(fields, lane)):
            for t, x in enumerate(tiles):
                nat[n // 2 + 3 * (n % 2), t, at, :] = x
        fields.clear()

    stencil_pass(field, wt, emit, 1, finish)
    stores = []
    for a in range(6):
        for t in range(2):
            out = (solution_out if a < 3 else residual_out).at[a % 3, :, pl.ds(128 * t, 128)]
            stores.append(pltpu.make_async_copy(nat.at[a, t, MID, :], out, copy_sems.at[len(stores)]))
    for copy in stores:
        copy.start()
    for copy in stores:
        copy.wait()


@functools.lru_cache(maxsize=None)
def tables(n_row, n_col):
    def sines(n):
        k = np.arange(1, n + 1)
        return math.sqrt(2.0 / (n + 1)) * np.sin(np.pi * ((k[:, None] * k[None, :]) % (2 * (n + 1))) / (n + 1))

    def eig(n):
        return 2.0 - 2.0 * np.cos(np.pi * np.arange(1, n + 1) / (n + 1))

    nr, nc = n_row * CROWS, n_col * CCOLS
    rows, cols = sines(nr), sines(nc)
    s_cols = np.zeros((n_col, 128, 128))
    t_back = np.zeros((n_col, 128, 128))
    col_eig = np.ones((n_col, 128))
    lane = np.arange(128)
    for j in range(n_col):
        own = slice(CCOLS * j, CCOLS * j + CCOLS)
        s_cols[j, :nc, :CCOLS] = cols[:, own]
        col_eig[j, : 3 * CCOLS] = np.tile(eig(nc)[own], 3)
        c = LCOLS * j + lane - LHALO
        ok = (c >= 0) & (c < n_col * LCOLS) & (lane < 96)
        t_back[j, :nc, ok] = cols[:, c[ok] // 4].T
    s_ext = np.zeros((nr + 16, nr))
    s_ext[8 : 8 + nr] = rows
    row_eig = np.repeat(eig(nr)[:, None], 128, axis=1)
    return tuple(x.astype(np.float32) for x in (s_cols, s_ext, t_back, row_eig, col_eig))


def shape(*dims, dtype=F32):
    return jax.ShapeDtypeStruct(dims, dtype)


IN_VMEM = pl.BlockSpec(memory_space=pltpu.VMEM)
IN_ANY = pl.BlockSpec(memory_space=pl.ANY)


def solution(mesh):
    n_row, n_col = mesh.shape["row"], mesh.shape["col"]

    def vmem(*dims, dtype=F32):
        return pltpu.VMEM(dims, dtype)

    n_copies = 12 + 2 * (2 * (n_col - 1) + (n_row - 1) + 16)
    scratch = [
        vmem(2, ROWS, COLS, dtype=jnp.int32), vmem(ROWS, COLS, dtype=jnp.int32),
        vmem(2, ROWS, 128), vmem(2, ROWS, 128),
        vmem(2, 3, HALO, COLS), vmem(2, 2, HALO, COLS, dtype=jnp.int32), vmem(2, HALO, COLS, dtype=jnp.int32),
        vmem(2, 2, ROWS, 128), vmem(4, 2, HALO, 128),
        vmem(6, 3, NAT, 128), vmem(3, K * 8, 128), vmem(3, (K + 1) * 8, 128),
        vmem(3, 3, K * 8, 128), vmem(4, 3, K * 8, 128), vmem(3, K * 8, 128),
        vmem(3, 3, (K + 2) * 8, 128), vmem(3, 3, (K + 2) * 8, 128),
        vmem(ROWS, 128), vmem(ROWS, 128),
        vmem(3, KL * 8, 128), vmem(KL * 8, 128), vmem((KL + 1) * 8, 128),
        vmem(4, KL * 8, 128), vmem(KL * 8, 128), vmem(KL * 8, 128), vmem(3, KL * 8, 128),
        vmem(3, (KL + 2) * 8, 128), vmem(3, (KL + 2) * 8, 128),
        vmem(11, LNAT, 128), vmem(3, LNAT, 128), vmem(8, LROWS, 128),
        vmem(LROWS, 128), vmem(LROWS, 128), vmem(CROWS // 2, 128),
        vmem(2, n_col, CROWS // 2, 128), vmem(2, n_row, CROWS // 2, 128), vmem(2, n_col, BROWS // 2, 128),
        vmem(CROWS // 2, 128), vmem(n_row * CROWS, 128), vmem(n_row * CROWS, 128),
        vmem(BROWS // 2, 128), vmem(3, BROWS, 128),
        vmem(2, 2, 3, 3, HALO, 128), vmem(2, 2, ROWS, 128), vmem(2, 4, HALO, 128),
        vmem(2, 2, 8, LHALO, 128), vmem(2, 2, LROWS, 128), vmem(2, 4, LHALO, 128),
        pltpu.SemaphoreType.DMA((12,)),
        pltpu.SemaphoreType.DMA((n_copies,)), pltpu.SemaphoreType.DMA((n_copies,)),
    ]
    call = pl.pallas_call(
        functools.partial(kernel, n_row, n_col),
        out_shape=[shape(3, ROWS, COLS)] * 2,
        in_specs=[IN_ANY] * 3 + [IN_VMEM] * 5,
        out_specs=[IN_ANY] * 2,
        scratch_shapes=scratch,
        compiler_params=pltpu.CompilerParams(collective_id=0, has_side_effects=True, vmem_limit_bytes=VMEM_LIMIT),
    )
    consts = tables(n_row, n_col)

    def local(sources, edge_codes, seam_labels):
        return tuple(call(sources, edge_codes, seam_labels, *consts))

    spec = P(None, "row", "col")
    return jax.shard_map(
        local, mesh=mesh, in_specs=(spec, spec, P("row", "col")), out_specs=(spec, spec), check_vma=False
    )
```

```python
import functools
import math

import jax
import jax.numpy as jnp
import numpy as np
from jax import lax
from jax.experimental import pallas as pl
from jax.experimental.pallas import tpu as pltpu
from jax.sharding import PartitionSpec as P

SWEEPS = 4
SCREEN = 2e-05
SEAM = 0.2
COARSE_SCALE = 0.0625
F32 = jnp.float32
MESH = pl.DeviceIdType.MESH
HIGHEST = lax.Precision.HIGHEST

ROWS, COLS = 512, 256
PAD = 48
HALO = 32
K = (ROWS + 2 * PAD) // 8
NAT = 8 + ROWS + 2 * PAD + 8
LROWS, LCOLS = 128, 64
LPAD = PAD // 4
LHALO = 16
KL = (LROWS + 2 * LPAD) // 8
LNAT = LROWS + 2 * LHALO
CROWS, CCOLS = 32, 16
BROWS = CROWS + 16
VMEM_LIMIT = 62 * 1024 * 1024


def chebyshev_weight(sweep_index):
    return 1.0 / (1.25 + 0.75 * math.cos(math.pi * (2 * sweep_index + 1) / (2 * SWEEPS)))


def lane_iota():
    return lax.broadcasted_iota(jnp.int32, (8, 128), 1)


def sub_iota():
    return lax.broadcasted_iota(jnp.int32, (8, 128), 0)


def lroll(x, shift):
    shift = shift % 128
    return x if shift == 0 else pltpu.roll(x, shift, 1)


def rows8(k):
    return pl.ds(pl.multiple_of(k * 8, 8), 8)


def lanes_take(x, idx):
    return jnp.take_along_axis(x, idx, axis=1)


def left_of(tiles, lane):
    rolled = [lroll(x, 1) for x in tiles]
    return [jnp.where(lane == 0, rolled[(t + 2) % 3], rolled[t]) for t in range(3)]


def set_pads(ref, lead, count):
    last = ref[lead + (rows8(count), slice(None))]
    first = ref[lead + (rows8(1), slice(None))]
    ref[lead + (rows8(0), slice(None))] = pltpu.roll(last, 1, 0)
    ref[lead + (rows8(count + 1), slice(None))] = pltpu.roll(first, 7, 0)


def pack_fine(tile_of, n_arrays, right, left, lane, rows):
    def body(i, carry):
        r = rows8(i)
        for first in range(0, n_arrays, 4):
            out_r = out_l = jnp.zeros((8, 128), F32)
            for a in range(first, min(first + 4, n_arrays)):
                g = a - first
                here = (lane >= 32 * g) & (lane < 32 * g + 32)
                out_r = jnp.where(here, lroll(tile_of(a, 1, r), 32 * g - 96), out_r)
                out_l = jnp.where(here, lroll(tile_of(a, 0, r), 32 * g), out_l)
            right[first // 4, r, :] = out_r
            left[first // 4, r, :] = out_l
        return carry

    lax.fori_loop(0, rows // 8, body, 0)


def unpack_fine(nat, n_arrays, at, count, from_left, from_right, lane):
    def body(i, carry):
        src = rows8(i)
        dst = pl.ds(pl.multiple_of(at + i * 8, 8), 8)
        for a in range(n_arrays):
            g = a % 4
            l = lroll(from_left[a // 4, src, :], 96 - 32 * g)
            r = lroll(from_right[a // 4, src, :], -32 * g)
            nat[a, 2, dst, :] = jnp.where(lane < 32, r, jnp.where(lane >= 96, l, 0.0))
        return carry

    lax.fori_loop(0, count, body, 0)


def zero_ends(nat, n_arrays):
    zero = jnp.zeros((8, 128), F32)
    for a in range(n_arrays):
        for t in range(3):
            for r in (0, 8, 16, NAT - 24, NAT - 16, NAT - 8):
                nat[a, t, r : r + 8, :] = zero


def unpack_columns(nat, n_arrays, cols, corners, lane):
    unpack_fine(nat, n_arrays, 8 + PAD, ROWS // 8, cols.at[0], cols.at[1], lane)
    unpack_fine(nat, n_arrays, 8 + PAD - HALO, HALO // 8, corners.at[0], corners.at[1], lane)
    unpack_fine(nat, n_arrays, 8 + PAD + ROWS, HALO // 8, corners.at[2], corners.at[3], lane)


CPAD = 64
EDGE, EDGE_RIGHT, EDGE_LEFT = 11, 96, 21


def pack_field(nat, right, left):
    lane = lane_iota()

    def body(i, carry):
        r = pl.ds(pl.multiple_of(8 + PAD + i * 8, 8), 8)
        out_r = out_l = jnp.zeros((8, 128), F32)
        for q in range(9):
            x = nat[q // 3, q % 3, r, :]
            here = (lane >= EDGE * q) & (lane < EDGE * q + EDGE)
            out_r = jnp.where(here, lroll(x, EDGE * q - EDGE_RIGHT), out_r)
            out_l = jnp.where(here, lroll(x, EDGE * q - EDGE_LEFT), out_l)
        right[rows8(i), :] = out_r
        left[rows8(i), :] = out_l
        return carry

    lax.fori_loop(0, ROWS // 8, body, 0, unroll=2)


def unpack_field(nat, at, count, own, from_left, from_right):
    lane = lane_iota()

    def body(i, carry):
        dst = pl.ds(pl.multiple_of(at + i * 8, 8), 8)
        l, r = from_left[rows8(i), :], from_right[rows8(i), :]
        for ch in range(3):
            for t in range(3):
                p = 3 * lane + t
                u = (t + 1) % 3
                a = lroll(l, EDGE_RIGHT - (86 if u == 0 else 85) - EDGE * (3 * ch + u))
                u = (t + 2) % 3
                b = lroll(r, EDGE_LEFT + (86 if u == 2 else 85) - EDGE * (3 * ch + u))
                x = jnp.where((p >= CPAD - HALO) & (p < CPAD), a, own(ch, t, i, dst))
                x = jnp.where((p >= CPAD + COLS) & (p < CPAD + COLS + HALO), b, x)
                nat[ch, t, dst, :] = x
        return carry

    lax.fori_loop(0, count, body, 0, unroll=2)


def dealt(fields, lane):
    out = [[] for _ in fields]
    for t in range(3):
        p = 3 * lane + t
        idx = (p - CPAD) % 128
        for x, y in zip(fields, out):
            got = [lanes_take(part, idx) for part in x]
            y.append(jnp.where((p < 64) | (p >= 320), got[2], jnp.where(p < 192, got[0], got[1])))
    return out


def undealt(fields, lane):
    out = [[] for _ in fields]
    for t in range(2):
        p = lane + (128 * t + CPAD)
        idx = p // 3
        for x, y in zip(fields, out):
            got = [lanes_take(part, idx) for part in x]
            y.append(jnp.where(p % 3 == 0, got[0], jnp.where(p % 3 == 1, got[1], got[2])))
    return out


def natural_place(k, t, lane, sub, row0, col0):
    row = row0 - PAD + sub * K + k
    if t < 2:
        return row, lane + (col0 + 128 * t)
    return row, jnp.where(lane < 64, lane + (col0 + 256), lane + (col0 - 128))


def fine_inside(k, t, lane, sub, row0, col0, n_rows, n_cols):
    row = row0 - PAD + sub * K + k
    col = 3 * lane + (t - CPAD + col0)
    return (row >= 0) & (row < n_rows) & (col >= 0) & (col < n_cols)


def level_inside(k, lane, sub, row0, col0, n_rows, n_cols):
    row = row0 - LPAD + sub * KL + k
    col = lane - LHALO + col0
    return (row >= 0) & (row < n_rows) & (col >= 0) & (col < n_cols) & (lane < 96)


def stencil_pass(v, wt, emit, unroll, end=None):
    def row(k):
        w = [[wt[n, t, rows8(k), :] for t in range(3)] for n in range(4)]
        for ch in range(3):
            here = [v[ch, t, rows8(k + 1), :] for t in range(3)]
            left = [lroll(here[2], 1), here[0], here[1]]
            right = [here[1], here[2], lroll(here[0], 127)]
            total = []
            for t in range(3):
                x = w[2][t] * v[ch, t, rows8(k), :] + w[3][t] * v[ch, t, rows8(k + 2), :]
                total.append(x + (w[0][t] * left[t] + w[1][t] * right[t]))
            emit(k, ch, here, total)

    def body(m, carry):
        for q in range(unroll):
            row(unroll * m + q)
        if end is not None:
            end(m)
        return carry

    lax.fori_loop(0, K // unroll, body, 0)


def fine_pads(v):
    for ch in range(3):
        for t in range(3):
            set_pads(v, (ch, t), K)


def fine_sweep(vin, vout, sp, wt, omega):
    def emit(k, ch, here, total):
        for t in range(3):
            new = sp[ch, t, rows8(k), :] + total[t]
            vout[ch, t, rows8(k + 1), :] = (1.0 - omega) * here[t] + omega * new

    stencil_pass(vin, wt, emit, 4)
    fine_pads(vout)


def fine_first(vout, sp):
    omega = chebyshev_weight(0)

    def body(k, carry):
        for ch in range(3):
            for t in range(3):
                vout[ch, t, rows8(k + 1), :] = omega * sp[ch, t, rows8(k), :]
        return carry

    lax.fori_loop(0, K, body, 0)
    fine_pads(vout)


def fine_smooth(va, vb, sp, wt, from_zero):
    bufs = [va, vb]
    at = 0
    for i in range(SWEEPS):
        if i == 0 and from_zero:
            fine_first(va, sp)
            continue
        fine_sweep(bufs[at], bufs[1 - at], sp, wt, chebyshev_weight(i))
        at = 1 - at
    return bufs[at], bufs[1 - at]


def pick(x, lane):
    got = [lanes_take(y, jnp.minimum((4 * lane) // 3, 127)) for y in x]
    return jnp.where(lane % 3 == 0, got[0], jnp.where(lane % 3 == 1, got[1], got[2]))


def to_level(x, lane):
    after = [lroll(y, 127) for y in x]
    mid, first = x[1] + x[2], after[0] + after[1]
    sums = [x[0] + mid + after[0], mid + first, x[2] + first + after[2]]
    return pick(sums, lane)


def fine_residual_to_level(v, sp, wt, dg, lsrc):
    lane = lane_iota()
    acc = {}

    def emit(k, ch, here, total):
        res = [dg[t, rows8(k), :] * (sp[ch, t, rows8(k), :] - here[t] + total[t]) for t in range(3)]
        acc[ch] = [a + b for a, b in zip(acc[ch], res)] if ch in acc else res

    def end(m):
        for ch in range(3):
            lsrc[ch, rows8(m), :] = to_level(acc.pop(ch), lane) * 0.0625

    stencil_pass(v, wt, emit, 4, end)


def level_weights(fx, fy, lw, ld, li, where):
    lane, sub = lane_iota(), sub_iota()
    fy[rows8(KL), :] = pltpu.roll(fy[rows8(0), :], 7, 0)

    def body(k, carry):
        left, up, down = fx[rows8(k), :], fy[rows8(k), :], fy[rows8(k + 1), :]
        right = lroll(left, 127)
        diag = SCREEN + left + right + up + down
        inv = jnp.where(level_inside(k, lane, sub, *where), 1.0 / diag, 0.0)
        ld[rows8(k), :] = diag
        li[rows8(k), :] = inv
        for n, face in enumerate((left, right, up, down)):
            lw[n, rows8(k), :] = face * inv
        return carry

    lax.fori_loop(0, KL, body, 0)


def level_neighbours(f, lw, k, ch):
    here = f[ch, rows8(k + 1), :]
    total = lw[0, rows8(k), :] * lroll(here, 1) + lw[1, rows8(k), :] * lroll(here, 127)
    return here, total + lw[2, rows8(k), :] * f[ch, rows8(k), :] + lw[3, rows8(k), :] * f[ch, rows8(k + 2), :]


def level_pads(f):
    for ch in range(3):
        set_pads(f, (ch,), KL)


def level_smooth(fa, fb, lsp, lw, from_zero):
    bufs = [fa, fb]
    at = 0
    for i in range(SWEEPS):
        omega = chebyshev_weight(i)
        src, dst = bufs[at], bufs[1 - at]
        if i == 0 and from_zero:

            def first(k, carry):
                for ch in range(3):
                    src[ch, rows8(k + 1), :] = omega * lsp[ch, rows8(k), :]
                return carry

            lax.fori_loop(0, KL, first, 0, unroll=True)
            level_pads(src)
            continue

        def body(k, carry):
            for ch in range(3):
                here, total = level_neighbours(src, lw, k, ch)
                dst[ch, rows8(k + 1), :] = (1.0 - omega) * here + omega * (lsp[ch, rows8(k), :] + total)
            return carry

        lax.fori_loop(0, KL, body, 0, unroll=True)
        level_pads(dst)
        at = 1 - at
    return bufs[at]


def level_down(lsrc, li, ld, lw, lsp, fa, fb, lnat, lev, lpr, lpl, g):
    lane = lane_iota()

    def scale(k, carry):
        for ch in range(3):
            lsp[ch, rows8(k), :] = lsrc[ch, rows8(k), :] * li[rows8(k), :]
        return carry

    lax.fori_loop(0, KL, scale, 0, unroll=True)
    f = level_smooth(fa, fb, lsp, lw, True)

    def out(k, carry):
        at = pl.ds(LHALO - LPAD + k, 8, stride=KL)
        for ch in range(3):
            here, total = level_neighbours(f, lw, k, ch)
            lnat[8 + ch, at, :] = ld[rows8(k), :] * (lsp[ch, rows8(k), :] - here + total)
            lnat[ch, at, :] = here
            lnat[3 + ch, at, :] = lsrc[ch, rows8(k), :]
        return carry

    lax.fori_loop(0, KL, out, 0, unroll=True)

    def copy(i, carry):
        src = pl.ds(pl.multiple_of(LHALO + i * 8, 8), 8)
        right = left = jnp.zeros((8, 128), F32)
        for a in range(8):
            x = lnat[a, src, :]
            lev[a, rows8(i), :] = x
            here = (lane >= 16 * a) & (lane < 16 * a + 16)
            right = jnp.where(here, lroll(x, 16 * a - 64), right)
            left = jnp.where(here, lroll(x, 16 * a - 16), left)
        lpr[rows8(i), :] = right
        lpl[rows8(i), :] = left
        return carry

    lax.fori_loop(0, LROWS // 8, copy, 0)
    idx = (LHALO + 4 * lane) % 128
    parts = []
    for i in range(CROWS // 8):
        total = jnp.zeros((8, 128), F32)
        for ch in range(3):
            x = sum(lnat[8 + ch, pl.ds(LHALO + 32 * i + q, 8, stride=4), :] for q in range(4))
            x = x + lroll(x, 127)
            x = x + lroll(x, 126)
            x = jnp.where(lane < CCOLS, lanes_take(x, idx), 0.0) * 0.0625
            total = total + lroll(x, CCOLS * ch)
        parts.append(total)
    half = len(parts) // 2
    for i in range(half):
        g[i * 8 : i * 8 + 8, :] = parts[i] + lroll(parts[half + i], 64)


def level_halos(lev, lrows, lcols, lcorn, lnat, fx, fy, lw, ld, li, where):
    lane = lane_iota()

    def place(dst_row, count, own, left, right):
        def body(i, carry):
            dst = pl.ds(pl.multiple_of(dst_row + i * 8, 8), 8)
            l, r = left(rows8(i)), right(rows8(i))
            for a in range(8):
                x = jnp.where((lane >= 80) & (lane < 96), lroll(r, 80 - 16 * a), 0.0)
                x = jnp.where((lane >= 16) & (lane < 80), own(a, rows8(i)), x)
                lnat[a, dst, :] = jnp.where(lane < 16, lroll(l, -16 * a), x)
            return carry

        lax.fori_loop(0, count, body, 0)

    place(0, LHALO // 8, lambda a, r: lrows[0, a, r, :], lambda r: lcorn[0, r, :], lambda r: lcorn[1, r, :])
    place(LHALO, LROWS // 8, lambda a, r: lev[a, r, :], lambda r: lcols[0, r, :], lambda r: lcols[1, r, :])
    place(LHALO + LROWS, LHALO // 8, lambda a, r: lrows[1, a, r, :], lambda r: lcorn[2, r, :], lambda r: lcorn[3, r, :])
    def faces(k, carry):
        at = pl.ds(LHALO - LPAD + k, 8, stride=KL)
        fx[rows8(k), :] = lnat[6, at, :]
        fy[rows8(k), :] = lnat[7, at, :]
        return carry

    lax.fori_loop(0, KL, faces, 0)
    level_weights(fx, fy, lw, ld, li, where)


def level_up(corr, lnat, lnc, lw, li, lsp, fa, fb, where):
    lane, sub = lane_iota(), sub_iota()
    for ch in range(3):
        for h in range(LNAT // 32):
            x = corr[ch, 4 + 8 * h : 12 + 8 * h, :]
            for q in range(4):
                lnc[ch, pl.ds(32 * h + q, 8, stride=4), :] = x

    def fields(k, carry):
        at = pl.ds(LHALO - LPAD + k, 8, stride=KL)
        inside = level_inside(k, lane, sub, *where)
        inv = li[rows8(k), :]
        for ch in range(3):
            fa[ch, rows8(k + 1), :] = jnp.where(inside, lnat[ch, at, :] + lnc[ch, at, :], 0.0)
            lsp[ch, rows8(k), :] = lnat[3 + ch, at, :] * inv
        return carry

    lax.fori_loop(0, KL, fields, 0, unroll=True)
    level_pads(fa)
    return level_smooth(fa, fb, lsp, lw, False)


def fine_halos(vrows, vcols, vcorn, nat):
    unpack_field(nat, 8 + PAD, ROWS // 8, lambda ch, t, i, r: nat[ch, t, r, :], vcols.at[0], vcols.at[1])
    for slot, at in ((0, 8 + PAD - HALO), (1, 8 + PAD + ROWS)):
        own = lambda ch, t, i, r, slot=slot: vrows[slot, ch, t, rows8(i), :]
        unpack_field(nat, at, HALO // 8, own, vcorn.at[2 * slot], vcorn.at[2 * slot + 1])


def fine_up(field, nat, va, where):
    lane, sub = lane_iota(), sub_iota()

    def body(kl, carry):
        for t in range(3):
            idx = jnp.minimum((3 * lane + t) // 4, 127)
            inside = [fine_inside(kl * 4 + q, t, lane, sub, *where) for q in range(4)]
            for ch in range(3):
                add = lanes_take(field[ch, rows8(kl + 1), :], idx)
                for q in range(4):
                    x = nat[ch, t, pl.ds(8 + kl * 4 + q, 8, stride=K), :] + add
                    va[ch, t, rows8(kl * 4 + q + 1), :] = jnp.where(inside[q], x, 0.0)
        return carry

    lax.fori_loop(0, KL, body, 0)
    fine_pads(va)


def field_out(field, nat, vpr, vpl):
    def body(m, carry):
        for q in range(2):
            k = 2 * m + q
            for ch in range(3):
                for t in range(3):
                    nat[ch, t, pl.ds(8 + k, 8, stride=K), :] = field[ch, t, rows8(k + 1), :]
        return carry

    lax.fori_loop(0, K // 2, body, 0)
    pack_field(nat, vpr, vpl)


def positions(n_row, n_col):
    i, j = lax.axis_index("row"), lax.axis_index("col")
    fine = (i * ROWS, j * COLS, n_row * ROWS, n_col * COLS)
    level = (i * LROWS, j * LCOLS, n_row * LROWS, n_col * LCOLS)
    return fine, level


TOP, LOW = pl.ds(0, HALO), pl.ds(ROWS - HALO, HALO)
LTOP, LLOW = pl.ds(0, LHALO), pl.ds(LROWS - LHALO, LHALO)
MID = pl.ds(8 + PAD, ROWS)
FIRST, LAST = pl.ds(8 + PAD, HALO), pl.ds(8 + PAD + ROWS - HALO, HALO)
ABOVE, BELOW = pl.ds(8 + PAD - HALO, HALO), pl.ds(8 + PAD + ROWS, HALO)


class Sender:
    def __init__(self, send_sems, recv_sems):
        self.send_sems, self.recv_sems, self.count = send_sems, recv_sems, 0

    def __call__(self, src, dst, device):
        n = self.count
        self.count += 1
        copy = pltpu.make_async_remote_copy(
            src_ref=src, dst_ref=dst, send_sem=self.send_sems.at[n], recv_sem=self.recv_sems.at[n],
            device_id=device, device_id_type=MESH,
        )
        copy.start()
        return copy


def fine_operator(nat, fxp, fyp, sp, wt, dg, lfx, lfy, lnat, where):
    lane, sub = lane_iota(), sub_iota()

    def edge(code, a, b):
        return jnp.exp2(code * 0.25 - 2.0) * jnp.where(a != b, SEAM, 1.0)

    def faces(k, carry):
        at, above = pl.ds(8 + k, 8, stride=K), pl.ds(7 + k, 8, stride=K)
        code = left_of([nat[3, t, at, :] for t in range(3)], lane)
        label = [nat[5, t, at, :] for t in range(3)]
        beside = left_of(label, lane)
        fx, fy = [], []
        for t in range(3):
            row, col = natural_place(k, t, lane, sub, where[0], where[1])
            inner = edge(code[t], beside[t], label[t])
            fx.append(jnp.where((col >= 1) & (col < where[3]), inner, 1.0))
            inner = edge(nat[4, t, above, :], nat[5, t, above, :], label[t])
            fy.append(jnp.where((row >= 1) & (row < where[2]), inner, 1.0))
        for ref, tiles in zip((fxp, fyp), dealt([fx, fy], lane)):
            for t, x in enumerate(tiles):
                ref[t, rows8(k), :] = x
        return carry

    lax.fori_loop(0, K, faces, 0, unroll=2)
    for t in range(3):
        fyp[t, rows8(K), :] = pltpu.roll(fyp[t, rows8(0), :], 7, 0)

    def weights(k, carry):
        left = [fxp[t, rows8(k), :] for t in range(3)]
        right = [left[1], left[2], lroll(left[0], 127)]
        at = pl.ds(8 + k, 8, stride=K)
        scale = []
        for t in range(3):
            up, down = fyp[t, rows8(k), :], fyp[t, rows8(k + 1), :]
            diag = SCREEN + left[t] + right[t] + up + down
            inv = jnp.where(fine_inside(k, t, lane, sub, *where), 1.0 / diag, 0.0)
            scale.append(inv)
            dg[t, rows8(k), :] = diag
            for n, face in enumerate((left[t], right[t], up, down)):
                wt[n, t, rows8(k), :] = face * inv
        natural = [[nat[ch, t, at, :] for t in range(3)] for ch in range(3)]
        for ch, tiles in enumerate(dealt(natural, lane)):
            for t, x in enumerate(tiles):
                sp[ch, t, rows8(k), :] = x * scale[t]
        return carry

    lax.fori_loop(0, K, weights, 0, unroll=2)

    def level_faces(kl, carry):
        rows = [sum(fxp[t, rows8(kl * 4 + q), :] for q in range(4)) for t in range(3)]
        x = pick(rows, lane) * 0.0625
        y = to_level([fyp[t, rows8(kl * 4), :] for t in range(3)], lane) * 0.0625
        at = pl.ds(LHALO - LPAD + kl, 8, stride=KL)
        lfx[rows8(kl), :] = x
        lfy[rows8(kl), :] = y
        lnat[6, at, :] = x
        lnat[7, at, :] = y
        return carry

    lax.fori_loop(0, KL, level_faces, 0)


def coarse_solve(
    n_row, n_col, place, send, g, s_cols, s_ext, t_back, row_eig, col_eig, nat, vpr, vpl, lev, lpr, lpl,
    vrows, vcols, vcorn, lrows, lcols, lcorn, one, two, three, mine, full, spec, back, corr,
    field_ready, with_halos,
):
    i, j, up, down, left, right = place
    n_modes = n_row * CROWS
    lane = lane_iota()

    first = [send(g, one.at[j], (i, lax.rem(j + d, n_col))) for d in range(1, n_col)]
    one[j] = g[...]
    halos = [
        send(lpr, lcols.at[0], (i, right)),
        send(lpl, lcols.at[1], (i, left)),
        send(lev.at[:, LTOP, :], lrows.at[1], (up, j)),
        send(lev.at[:, LLOW, :], lrows.at[0], (down, j)),
        send(lpr.at[LLOW, :], lcorn.at[0], (down, right)),
        send(lpl.at[LLOW, :], lcorn.at[1], (down, left)),
        send(lpr.at[LTOP, :], lcorn.at[2], (up, right)),
        send(lpl.at[LTOP, :], lcorn.at[3], (up, left)),
    ]
    field_ready()
    for copy in first:
        copy.wait()

    def placed(ref, n_rows):
        out = []
        for ch in range(3):
            parts = []
            for r in range(n_rows // 8):
                x = jnp.zeros((8, 128), F32)
                for p in range(n_col):
                    here = (lane >= CCOLS * p) & (lane < CCOLS * p + CCOLS)
                    low_half = r * 16 >= n_rows
                    row = r * 8 - n_rows // 2 if low_half else r * 8
                    y = lroll(ref[p, row : row + 8, :], CCOLS * (p - ch) - (64 if low_half else 0))
                    x = jnp.where(here, y, x)
                parts.append(x)
            out.append(jnp.concatenate(parts, axis=0))
        return out

    x = jnp.concatenate(placed(one, CROWS), axis=0)
    x = jnp.dot(x, s_cols[...], precision=HIGHEST, preferred_element_type=F32)
    total = lax.slice_in_dim(x, 0, CROWS)
    for ch in (1, 2):
        total = total + pltpu.roll(lax.slice_in_dim(x, CROWS * ch, CROWS * ch + CROWS), CCOLS * ch, 1)
    half = CROWS // 2
    total = lax.slice_in_dim(total, 0, half) + pltpu.roll(lax.slice_in_dim(total, half, CROWS), 64, 1)
    mine[...] = total
    second = [send(mine, two.at[i], (lax.rem(i + d, n_row), j)) for d in range(1, n_row)]
    two[i] = total
    halos += [
        send(vpr, vcols.at[0], (i, right)),
        send(vpl, vcols.at[1], (i, left)),
        send(vpr.at[LOW, :], vcorn.at[0], (down, right)),
        send(vpl.at[LOW, :], vcorn.at[1], (down, left)),
        send(vpr.at[TOP, :], vcorn.at[2], (up, right)),
        send(vpl.at[TOP, :], vcorn.at[3], (up, left)),
    ]
    for copy in second:
        copy.wait()
    halos += [
        send(nat.at[pl.ds(0, 3), :, FIRST, :], vrows.at[1], (up, j)),
        send(nat.at[pl.ds(0, 3), :, LAST, :], vrows.at[0], (down, j)),
    ]
    for p in range(n_row):
        for r in range(0, half, 8):
            x = two[p, r : r + 8, :]
            full[p * CROWS + r : p * CROWS + r + 8, :] = x
            full[p * CROWS + half + r : p * CROWS + half + r + 8, :] = lroll(x, 64)
    y = jnp.dot(s_ext[8 : 8 + n_modes, :], full[...], precision=HIGHEST, preferred_element_type=F32)
    eig = SCREEN + COARSE_SCALE * (row_eig[...] + col_eig[pl.ds(j, 1), :])
    spec[...] = y / eig
    rows = s_ext[pl.ds(pl.multiple_of(i * CROWS, CROWS), BROWS), :]
    z = jnp.dot(rows, spec[...], precision=HIGHEST, preferred_element_type=F32)
    half = BROWS // 2
    z = jnp.where(
        lax.broadcasted_iota(jnp.int32, (half, 128), 1) < 64,
        lax.slice_in_dim(z, 0, half), pltpu.roll(lax.slice_in_dim(z, half, BROWS), 64, 1),
    )
    back[...] = z
    third = [send(back, three.at[j], (i, lax.rem(j + d, n_col))) for d in range(1, n_col)]
    three[j] = z
    for copy in halos:
        copy.wait()
    with_halos()
    for copy in third:
        copy.wait()
    z = jnp.concatenate(placed(three, BROWS), axis=0)
    z = jnp.dot(z, t_back[...], precision=HIGHEST, preferred_element_type=F32)
    for ch in range(3):
        corr[ch] = lax.slice_in_dim(z, BROWS * ch, BROWS * ch + BROWS)


def kernel(n_row, n_col, src, codes, labels, *refs):
    tables_in, solution_out, residual_out = refs[:5], refs[5], refs[6]
    (
        codes_v, labels_v, right_pack, left_pack, srows, crows, labrows, cols, corners,
        nat, fxp, fyp, sp, wt, dg, va, vb, vpr, vpl,
        lsrc, lfx, lfy, lw, ld, li, lsp, fa, fb, lnat, lnc, lev, lpr, lpl, g,
        one, two, three, mine, full, spec, back, corr,
        vrows, vcols, vcorn, lrows, lcols, lcorn,
        s_cols, s_ext, t_back, row_eig, col_eig,
        copy_sems, table_sems, send_sems, recv_sems,
    ) = refs[7:]
    i, j = lax.axis_index("row"), lax.axis_index("col")
    up, down = lax.rem(i + n_row - 1, n_row), lax.rem(i + 1, n_row)
    left, right = lax.rem(j + n_col - 1, n_col), lax.rem(j + 1, n_col)
    where, lwhere = positions(n_row, n_col)
    lane = lane_iota()

    barrier = pltpu.get_barrier_semaphore()
    peers = [(i, lax.rem(j + d, n_col)) for d in range(1, n_col)]
    peers += [(lax.rem(i + d, n_row), j) for d in range(1, n_row)]
    peers += [(r, c) for r in (up, down) for c in (left, right)]
    for peer in peers:
        pl.semaphore_signal(barrier, inc=1, device_id=peer, device_id_type=MESH)

    loads = [pltpu.make_async_copy(codes, codes_v, copy_sems.at[0])]
    loads.append(pltpu.make_async_copy(labels, labels_v, copy_sems.at[1]))
    for a in range(3):
        for t in range(2):
            part = src.at[a, :, pl.ds(128 * t, 128)]
            loads.append(pltpu.make_async_copy(part, nat.at[a, t, MID, :], copy_sems.at[len(loads)]))
    for copy in loads:
        copy.start()
    table_loads = []
    for n, (table, ref) in enumerate(zip(tables_in, (s_cols, s_ext, t_back, row_eig, col_eig))):
        table_loads.append(pltpu.make_async_copy(table.at[j] if n in (0, 2) else table, ref, table_sems.at[n]))
        table_loads[-1].start()
    zero_ends(nat, 6)
    pl.semaphore_wait(barrier, n_col + n_row + 2)
    send = Sender(send_sems, recv_sems)
    copies = []
    for slot, rows, device in ((1, TOP, up), (0, LOW, down)):
        copies.append(send(src.at[:, rows, :], srows.at[slot], (device, j)))
        copies.append(send(codes.at[:, rows, :], crows.at[slot], (device, j)))
        copies.append(send(labels.at[rows, :], labrows.at[slot], (device, j)))
    for copy in loads:
        copy.wait()

    def convert(n, carry):
        r = rows8(n)
        at = pl.ds(pl.multiple_of(8 + PAD + 8 * n, 8), 8)
        for t in range(2):
            c = slice(128 * t, 128 * t + 128)
            nat[3, t, at, :] = codes_v[0, r, c].astype(F32)
            nat[4, t, at, :] = codes_v[1, r, c].astype(F32)
            nat[5, t, at, :] = labels_v[r, c].astype(F32)
        return carry

    lax.fori_loop(0, ROWS // 8, convert, 0, unroll=2)

    def natural(a, t, r):
        return nat[a, t, pl.ds(pl.multiple_of(8 + PAD + r.start, 8), 8), :]

    for tile, count in ((1, 2), (0, 4)):
        shifted = lambda a, t, r, tile=tile: natural(4 * tile + a, t, r)
        pack_fine(shifted, count, right_pack.at[pl.ds(tile, 1)], left_pack.at[pl.ds(tile, 1)], lane, ROWS)
        copies.append(send(right_pack.at[tile], cols.at[0, tile], (i, right)))
        copies.append(send(left_pack.at[tile], cols.at[1, tile], (i, left)))
    copies.append(send(right_pack.at[:, LOW, :], corners.at[0], (down, right)))
    copies.append(send(left_pack.at[:, LOW, :], corners.at[1], (down, left)))
    copies.append(send(right_pack.at[:, TOP, :], corners.at[2], (up, right)))
    copies.append(send(left_pack.at[:, TOP, :], corners.at[3], (up, left)))
    for copy in copies:
        copy.wait()

    for t in range(2):
        c = slice(128 * t, 128 * t + 128)
        for slot, rows in ((0, ABOVE), (1, BELOW)):
            for a in range(3):
                nat[a, t, rows, :] = srows[slot, a, :, c]
            for a in range(2):
                nat[3 + a, t, rows, :] = crows[slot, a, :, c].astype(F32)
            nat[5, t, rows, :] = labrows[slot, :, c].astype(F32)
    unpack_columns(nat, 6, cols, corners, lane)
    fine_operator(nat, fxp, fyp, sp, wt, dg, lfx, lfy, lnat, where)
    level_weights(lfx, lfy, lw, ld, li, lwhere)

    field, other = fine_smooth(va, vb, sp, wt, True)
    for cycle in range(2):
        fine_residual_to_level(field, sp, wt, dg, lsrc)
        level_down(lsrc, li, ld, lw, lsp, fa, fb, lnat, lev, lpr, lpl, g)
        got = [ref.at[cycle] for ref in (vrows, vcols, vcorn, lrows, lcols, lcorn, one, two, three)]

        def field_ready(field=field, cycle=cycle):
            field_out(field, nat, vpr, vpl)
            if cycle == 0:
                for copy in table_loads:
                    copy.wait()

        def with_halos(got=got):
            level_halos(lev, got[3], got[4], got[5], lnat, lfx, lfy, lw, ld, li, lwhere)
            fine_halos(got[0], got[1], got[2], nat)

        coarse_solve(
            n_row, n_col, (i, j, up, down, left, right), send, g, s_cols, s_ext, t_back, row_eig, col_eig,
            nat, vpr, vpl, lev, lpr, lpl, *got, mine, full, spec, back, corr, field_ready, with_halos,
        )
        level = level_up(corr, lnat, lnc, lw, li, lsp, fa, fb, lwhere)
        fine_up(level, nat, va, where)
        field, other = fine_smooth(va, vb, sp, wt, False)
        if cycle == 0:
            field, other = fine_smooth(field, other, sp, wt, False)

    fields = []

    def emit(k, ch, here, total):
        fields.append(here)
        fields.append(
            [dg[t, rows8(k), :] * (sp[ch, t, rows8(k), :] - here[t] + total[t]) for t in range(3)]
        )

    def finish(k):
        at = pl.ds(8 + k, 8, stride=K)
        for n, tiles in enumerate(undealt(fields, lane)):
            for t, x in enumerate(tiles):
                nat[n // 2 + 3 * (n % 2), t, at, :] = x
        fields.clear()

    stencil_pass(field, wt, emit, 1, finish)
    stores = []
    for a in range(6):
        for t in range(2):
            out = (solution_out if a < 3 else residual_out).at[a % 3, :, pl.ds(128 * t, 128)]
            stores.append(pltpu.make_async_copy(nat.at[a, t, MID, :], out, copy_sems.at[len(stores)]))
    for copy in stores:
        copy.start()
    for copy in stores:
        copy.wait()


@functools.lru_cache(maxsize=None)
def tables(n_row, n_col):
    def sines(n):
        k = np.arange(1, n + 1)
        return math.sqrt(2.0 / (n + 1)) * np.sin(np.pi * ((k[:, None] * k[None, :]) % (2 * (n + 1))) / (n + 1))

    def eig(n):
        return 2.0 - 2.0 * np.cos(np.pi * np.arange(1, n + 1) / (n + 1))

    nr, nc = n_row * CROWS, n_col * CCOLS
    rows, cols = sines(nr), sines(nc)
    s_cols = np.zeros((n_col, 128, 128))
    t_back = np.zeros((n_col, 128, 128))
    col_eig = np.ones((n_col, 128))
    lane = np.arange(128)
    for j in range(n_col):
        own = slice(CCOLS * j, CCOLS * j + CCOLS)
        s_cols[j, :nc, :CCOLS] = cols[:, own]
        col_eig[j, : 3 * CCOLS] = np.tile(eig(nc)[own], 3)
        c = LCOLS * j + lane - LHALO
        ok = (c >= 0) & (c < n_col * LCOLS) & (lane < 96)
        t_back[j, :nc, ok] = cols[:, c[ok] // 4].T
    s_ext = np.zeros((nr + 16, nr))
    s_ext[8 : 8 + nr] = rows
    row_eig = np.repeat(eig(nr)[:, None], 128, axis=1)
    return tuple(x.astype(np.float32) for x in (s_cols, s_ext, t_back, row_eig, col_eig))


def shape(*dims, dtype=F32):
    return jax.ShapeDtypeStruct(dims, dtype)


IN_VMEM = pl.BlockSpec(memory_space=pltpu.VMEM)
IN_ANY = pl.BlockSpec(memory_space=pl.ANY)


def solution(mesh):
    n_row, n_col = mesh.shape["row"], mesh.shape["col"]

    def vmem(*dims, dtype=F32):
        return pltpu.VMEM(dims, dtype)

    n_copies = 14 + 2 * (2 * (n_col - 1) + (n_row - 1) + 16)
    scratch = [
        vmem(2, ROWS, COLS, dtype=jnp.int32), vmem(ROWS, COLS, dtype=jnp.int32),
        vmem(2, ROWS, 128), vmem(2, ROWS, 128),
        vmem(2, 3, HALO, COLS), vmem(2, 2, HALO, COLS, dtype=jnp.int32), vmem(2, HALO, COLS, dtype=jnp.int32),
        vmem(2, 2, ROWS, 128), vmem(4, 2, HALO, 128),
        vmem(6, 3, NAT, 128), vmem(3, K * 8, 128), vmem(3, (K + 1) * 8, 128),
        vmem(3, 3, K * 8, 128), vmem(4, 3, K * 8, 128), vmem(3, K * 8, 128),
        vmem(3, 3, (K + 2) * 8, 128), vmem(3, 3, (K + 2) * 8, 128),
        vmem(ROWS, 128), vmem(ROWS, 128),
        vmem(3, KL * 8, 128), vmem(KL * 8, 128), vmem((KL + 1) * 8, 128),
        vmem(4, KL * 8, 128), vmem(KL * 8, 128), vmem(KL * 8, 128), vmem(3, KL * 8, 128),
        vmem(3, (KL + 2) * 8, 128), vmem(3, (KL + 2) * 8, 128),
        vmem(11, LNAT, 128), vmem(3, LNAT, 128), vmem(8, LROWS, 128),
        vmem(LROWS, 128), vmem(LROWS, 128), vmem(CROWS // 2, 128),
        vmem(2, n_col, CROWS // 2, 128), vmem(2, n_row, CROWS // 2, 128), vmem(2, n_col, BROWS // 2, 128),
        vmem(CROWS // 2, 128), vmem(n_row * CROWS, 128), vmem(n_row * CROWS, 128),
        vmem(BROWS // 2, 128), vmem(3, BROWS, 128),
        vmem(2, 2, 3, 3, HALO, 128), vmem(2, 2, ROWS, 128), vmem(2, 4, HALO, 128),
        vmem(2, 2, 8, LHALO, 128), vmem(2, 2, LROWS, 128), vmem(2, 4, LHALO, 128),
        vmem(128, 128), vmem(n_row * CROWS + 16, n_row * CROWS), vmem(128, 128),
        vmem(n_row * CROWS, 128), vmem(n_col, 128),
        pltpu.SemaphoreType.DMA((12,)), pltpu.SemaphoreType.DMA((5,)),
        pltpu.SemaphoreType.DMA((n_copies,)), pltpu.SemaphoreType.DMA((n_copies,)),
    ]
    call = pl.pallas_call(
        functools.partial(kernel, n_row, n_col),
        out_shape=[shape(3, ROWS, COLS)] * 2,
        in_specs=[IN_ANY] * 8,
        out_specs=[IN_ANY] * 2,
        scratch_shapes=scratch,
        compiler_params=pltpu.CompilerParams(collective_id=0, has_side_effects=True, vmem_limit_bytes=VMEM_LIMIT),
    )
    consts = tables(n_row, n_col)

    def local(sources, edge_codes, seam_labels):
        return tuple(call(sources, edge_codes, seam_labels, *consts))

    spec = P(None, "row", "col")
    return jax.shard_map(
        local, mesh=mesh, in_specs=(spec, spec, P("row", "col")), out_specs=(spec, spec), check_vma=False
    )
```

```python
import functools
import math

import jax
import jax.numpy as jnp
import numpy as np
from jax import lax
from jax.experimental import pallas as pl
from jax.experimental.pallas import tpu as pltpu
from jax.sharding import PartitionSpec as P

SWEEPS = 4
SCREEN = 2e-05
SEAM = 0.2
COARSE_SCALE = 0.0625
F32 = jnp.float32
MESH = pl.DeviceIdType.MESH
HIGHEST = lax.Precision.HIGHEST

ROWS, COLS = 512, 256
PAD = 48
HALO = 32
K = (ROWS + 2 * PAD) // 8
NAT = 8 + ROWS + 2 * PAD + 8
LROWS, LCOLS = 128, 64
LPAD = PAD // 4
LHALO = 16
KL = (LROWS + 2 * LPAD) // 8
LNAT = LROWS + 2 * LHALO
CROWS, CCOLS = 32, 16
BROWS = CROWS + 16
VMEM_LIMIT = 62 * 1024 * 1024


def chebyshev_weight(sweep_index):
    return 1.0 / (1.25 + 0.75 * math.cos(math.pi * (2 * sweep_index + 1) / (2 * SWEEPS)))


def lane_iota():
    return lax.broadcasted_iota(jnp.int32, (8, 128), 1)


def sub_iota():
    return lax.broadcasted_iota(jnp.int32, (8, 128), 0)


def lroll(x, shift):
    shift = shift % 128
    return x if shift == 0 else pltpu.roll(x, shift, 1)


def rows8(k):
    return pl.ds(pl.multiple_of(k * 8, 8), 8)


def lanes_take(x, idx):
    return jnp.take_along_axis(x, idx, axis=1)


def left_of(tiles, lane):
    rolled = [lroll(x, 1) for x in tiles]
    return [jnp.where(lane == 0, rolled[(t + 2) % 3], rolled[t]) for t in range(3)]


def set_pads(ref, lead, count):
    last = ref[lead + (rows8(count), slice(None))]
    first = ref[lead + (rows8(1), slice(None))]
    ref[lead + (rows8(0), slice(None))] = pltpu.roll(last, 1, 0)
    ref[lead + (rows8(count + 1), slice(None))] = pltpu.roll(first, 7, 0)


def pack_fine(tile_of, n_arrays, right, left, lane, rows):
    def body(i, carry):
        r = rows8(i)
        for first in range(0, n_arrays, 4):
            out_r = out_l = jnp.zeros((8, 128), F32)
            for a in range(first, min(first + 4, n_arrays)):
                g = a - first
                here = (lane >= 32 * g) & (lane < 32 * g + 32)
                out_r = jnp.where(here, lroll(tile_of(a, 1, r), 32 * g - 96), out_r)
                out_l = jnp.where(here, lroll(tile_of(a, 0, r), 32 * g), out_l)
            right[first // 4, r, :] = out_r
            left[first // 4, r, :] = out_l
        return carry

    lax.fori_loop(0, rows // 8, body, 0)


def unpack_fine(nat, n_arrays, at, count, from_left, from_right, lane):
    def body(i, carry):
        src = rows8(i)
        dst = pl.ds(pl.multiple_of(at + i * 8, 8), 8)
        for a in range(n_arrays):
            g = a % 4
            l = lroll(from_left[a // 4, src, :], 96 - 32 * g)
            r = lroll(from_right[a // 4, src, :], -32 * g)
            nat[a, 2, dst, :] = jnp.where(lane < 32, r, jnp.where(lane >= 96, l, 0.0))
        return carry

    lax.fori_loop(0, count, body, 0)


def zero_ends(nat, n_arrays):
    zero = jnp.zeros((8, 128), F32)
    for a in range(n_arrays):
        for t in range(3):
            for r in (0, 8, 16, NAT - 24, NAT - 16, NAT - 8):
                nat[a, t, r : r + 8, :] = zero


def unpack_columns(nat, n_arrays, cols, corners, lane):
    unpack_fine(nat, n_arrays, 8 + PAD, ROWS // 8, cols.at[0], cols.at[1], lane)
    unpack_fine(nat, n_arrays, 8 + PAD - HALO, HALO // 8, corners.at[0], corners.at[1], lane)
    unpack_fine(nat, n_arrays, 8 + PAD + ROWS, HALO // 8, corners.at[2], corners.at[3], lane)


CPAD = 64
EDGE, EDGE_RIGHT, EDGE_LEFT = 11, 96, 21


def pack_field(nat, right, left):
    lane = lane_iota()

    def body(i, carry):
        r = pl.ds(pl.multiple_of(8 + PAD + i * 8, 8), 8)
        out_r = out_l = jnp.zeros((8, 128), F32)
        for q in range(9):
            x = nat[q // 3, q % 3, r, :]
            here = (lane >= EDGE * q) & (lane < EDGE * q + EDGE)
            out_r = jnp.where(here, lroll(x, EDGE * q - EDGE_RIGHT), out_r)
            out_l = jnp.where(here, lroll(x, EDGE * q - EDGE_LEFT), out_l)
        right[rows8(i), :] = out_r
        left[rows8(i), :] = out_l
        return carry

    lax.fori_loop(0, ROWS // 8, body, 0, unroll=2)


def unpack_field(nat, at, count, own, from_left, from_right):
    lane = lane_iota()

    def body(i, carry):
        dst = pl.ds(pl.multiple_of(at + i * 8, 8), 8)
        l, r = from_left[rows8(i), :], from_right[rows8(i), :]
        for ch in range(3):
            for t in range(3):
                p = 3 * lane + t
                u = (t + 1) % 3
                a = lroll(l, EDGE_RIGHT - (86 if u == 0 else 85) - EDGE * (3 * ch + u))
                u = (t + 2) % 3
                b = lroll(r, EDGE_LEFT + (86 if u == 2 else 85) - EDGE * (3 * ch + u))
                x = jnp.where((p >= CPAD - HALO) & (p < CPAD), a, own(ch, t, i, dst))
                x = jnp.where((p >= CPAD + COLS) & (p < CPAD + COLS + HALO), b, x)
                nat[ch, t, dst, :] = x
        return carry

    lax.fori_loop(0, count, body, 0, unroll=2)


def dealt(fields, lane):
    out = [[] for _ in fields]
    for t in range(3):
        p = 3 * lane + t
        idx = (p - CPAD) % 128
        for x, y in zip(fields, out):
            got = [lanes_take(part, idx) for part in x]
            y.append(jnp.where((p < 64) | (p >= 320), got[2], jnp.where(p < 192, got[0], got[1])))
    return out


def deal_sources(nat, out, at, count, parts):
    lane = lane_iota()

    def body(i, carry):
        r = pl.ds(pl.multiple_of(at + 8 * i, 8), 8)
        for t in range(3):
            p = 3 * lane + t
            idx = (p - CPAD) % 128
            for ch in range(3):
                got = {n: lanes_take(nat[ch, n, r, :], idx) for n in parts}
                x = jnp.where(p < 192, got[0], got[1]) if 0 in got else out[ch, t, r, :]
                out[ch, t, r, :] = jnp.where((p < 64) | (p >= 320), got[2], x) if 2 in got else x
        return carry

    lax.fori_loop(0, count, body, 0, unroll=2)


def undealt(fields, lane):
    out = [[] for _ in fields]
    for t in range(2):
        p = lane + (128 * t + CPAD)
        idx = p // 3
        for x, y in zip(fields, out):
            got = [lanes_take(part, idx) for part in x]
            y.append(jnp.where(p % 3 == 0, got[0], jnp.where(p % 3 == 1, got[1], got[2])))
    return out


def natural_place(k, t, lane, sub, row0, col0):
    row = row0 - PAD + sub * K + k
    if t < 2:
        return row, lane + (col0 + 128 * t)
    return row, jnp.where(lane < 64, lane + (col0 + 256), lane + (col0 - 128))


def fine_inside(k, t, lane, sub, row0, col0, n_rows, n_cols):
    row = row0 - PAD + sub * K + k
    col = 3 * lane + (t - CPAD + col0)
    return (row >= 0) & (row < n_rows) & (col >= 0) & (col < n_cols)


def level_inside(k, lane, sub, row0, col0, n_rows, n_cols):
    row = row0 - LPAD + sub * KL + k
    col = lane - LHALO + col0
    return (row >= 0) & (row < n_rows) & (col >= 0) & (col < n_cols) & (lane < 96)


def stencil_pass(v, wt, emit, unroll, end=None):
    def row(k):
        w = [[wt[n, t, rows8(k), :] for t in range(3)] for n in range(4)]
        for ch in range(3):
            here = [v[ch, t, rows8(k + 1), :] for t in range(3)]
            left = [lroll(here[2], 1), here[0], here[1]]
            right = [here[1], here[2], lroll(here[0], 127)]
            total = []
            for t in range(3):
                x = w[2][t] * v[ch, t, rows8(k), :] + w[3][t] * v[ch, t, rows8(k + 2), :]
                total.append(x + (w[0][t] * left[t] + w[1][t] * right[t]))
            emit(k, ch, here, total)

    def body(m, carry):
        for q in range(unroll):
            row(unroll * m + q)
        if end is not None:
            end(m)
        return carry

    lax.fori_loop(0, K // unroll, body, 0)


def fine_pads(v):
    for ch in range(3):
        for t in range(3):
            set_pads(v, (ch, t), K)


def fine_sweep(vin, vout, sp, wt, omega):
    def emit(k, ch, here, total):
        for t in range(3):
            new = sp[ch, t, rows8(k), :] + total[t]
            vout[ch, t, rows8(k + 1), :] = (1.0 - omega) * here[t] + omega * new

    stencil_pass(vin, wt, emit, 4)
    fine_pads(vout)


def fine_first(vout, sp):
    omega = chebyshev_weight(0)

    def body(k, carry):
        for ch in range(3):
            for t in range(3):
                vout[ch, t, rows8(k + 1), :] = omega * sp[ch, t, rows8(k), :]
        return carry

    lax.fori_loop(0, K, body, 0)
    fine_pads(vout)


def fine_smooth(va, vb, sp, wt, from_zero):
    bufs = [va, vb]
    at = 0
    for i in range(SWEEPS):
        if i == 0 and from_zero:
            fine_first(va, sp)
            continue
        fine_sweep(bufs[at], bufs[1 - at], sp, wt, chebyshev_weight(i))
        at = 1 - at
    return bufs[at], bufs[1 - at]


def pick(x, lane):
    got = [lanes_take(y, jnp.minimum((4 * lane) // 3, 127)) for y in x]
    return jnp.where(lane % 3 == 0, got[0], jnp.where(lane % 3 == 1, got[1], got[2]))


def to_level(x, lane):
    after = [lroll(y, 127) for y in x]
    mid, first = x[1] + x[2], after[0] + after[1]
    sums = [x[0] + mid + after[0], mid + first, x[2] + first + after[2]]
    return pick(sums, lane)


def fine_residual_to_level(v, sp, wt, dg, lsrc):
    lane = lane_iota()
    acc = {}

    def emit(k, ch, here, total):
        res = [dg[t, rows8(k), :] * (sp[ch, t, rows8(k), :] - here[t] + total[t]) for t in range(3)]
        acc[ch] = [a + b for a, b in zip(acc[ch], res)] if ch in acc else res

    def end(m):
        for ch in range(3):
            lsrc[ch, rows8(m), :] = to_level(acc.pop(ch), lane) * 0.0625

    stencil_pass(v, wt, emit, 4, end)


def level_weights(fx, fy, lw, ld, li, where):
    lane, sub = lane_iota(), sub_iota()
    fy[rows8(KL), :] = pltpu.roll(fy[rows8(0), :], 7, 0)

    def body(k, carry):
        left, up, down = fx[rows8(k), :], fy[rows8(k), :], fy[rows8(k + 1), :]
        right = lroll(left, 127)
        diag = SCREEN + left + right + up + down
        inv = jnp.where(level_inside(k, lane, sub, *where), 1.0 / diag, 0.0)
        ld[rows8(k), :] = diag
        li[rows8(k), :] = inv
        for n, face in enumerate((left, right, up, down)):
            lw[n, rows8(k), :] = face * inv
        return carry

    lax.fori_loop(0, KL, body, 0)


def level_neighbours(f, lw, k, ch):
    here = f[ch, rows8(k + 1), :]
    total = lw[0, rows8(k), :] * lroll(here, 1) + lw[1, rows8(k), :] * lroll(here, 127)
    return here, total + lw[2, rows8(k), :] * f[ch, rows8(k), :] + lw[3, rows8(k), :] * f[ch, rows8(k + 2), :]


def level_pads(f):
    for ch in range(3):
        set_pads(f, (ch,), KL)


def level_smooth(fa, fb, lsp, lw, from_zero):
    bufs = [fa, fb]
    at = 0
    for i in range(SWEEPS):
        omega = chebyshev_weight(i)
        src, dst = bufs[at], bufs[1 - at]
        if i == 0 and from_zero:

            def first(k, carry):
                for ch in range(3):
                    src[ch, rows8(k + 1), :] = omega * lsp[ch, rows8(k), :]
                return carry

            lax.fori_loop(0, KL, first, 0, unroll=True)
            level_pads(src)
            continue

        def body(k, carry):
            for ch in range(3):
                here, total = level_neighbours(src, lw, k, ch)
                dst[ch, rows8(k + 1), :] = (1.0 - omega) * here + omega * (lsp[ch, rows8(k), :] + total)
            return carry

        lax.fori_loop(0, KL, body, 0, unroll=True)
        level_pads(dst)
        at = 1 - at
    return bufs[at]


def level_down(lsrc, li, ld, lw, lsp, fa, fb, lnat, lev, lpr, lpl, g):
    lane = lane_iota()

    def scale(k, carry):
        for ch in range(3):
            lsp[ch, rows8(k), :] = lsrc[ch, rows8(k), :] * li[rows8(k), :]
        return carry

    lax.fori_loop(0, KL, scale, 0, unroll=True)
    f = level_smooth(fa, fb, lsp, lw, True)

    def out(k, carry):
        at = pl.ds(LHALO - LPAD + k, 8, stride=KL)
        for ch in range(3):
            here, total = level_neighbours(f, lw, k, ch)
            lnat[8 + ch, at, :] = ld[rows8(k), :] * (lsp[ch, rows8(k), :] - here + total)
            lnat[ch, at, :] = here
            lnat[3 + ch, at, :] = lsrc[ch, rows8(k), :]
        return carry

    lax.fori_loop(0, KL, out, 0, unroll=True)

    def copy(i, carry):
        src = pl.ds(pl.multiple_of(LHALO + i * 8, 8), 8)
        right = left = jnp.zeros((8, 128), F32)
        for a in range(8):
            x = lnat[a, src, :]
            lev[a, rows8(i), :] = x
            here = (lane >= 16 * a) & (lane < 16 * a + 16)
            right = jnp.where(here, lroll(x, 16 * a - 64), right)
            left = jnp.where(here, lroll(x, 16 * a - 16), left)
        lpr[rows8(i), :] = right
        lpl[rows8(i), :] = left
        return carry

    lax.fori_loop(0, LROWS // 8, copy, 0)
    idx = (LHALO + 4 * lane) % 128
    parts = []
    for i in range(CROWS // 8):
        total = jnp.zeros((8, 128), F32)
        for ch in range(3):
            x = sum(lnat[8 + ch, pl.ds(LHALO + 32 * i + q, 8, stride=4), :] for q in range(4))
            x = x + lroll(x, 127)
            x = x + lroll(x, 126)
            x = jnp.where(lane < CCOLS, lanes_take(x, idx), 0.0) * 0.0625
            total = total + lroll(x, CCOLS * ch)
        parts.append(total)
    half = len(parts) // 2
    for i in range(half):
        g[i * 8 : i * 8 + 8, :] = parts[i] + lroll(parts[half + i], 64)


def level_halos(lev, lrows, lcols, lcorn, lnat, fx, fy, lw, ld, li, where):
    lane = lane_iota()

    def place(dst_row, count, own, left, right):
        def body(i, carry):
            dst = pl.ds(pl.multiple_of(dst_row + i * 8, 8), 8)
            l, r = left(rows8(i)), right(rows8(i))
            for a in range(8):
                x = jnp.where((lane >= 80) & (lane < 96), lroll(r, 80 - 16 * a), 0.0)
                x = jnp.where((lane >= 16) & (lane < 80), own(a, rows8(i)), x)
                lnat[a, dst, :] = jnp.where(lane < 16, lroll(l, -16 * a), x)
            return carry

        lax.fori_loop(0, count, body, 0)

    place(0, LHALO // 8, lambda a, r: lrows[0, a, r, :], lambda r: lcorn[0, r, :], lambda r: lcorn[1, r, :])
    place(LHALO, LROWS // 8, lambda a, r: lev[a, r, :], lambda r: lcols[0, r, :], lambda r: lcols[1, r, :])
    place(LHALO + LROWS, LHALO // 8, lambda a, r: lrows[1, a, r, :], lambda r: lcorn[2, r, :], lambda r: lcorn[3, r, :])
    def faces(k, carry):
        at = pl.ds(LHALO - LPAD + k, 8, stride=KL)
        fx[rows8(k), :] = lnat[6, at, :]
        fy[rows8(k), :] = lnat[7, at, :]
        return carry

    lax.fori_loop(0, KL, faces, 0)
    level_weights(fx, fy, lw, ld, li, where)


def level_up(corr, lnat, lnc, lw, li, lsp, fa, fb, where):
    lane, sub = lane_iota(), sub_iota()
    for ch in range(3):
        for h in range(LNAT // 32):
            x = corr[ch, 4 + 8 * h : 12 + 8 * h, :]
            for q in range(4):
                lnc[ch, pl.ds(32 * h + q, 8, stride=4), :] = x

    def fields(k, carry):
        at = pl.ds(LHALO - LPAD + k, 8, stride=KL)
        inside = level_inside(k, lane, sub, *where)
        inv = li[rows8(k), :]
        for ch in range(3):
            fa[ch, rows8(k + 1), :] = jnp.where(inside, lnat[ch, at, :] + lnc[ch, at, :], 0.0)
            lsp[ch, rows8(k), :] = lnat[3 + ch, at, :] * inv
        return carry

    lax.fori_loop(0, KL, fields, 0, unroll=True)
    level_pads(fa)
    return level_smooth(fa, fb, lsp, lw, False)


def fine_halos(vrows, vcols, vcorn, nat):
    unpack_field(nat, 8 + PAD, ROWS // 8, lambda ch, t, i, r: nat[ch, t, r, :], vcols.at[0], vcols.at[1])
    for slot, at in ((0, 8 + PAD - HALO), (1, 8 + PAD + ROWS)):
        own = lambda ch, t, i, r, slot=slot: vrows[slot, ch, t, rows8(i), :]
        unpack_field(nat, at, HALO // 8, own, vcorn.at[2 * slot], vcorn.at[2 * slot + 1])


def fine_up(field, nat, va, where):
    lane, sub = lane_iota(), sub_iota()

    def body(kl, carry):
        for t in range(3):
            idx = jnp.minimum((3 * lane + t) // 4, 127)
            inside = [fine_inside(kl * 4 + q, t, lane, sub, *where) for q in range(4)]
            for ch in range(3):
                add = lanes_take(field[ch, rows8(kl + 1), :], idx)
                for q in range(4):
                    x = nat[ch, t, pl.ds(8 + kl * 4 + q, 8, stride=K), :] + add
                    va[ch, t, rows8(kl * 4 + q + 1), :] = jnp.where(inside[q], x, 0.0)
        return carry

    lax.fori_loop(0, KL, body, 0)
    fine_pads(va)


def field_out(field, nat, vpr, vpl):
    def body(m, carry):
        for q in range(2):
            k = 2 * m + q
            for ch in range(3):
                for t in range(3):
                    nat[ch, t, pl.ds(8 + k, 8, stride=K), :] = field[ch, t, rows8(k + 1), :]
        return carry

    lax.fori_loop(0, K // 2, body, 0)
    pack_field(nat, vpr, vpl)


def positions(n_row, n_col):
    i, j = lax.axis_index("row"), lax.axis_index("col")
    fine = (i * ROWS, j * COLS, n_row * ROWS, n_col * COLS)
    level = (i * LROWS, j * LCOLS, n_row * LROWS, n_col * LCOLS)
    return fine, level


TOP, LOW = pl.ds(0, HALO), pl.ds(ROWS - HALO, HALO)
LTOP, LLOW = pl.ds(0, LHALO), pl.ds(LROWS - LHALO, LHALO)
MID = pl.ds(8 + PAD, ROWS)
FIRST, LAST = pl.ds(8 + PAD, HALO), pl.ds(8 + PAD + ROWS - HALO, HALO)
ABOVE, BELOW = pl.ds(8 + PAD - HALO, HALO), pl.ds(8 + PAD + ROWS, HALO)


class Sender:
    def __init__(self, send_sems, recv_sems):
        self.send_sems, self.recv_sems, self.count = send_sems, recv_sems, 0

    def __call__(self, src, dst, device):
        n = self.count
        self.count += 1
        copy = pltpu.make_async_remote_copy(
            src_ref=src, dst_ref=dst, send_sem=self.send_sems.at[n], recv_sem=self.recv_sems.at[n],
            device_id=device, device_id_type=MESH,
        )
        copy.start()
        return copy


def fine_operator(nat, dealt_src, fxp, fyp, sp, wt, dg, lfx, lfy, lnat, where):
    lane, sub = lane_iota(), sub_iota()

    def edge(code, a, b):
        return jnp.exp2(code * 0.25 - 2.0) * jnp.where(a != b, SEAM, 1.0)

    def faces(k, carry):
        at, above = pl.ds(8 + k, 8, stride=K), pl.ds(7 + k, 8, stride=K)
        code = left_of([nat[3, t, at, :] for t in range(3)], lane)
        label = [nat[5, t, at, :] for t in range(3)]
        beside = left_of(label, lane)
        fx, fy = [], []
        for t in range(3):
            row, col = natural_place(k, t, lane, sub, where[0], where[1])
            inner = edge(code[t], beside[t], label[t])
            fx.append(jnp.where((col >= 1) & (col < where[3]), inner, 1.0))
            inner = edge(nat[4, t, above, :], nat[5, t, above, :], label[t])
            fy.append(jnp.where((row >= 1) & (row < where[2]), inner, 1.0))
        for ref, tiles in zip((fxp, fyp), dealt([fx, fy], lane)):
            for t, x in enumerate(tiles):
                ref[t, rows8(k), :] = x
        return carry

    lax.fori_loop(0, K, faces, 0, unroll=2)
    for t in range(3):
        fyp[t, rows8(K), :] = pltpu.roll(fyp[t, rows8(0), :], 7, 0)

    def weights(k, carry):
        left = [fxp[t, rows8(k), :] for t in range(3)]
        right = [left[1], left[2], lroll(left[0], 127)]
        at = pl.ds(8 + k, 8, stride=K)
        scale = []
        for t in range(3):
            up, down = fyp[t, rows8(k), :], fyp[t, rows8(k + 1), :]
            diag = SCREEN + left[t] + right[t] + up + down
            inv = jnp.where(fine_inside(k, t, lane, sub, *where), 1.0 / diag, 0.0)
            scale.append(inv)
            dg[t, rows8(k), :] = diag
            for n, face in enumerate((left[t], right[t], up, down)):
                wt[n, t, rows8(k), :] = face * inv
        for ch in range(3):
            for t in range(3):
                sp[ch, t, rows8(k), :] = dealt_src[ch, t, at, :] * scale[t]
        return carry

    lax.fori_loop(0, K, weights, 0, unroll=2)

    def level_faces(kl, carry):
        rows = [sum(fxp[t, rows8(kl * 4 + q), :] for q in range(4)) for t in range(3)]
        x = pick(rows, lane) * 0.0625
        y = to_level([fyp[t, rows8(kl * 4), :] for t in range(3)], lane) * 0.0625
        at = pl.ds(LHALO - LPAD + kl, 8, stride=KL)
        lfx[rows8(kl), :] = x
        lfy[rows8(kl), :] = y
        lnat[6, at, :] = x
        lnat[7, at, :] = y
        return carry

    lax.fori_loop(0, KL, level_faces, 0)


def coarse_solve(
    n_row, n_col, place, send, g, s_cols, s_ext, t_back, row_eig, col_eig, nat, vpr, vpl, lev, lpr, lpl,
    vrows, vcols, vcorn, lrows, lcols, lcorn, one, two, three, mine, full, spec, back, corr,
    field_ready, with_halos,
):
    i, j, up, down, left, right = place
    n_modes = n_row * CROWS
    lane = lane_iota()

    first = [send(g, one.at[j], (i, lax.rem(j + d, n_col))) for d in range(1, n_col)]
    one[j] = g[...]
    halos = [
        send(lpr, lcols.at[0], (i, right)),
        send(lpl, lcols.at[1], (i, left)),
        send(lev.at[:, LTOP, :], lrows.at[1], (up, j)),
        send(lev.at[:, LLOW, :], lrows.at[0], (down, j)),
        send(lpr.at[LLOW, :], lcorn.at[0], (down, right)),
        send(lpl.at[LLOW, :], lcorn.at[1], (down, left)),
        send(lpr.at[LTOP, :], lcorn.at[2], (up, right)),
        send(lpl.at[LTOP, :], lcorn.at[3], (up, left)),
    ]
    field_ready()
    for copy in first:
        copy.wait()

    def placed(ref, n_rows):
        out = []
        for ch in range(3):
            parts = []
            for r in range(n_rows // 8):
                x = jnp.zeros((8, 128), F32)
                for p in range(n_col):
                    here = (lane >= CCOLS * p) & (lane < CCOLS * p + CCOLS)
                    low_half = r * 16 >= n_rows
                    row = r * 8 - n_rows // 2 if low_half else r * 8
                    y = lroll(ref[p, row : row + 8, :], CCOLS * (p - ch) - (64 if low_half else 0))
                    x = jnp.where(here, y, x)
                parts.append(x)
            out.append(jnp.concatenate(parts, axis=0))
        return out

    x = jnp.concatenate(placed(one, CROWS), axis=0)
    x = jnp.dot(x, s_cols[...], precision=HIGHEST, preferred_element_type=F32)
    total = lax.slice_in_dim(x, 0, CROWS)
    for ch in (1, 2):
        total = total + pltpu.roll(lax.slice_in_dim(x, CROWS * ch, CROWS * ch + CROWS), CCOLS * ch, 1)
    half = CROWS // 2
    total = lax.slice_in_dim(total, 0, half) + pltpu.roll(lax.slice_in_dim(total, half, CROWS), 64, 1)
    mine[...] = total
    second = [send(mine, two.at[i], (lax.rem(i + d, n_row), j)) for d in range(1, n_row)]
    two[i] = total
    halos += [
        send(vpr, vcols.at[0], (i, right)),
        send(vpl, vcols.at[1], (i, left)),
        send(vpr.at[LOW, :], vcorn.at[0], (down, right)),
        send(vpl.at[LOW, :], vcorn.at[1], (down, left)),
        send(vpr.at[TOP, :], vcorn.at[2], (up, right)),
        send(vpl.at[TOP, :], vcorn.at[3], (up, left)),
    ]
    for copy in second:
        copy.wait()
    halos += [
        send(nat.at[pl.ds(0, 3), :, FIRST, :], vrows.at[1], (up, j)),
        send(nat.at[pl.ds(0, 3), :, LAST, :], vrows.at[0], (down, j)),
    ]
    for p in range(n_row):
        for r in range(0, half, 8):
            x = two[p, r : r + 8, :]
            full[p * CROWS + r : p * CROWS + r + 8, :] = x
            full[p * CROWS + half + r : p * CROWS + half + r + 8, :] = lroll(x, 64)
    y = jnp.dot(s_ext[8 : 8 + n_modes, :], full[...], precision=HIGHEST, preferred_element_type=F32)
    eig = SCREEN + COARSE_SCALE * (row_eig[...] + col_eig[pl.ds(j, 1), :])
    spec[...] = y / eig
    rows = s_ext[pl.ds(pl.multiple_of(i * CROWS, CROWS), BROWS), :]
    z = jnp.dot(rows, spec[...], precision=HIGHEST, preferred_element_type=F32)
    half = BROWS // 2
    z = jnp.where(
        lax.broadcasted_iota(jnp.int32, (half, 128), 1) < 64,
        lax.slice_in_dim(z, 0, half), pltpu.roll(lax.slice_in_dim(z, half, BROWS), 64, 1),
    )
    back[...] = z
    third = [send(back, three.at[j], (i, lax.rem(j + d, n_col))) for d in range(1, n_col)]
    three[j] = z
    for copy in halos:
        copy.wait()
    with_halos()
    for copy in third:
        copy.wait()
    z = jnp.concatenate(placed(three, BROWS), axis=0)
    z = jnp.dot(z, t_back[...], precision=HIGHEST, preferred_element_type=F32)
    for ch in range(3):
        corr[ch] = lax.slice_in_dim(z, BROWS * ch, BROWS * ch + BROWS)


def kernel(n_row, n_col, src, codes, labels, *refs):
    tables_in, solution_out, residual_out = refs[:5], refs[5], refs[6]
    (
        codes_v, labels_v, right_pack, left_pack, srows, crows, labrows, cols, corners,
        nat, fxp, fyp, sp, wt, dg, va, vb, vpr, vpl,
        lsrc, lfx, lfy, lw, ld, li, lsp, fa, fb, lnat, lnc, lev, lpr, lpl, g,
        one, two, three, mine, full, spec, back, corr,
        vrows, vcols, vcorn, lrows, lcols, lcorn,
        s_cols, s_ext, t_back, row_eig, col_eig,
        copy_sems, table_sems, send_sems, recv_sems,
    ) = refs[7:]
    i, j = lax.axis_index("row"), lax.axis_index("col")
    up, down = lax.rem(i + n_row - 1, n_row), lax.rem(i + 1, n_row)
    left, right = lax.rem(j + n_col - 1, n_col), lax.rem(j + 1, n_col)
    where, lwhere = positions(n_row, n_col)
    lane = lane_iota()

    barrier = pltpu.get_barrier_semaphore()
    peers = [(i, lax.rem(j + d, n_col)) for d in range(1, n_col)]
    peers += [(lax.rem(i + d, n_row), j) for d in range(1, n_row)]
    peers += [(r, c) for r in (up, down) for c in (left, right)]
    for peer in peers:
        pl.semaphore_signal(barrier, inc=1, device_id=peer, device_id_type=MESH)

    loads = [pltpu.make_async_copy(codes, codes_v, copy_sems.at[0])]
    loads.append(pltpu.make_async_copy(labels, labels_v, copy_sems.at[1]))
    for a in range(3):
        for t in range(2):
            part = src.at[a, :, pl.ds(128 * t, 128)]
            loads.append(pltpu.make_async_copy(part, nat.at[a, t, MID, :], copy_sems.at[len(loads)]))
    for copy in loads:
        copy.start()
    table_loads = []
    for n, (table, ref) in enumerate(zip(tables_in, (s_cols, s_ext, t_back, row_eig, col_eig))):
        table_loads.append(pltpu.make_async_copy(table.at[j] if n in (0, 2) else table, ref, table_sems.at[n]))
        table_loads[-1].start()
    zero_ends(nat, 6)
    pl.semaphore_wait(barrier, n_col + n_row + 2)
    send = Sender(send_sems, recv_sems)
    copies = []
    for slot, rows, device in ((1, TOP, up), (0, LOW, down)):
        copies.append(send(src.at[:, rows, :], srows.at[slot], (device, j)))
        copies.append(send(codes.at[:, rows, :], crows.at[slot], (device, j)))
        copies.append(send(labels.at[rows, :], labrows.at[slot], (device, j)))
    for copy in loads:
        copy.wait()

    def convert(n, carry):
        r = rows8(n)
        at = pl.ds(pl.multiple_of(8 + PAD + 8 * n, 8), 8)
        for t in range(2):
            c = slice(128 * t, 128 * t + 128)
            nat[3, t, at, :] = codes_v[0, r, c].astype(F32)
            nat[4, t, at, :] = codes_v[1, r, c].astype(F32)
            nat[5, t, at, :] = labels_v[r, c].astype(F32)
        return carry

    lax.fori_loop(0, ROWS // 8, convert, 0, unroll=2)

    def natural(a, t, r):
        return nat[a, t, pl.ds(pl.multiple_of(8 + PAD + r.start, 8), 8), :]

    for tile, count in ((1, 2), (0, 4)):
        shifted = lambda a, t, r, tile=tile: natural(4 * tile + a, t, r)
        pack_fine(shifted, count, right_pack.at[pl.ds(tile, 1)], left_pack.at[pl.ds(tile, 1)], lane, ROWS)
        copies.append(send(right_pack.at[tile], cols.at[0, tile], (i, right)))
        copies.append(send(left_pack.at[tile], cols.at[1, tile], (i, left)))
    copies.append(send(right_pack.at[:, LOW, :], corners.at[0], (down, right)))
    copies.append(send(left_pack.at[:, LOW, :], corners.at[1], (down, left)))
    copies.append(send(right_pack.at[:, TOP, :], corners.at[2], (up, right)))
    copies.append(send(left_pack.at[:, TOP, :], corners.at[3], (up, left)))
    zero = jnp.zeros((8, 128), F32)
    for ch in range(3):
        for t in range(3):
            for r in (0, 8, 16, NAT - 24, NAT - 16, NAT - 8):
                va[ch, t, r : r + 8, :] = zero
    deal_sources(nat, va, 8 + PAD, ROWS // 8, (0, 1))
    for copy in copies:
        copy.wait()

    for t in range(2):
        c = slice(128 * t, 128 * t + 128)
        for slot, rows in ((0, ABOVE), (1, BELOW)):
            for a in range(3):
                nat[a, t, rows, :] = srows[slot, a, :, c]
            for a in range(2):
                nat[3 + a, t, rows, :] = crows[slot, a, :, c].astype(F32)
            nat[5, t, rows, :] = labrows[slot, :, c].astype(F32)
    unpack_columns(nat, 6, cols, corners, lane)
    deal_sources(nat, va, 8 + PAD - HALO, HALO // 8, (0, 1, 2))
    deal_sources(nat, va, 8 + PAD, ROWS // 8, (2,))
    deal_sources(nat, va, 8 + PAD + ROWS, HALO // 8, (0, 1, 2))
    fine_operator(nat, va, fxp, fyp, sp, wt, dg, lfx, lfy, lnat, where)
    level_weights(lfx, lfy, lw, ld, li, lwhere)

    field, other = fine_smooth(va, vb, sp, wt, True)
    for cycle in range(2):
        fine_residual_to_level(field, sp, wt, dg, lsrc)
        level_down(lsrc, li, ld, lw, lsp, fa, fb, lnat, lev, lpr, lpl, g)
        got = [ref.at[cycle] for ref in (vrows, vcols, vcorn, lrows, lcols, lcorn, one, two, three)]

        def field_ready(field=field, cycle=cycle):
            field_out(field, nat, vpr, vpl)
            if cycle == 0:
                for copy in table_loads:
                    copy.wait()

        def with_halos(got=got):
            level_halos(lev, got[3], got[4], got[5], lnat, lfx, lfy, lw, ld, li, lwhere)
            fine_halos(got[0], got[1], got[2], nat)

        coarse_solve(
            n_row, n_col, (i, j, up, down, left, right), send, g, s_cols, s_ext, t_back, row_eig, col_eig,
            nat, vpr, vpl, lev, lpr, lpl, *got, mine, full, spec, back, corr, field_ready, with_halos,
        )
        level = level_up(corr, lnat, lnc, lw, li, lsp, fa, fb, lwhere)
        fine_up(level, nat, va, where)
        field, other = fine_smooth(va, vb, sp, wt, False)
        if cycle == 0:
            field, other = fine_smooth(field, other, sp, wt, False)

    def solution_rows(m, carry):
        ks = (2 * m, 2 * m + 1)
        fields = [[field[ch, t, rows8(k + 1), :] for t in range(3)] for k in ks for ch in range(3)]
        for n, tiles in enumerate(undealt(fields, lane)):
            for t, x in enumerate(tiles):
                nat[n % 3, t, pl.ds(8 + ks[n // 3], 8, stride=K), :] = x
        return carry

    lax.fori_loop(0, K // 2, solution_rows, 0)
    stores = []

    def store(first, ref):
        for a in range(3):
            for t in range(2):
                out = ref.at[a, :, pl.ds(128 * t, 128)]
                copy = pltpu.make_async_copy(nat.at[first + a, t, MID, :], out, copy_sems.at[len(stores)])
                copy.start()
                stores.append(copy)

    store(0, solution_out)
    fields = []

    def emit(k, ch, here, total):
        fields.append(
            [dg[t, rows8(k), :] * (sp[ch, t, rows8(k), :] - here[t] + total[t]) for t in range(3)]
        )

    def finish(m):
        for n, tiles in enumerate(undealt(fields, lane)):
            for t, x in enumerate(tiles):
                nat[3 + n % 3, t, pl.ds(8 + 2 * m + n // 3, 8, stride=K), :] = x
        fields.clear()

    stencil_pass(field, wt, emit, 2, finish)
    store(3, residual_out)
    for copy in stores:
        copy.wait()


@functools.lru_cache(maxsize=None)
def tables(n_row, n_col):
    def sines(n):
        k = np.arange(1, n + 1)
        return math.sqrt(2.0 / (n + 1)) * np.sin(np.pi * ((k[:, None] * k[None, :]) % (2 * (n + 1))) / (n + 1))

    def eig(n):
        return 2.0 - 2.0 * np.cos(np.pi * np.arange(1, n + 1) / (n + 1))

    nr, nc = n_row * CROWS, n_col * CCOLS
    rows, cols = sines(nr), sines(nc)
    s_cols = np.zeros((n_col, 128, 128))
    t_back = np.zeros((n_col, 128, 128))
    col_eig = np.ones((n_col, 128))
    lane = np.arange(128)
    for j in range(n_col):
        own = slice(CCOLS * j, CCOLS * j + CCOLS)
        s_cols[j, :nc, :CCOLS] = cols[:, own]
        col_eig[j, : 3 * CCOLS] = np.tile(eig(nc)[own], 3)
        c = LCOLS * j + lane - LHALO
        ok = (c >= 0) & (c < n_col * LCOLS) & (lane < 96)
        t_back[j, :nc, ok] = cols[:, c[ok] // 4].T
    s_ext = np.zeros((nr + 16, nr))
    s_ext[8 : 8 + nr] = rows
    row_eig = np.repeat(eig(nr)[:, None], 128, axis=1)
    return tuple(x.astype(np.float32) for x in (s_cols, s_ext, t_back, row_eig, col_eig))


def shape(*dims, dtype=F32):
    return jax.ShapeDtypeStruct(dims, dtype)


IN_VMEM = pl.BlockSpec(memory_space=pltpu.VMEM)
IN_ANY = pl.BlockSpec(memory_space=pl.ANY)


def solution(mesh):
    n_row, n_col = mesh.shape["row"], mesh.shape["col"]

    def vmem(*dims, dtype=F32):
        return pltpu.VMEM(dims, dtype)

    n_copies = 14 + 2 * (2 * (n_col - 1) + (n_row - 1) + 16)
    scratch = [
        vmem(2, ROWS, COLS, dtype=jnp.int32), vmem(ROWS, COLS, dtype=jnp.int32),
        vmem(2, ROWS, 128), vmem(2, ROWS, 128),
        vmem(2, 3, HALO, COLS), vmem(2, 2, HALO, COLS, dtype=jnp.int32), vmem(2, HALO, COLS, dtype=jnp.int32),
        vmem(2, 2, ROWS, 128), vmem(4, 2, HALO, 128),
        vmem(6, 3, NAT, 128), vmem(3, K * 8, 128), vmem(3, (K + 1) * 8, 128),
        vmem(3, 3, K * 8, 128), vmem(4, 3, K * 8, 128), vmem(3, K * 8, 128),
        vmem(3, 3, (K + 2) * 8, 128), vmem(3, 3, (K + 2) * 8, 128),
        vmem(ROWS, 128), vmem(ROWS, 128),
        vmem(3, KL * 8, 128), vmem(KL * 8, 128), vmem((KL + 1) * 8, 128),
        vmem(4, KL * 8, 128), vmem(KL * 8, 128), vmem(KL * 8, 128), vmem(3, KL * 8, 128),
        vmem(3, (KL + 2) * 8, 128), vmem(3, (KL + 2) * 8, 128),
        vmem(11, LNAT, 128), vmem(3, LNAT, 128), vmem(8, LROWS, 128),
        vmem(LROWS, 128), vmem(LROWS, 128), vmem(CROWS // 2, 128),
        vmem(2, n_col, CROWS // 2, 128), vmem(2, n_row, CROWS // 2, 128), vmem(2, n_col, BROWS // 2, 128),
        vmem(CROWS // 2, 128), vmem(n_row * CROWS, 128), vmem(n_row * CROWS, 128),
        vmem(BROWS // 2, 128), vmem(3, BROWS, 128),
        vmem(2, 2, 3, 3, HALO, 128), vmem(2, 2, ROWS, 128), vmem(2, 4, HALO, 128),
        vmem(2, 2, 8, LHALO, 128), vmem(2, 2, LROWS, 128), vmem(2, 4, LHALO, 128),
        vmem(128, 128), vmem(n_row * CROWS + 16, n_row * CROWS), vmem(128, 128),
        vmem(n_row * CROWS, 128), vmem(n_col, 128),
        pltpu.SemaphoreType.DMA((12,)), pltpu.SemaphoreType.DMA((5,)),
        pltpu.SemaphoreType.DMA((n_copies,)), pltpu.SemaphoreType.DMA((n_copies,)),
    ]
    call = pl.pallas_call(
        functools.partial(kernel, n_row, n_col),
        out_shape=[shape(3, ROWS, COLS)] * 2,
        in_specs=[IN_ANY] * 8,
        out_specs=[IN_ANY] * 2,
        scratch_shapes=scratch,
        compiler_params=pltpu.CompilerParams(collective_id=0, has_side_effects=True, vmem_limit_bytes=VMEM_LIMIT),
    )
    consts = tables(n_row, n_col)

    def local(sources, edge_codes, seam_labels):
        return tuple(call(sources, edge_codes, seam_labels, *consts))

    spec = P(None, "row", "col")
    return jax.shard_map(
        local, mesh=mesh, in_specs=(spec, spec, P("row", "col")), out_specs=(spec, spec), check_vma=False
    )
```

```python
import functools
import math

import jax
import jax.numpy as jnp
import numpy as np
from jax import lax
from jax.experimental import pallas as pl
from jax.experimental.pallas import tpu as pltpu
from jax.sharding import PartitionSpec as P

SWEEPS = 4
SCREEN = 2e-05
SEAM = 0.2
COARSE_SCALE = 0.0625
F32 = jnp.float32
MESH = pl.DeviceIdType.MESH
HIGHEST = lax.Precision.HIGHEST

ROWS, COLS = 512, 256
PAD = 48
HALO = 32
K = (ROWS + 2 * PAD) // 8
NAT = 8 + ROWS + 2 * PAD + 8
LROWS, LCOLS = 128, 64
LPAD = PAD // 4
LHALO = 16
KL = (LROWS + 2 * LPAD) // 8
LNAT = LROWS + 2 * LHALO
CROWS, CCOLS = 32, 16
BROWS = CROWS + 16
VMEM_LIMIT = 62 * 1024 * 1024


def chebyshev_weight(sweep_index):
    return 1.0 / (1.25 + 0.75 * math.cos(math.pi * (2 * sweep_index + 1) / (2 * SWEEPS)))


def lane_iota():
    return lax.broadcasted_iota(jnp.int32, (8, 128), 1)


def sub_iota():
    return lax.broadcasted_iota(jnp.int32, (8, 128), 0)


def lroll(x, shift):
    shift = shift % 128
    return x if shift == 0 else pltpu.roll(x, shift, 1)


def rows8(k):
    return pl.ds(pl.multiple_of(k * 8, 8), 8)


def lanes_take(x, idx):
    return jnp.take_along_axis(x, idx, axis=1)


def left_of(tiles, lane):
    rolled = [lroll(x, 1) for x in tiles]
    return [jnp.where(lane == 0, rolled[(t + 2) % 3], rolled[t]) for t in range(3)]


def set_pads(ref, lead, count):
    last = ref[lead + (rows8(count), slice(None))]
    first = ref[lead + (rows8(1), slice(None))]
    ref[lead + (rows8(0), slice(None))] = pltpu.roll(last, 1, 0)
    ref[lead + (rows8(count + 1), slice(None))] = pltpu.roll(first, 7, 0)


def pack_fine(tile_of, n_arrays, right, left, lane, rows):
    def body(i, carry):
        r = rows8(i)
        for first in range(0, n_arrays, 4):
            out_r = out_l = jnp.zeros((8, 128), F32)
            for a in range(first, min(first + 4, n_arrays)):
                g = a - first
                here = (lane >= 32 * g) & (lane < 32 * g + 32)
                out_r = jnp.where(here, lroll(tile_of(a, 1, r), 32 * g - 96), out_r)
                out_l = jnp.where(here, lroll(tile_of(a, 0, r), 32 * g), out_l)
            right[first // 4, r, :] = out_r
            left[first // 4, r, :] = out_l
        return carry

    lax.fori_loop(0, rows // 8, body, 0)


def unpack_fine(nat, n_arrays, at, count, from_left, from_right, lane):
    def body(i, carry):
        src = rows8(i)
        dst = pl.ds(pl.multiple_of(at + i * 8, 8), 8)
        for a in range(n_arrays):
            g = a % 4
            l = lroll(from_left[a // 4, src, :], 96 - 32 * g)
            r = lroll(from_right[a // 4, src, :], -32 * g)
            nat[a, 2, dst, :] = jnp.where(lane < 32, r, jnp.where(lane >= 96, l, 0.0))
        return carry

    lax.fori_loop(0, count, body, 0)


def zero_ends(nat, n_arrays):
    zero = jnp.zeros((8, 128), F32)
    for a in range(n_arrays):
        for t in range(3):
            for r in (0, 8, 16, NAT - 24, NAT - 16, NAT - 8):
                nat[a, t, r : r + 8, :] = zero


def unpack_columns(nat, n_arrays, cols, corners, lane):
    unpack_fine(nat, n_arrays, 8 + PAD, ROWS // 8, cols.at[0], cols.at[1], lane)
    unpack_fine(nat, n_arrays, 8 + PAD - HALO, HALO // 8, corners.at[0], corners.at[1], lane)
    unpack_fine(nat, n_arrays, 8 + PAD + ROWS, HALO // 8, corners.at[2], corners.at[3], lane)


CPAD = 64
EDGE, EDGE_RIGHT, EDGE_LEFT = 11, 96, 21


def pack_field(nat, right, left):
    lane = lane_iota()

    def body(i, carry):
        r = pl.ds(pl.multiple_of(8 + PAD + i * 8, 8), 8)
        out_r = out_l = jnp.zeros((8, 128), F32)
        for q in range(9):
            x = nat[q // 3, q % 3, r, :]
            here = (lane >= EDGE * q) & (lane < EDGE * q + EDGE)
            out_r = jnp.where(here, lroll(x, EDGE * q - EDGE_RIGHT), out_r)
            out_l = jnp.where(here, lroll(x, EDGE * q - EDGE_LEFT), out_l)
        right[rows8(i), :] = out_r
        left[rows8(i), :] = out_l
        return carry

    lax.fori_loop(0, ROWS // 8, body, 0, unroll=2)


def unpack_field(nat, at, count, own, from_left, from_right):
    lane = lane_iota()

    def body(i, carry):
        dst = pl.ds(pl.multiple_of(at + i * 8, 8), 8)
        l, r = from_left[rows8(i), :], from_right[rows8(i), :]
        for ch in range(3):
            for t in range(3):
                p = 3 * lane + t
                u = (t + 1) % 3
                a = lroll(l, EDGE_RIGHT - (86 if u == 0 else 85) - EDGE * (3 * ch + u))
                u = (t + 2) % 3
                b = lroll(r, EDGE_LEFT + (86 if u == 2 else 85) - EDGE * (3 * ch + u))
                x = jnp.where((p >= CPAD - HALO) & (p < CPAD), a, own(ch, t, i, dst))
                x = jnp.where((p >= CPAD + COLS) & (p < CPAD + COLS + HALO), b, x)
                nat[ch, t, dst, :] = x
        return carry

    lax.fori_loop(0, count, body, 0, unroll=2)


def dealt(fields, lane):
    out = [[] for _ in fields]
    for t in range(3):
        p = 3 * lane + t
        idx = (p - CPAD) % 128
        for x, y in zip(fields, out):
            got = [lanes_take(part, idx) for part in x]
            y.append(jnp.where((p < 64) | (p >= 320), got[2], jnp.where(p < 192, got[0], got[1])))
    return out


def deal_sources(nat, out, at, count, parts):
    lane = lane_iota()

    def body(i, carry):
        r = pl.ds(pl.multiple_of(at + 8 * i, 8), 8)
        for t in range(3):
            p = 3 * lane + t
            idx = (p - CPAD) % 128
            for ch in range(3):
                got = {n: lanes_take(nat[ch, n, r, :], idx) for n in parts}
                x = jnp.where(p < 192, got[0], got[1]) if 0 in got else out[ch, t, r, :]
                out[ch, t, r, :] = jnp.where((p < 64) | (p >= 320), got[2], x) if 2 in got else x
        return carry

    lax.fori_loop(0, count, body, 0, unroll=2)


def undealt(fields, lane):
    out = [[] for _ in fields]
    for t in range(2):
        p = lane + (128 * t + CPAD)
        idx = p // 3
        for x, y in zip(fields, out):
            got = [lanes_take(part, idx) for part in x]
            y.append(jnp.where(p % 3 == 0, got[0], jnp.where(p % 3 == 1, got[1], got[2])))
    return out


def natural_place(k, t, lane, sub, row0, col0):
    row = row0 - PAD + sub * K + k
    if t < 2:
        return row, lane + (col0 + 128 * t)
    return row, jnp.where(lane < 64, lane + (col0 + 256), lane + (col0 - 128))


def fine_inside(k, t, lane, sub, row0, col0, n_rows, n_cols):
    row = row0 - PAD + sub * K + k
    col = 3 * lane + (t - CPAD + col0)
    return (row >= 0) & (row < n_rows) & (col >= 0) & (col < n_cols)


def level_inside(k, lane, sub, row0, col0, n_rows, n_cols):
    row = row0 - LPAD + sub * KL + k
    col = lane - LHALO + col0
    return (row >= 0) & (row < n_rows) & (col >= 0) & (col < n_cols) & (lane < 96)


def stencil_pass(v, wt, emit, unroll, end=None):
    def row(k):
        w = [[wt[n, t, rows8(k), :] for t in range(3)] for n in range(4)]
        for ch in range(3):
            here = [v[ch, t, rows8(k + 1), :] for t in range(3)]
            left = [lroll(here[2], 1), here[0], here[1]]
            right = [here[1], here[2], lroll(here[0], 127)]
            total = []
            for t in range(3):
                x = w[2][t] * v[ch, t, rows8(k), :] + w[3][t] * v[ch, t, rows8(k + 2), :]
                total.append(x + (w[0][t] * left[t] + w[1][t] * right[t]))
            emit(k, ch, here, total)

    def body(m, carry):
        for q in range(unroll):
            row(unroll * m + q)
        if end is not None:
            end(m)
        return carry

    lax.fori_loop(0, K // unroll, body, 0)


def fine_pads(v):
    for ch in range(3):
        for t in range(3):
            set_pads(v, (ch, t), K)


def fine_sweep(vin, vout, sp, wt, omega):
    def emit(k, ch, here, total):
        for t in range(3):
            new = sp[ch, t, rows8(k), :] + total[t]
            vout[ch, t, rows8(k + 1), :] = (1.0 - omega) * here[t] + omega * new

    stencil_pass(vin, wt, emit, 4)
    fine_pads(vout)


def fine_first(vout, sp):
    omega = chebyshev_weight(0)

    def body(k, carry):
        for ch in range(3):
            for t in range(3):
                vout[ch, t, rows8(k + 1), :] = omega * sp[ch, t, rows8(k), :]
        return carry

    lax.fori_loop(0, K, body, 0)
    fine_pads(vout)


def fine_smooth(va, vb, sp, wt, from_zero):
    bufs = [va, vb]
    at = 0
    for i in range(SWEEPS):
        if i == 0 and from_zero:
            fine_first(va, sp)
            continue
        fine_sweep(bufs[at], bufs[1 - at], sp, wt, chebyshev_weight(i))
        at = 1 - at
    return bufs[at], bufs[1 - at]


def pick(x, lane):
    got = [lanes_take(y, jnp.minimum((4 * lane) // 3, 127)) for y in x]
    return jnp.where(lane % 3 == 0, got[0], jnp.where(lane % 3 == 1, got[1], got[2]))


def to_level(x, lane):
    after = [lroll(y, 127) for y in x]
    mid, first = x[1] + x[2], after[0] + after[1]
    sums = [x[0] + mid + after[0], mid + first, x[2] + first + after[2]]
    return pick(sums, lane)


def fine_residual_to_level(v, sp, wt, dg, lsrc):
    lane = lane_iota()
    acc = {}

    def emit(k, ch, here, total):
        res = [dg[t, rows8(k), :] * (sp[ch, t, rows8(k), :] - here[t] + total[t]) for t in range(3)]
        acc[ch] = [a + b for a, b in zip(acc[ch], res)] if ch in acc else res

    def end(m):
        for ch in range(3):
            lsrc[ch, rows8(m), :] = to_level(acc.pop(ch), lane) * 0.0625

    stencil_pass(v, wt, emit, 4, end)


def level_weights(fx, fy, lw, ld, li, where):
    lane, sub = lane_iota(), sub_iota()
    fy[rows8(KL), :] = pltpu.roll(fy[rows8(0), :], 7, 0)

    def body(k, carry):
        left, up, down = fx[rows8(k), :], fy[rows8(k), :], fy[rows8(k + 1), :]
        right = lroll(left, 127)
        diag = SCREEN + left + right + up + down
        inv = jnp.where(level_inside(k, lane, sub, *where), 1.0 / diag, 0.0)
        ld[rows8(k), :] = diag
        li[rows8(k), :] = inv
        for n, face in enumerate((left, right, up, down)):
            lw[n, rows8(k), :] = face * inv
        return carry

    lax.fori_loop(0, KL, body, 0)


def level_neighbours(f, lw, k, ch):
    here = f[ch, rows8(k + 1), :]
    total = lw[0, rows8(k), :] * lroll(here, 1) + lw[1, rows8(k), :] * lroll(here, 127)
    return here, total + lw[2, rows8(k), :] * f[ch, rows8(k), :] + lw[3, rows8(k), :] * f[ch, rows8(k + 2), :]


def level_pads(f):
    for ch in range(3):
        set_pads(f, (ch,), KL)


def level_smooth(fa, fb, lsp, lw, from_zero):
    bufs = [fa, fb]
    at = 0
    for i in range(SWEEPS):
        omega = chebyshev_weight(i)
        src, dst = bufs[at], bufs[1 - at]
        if i == 0 and from_zero:

            def first(k, carry):
                for ch in range(3):
                    src[ch, rows8(k + 1), :] = omega * lsp[ch, rows8(k), :]
                return carry

            lax.fori_loop(0, KL, first, 0, unroll=True)
            level_pads(src)
            continue

        def body(k, carry):
            for ch in range(3):
                here, total = level_neighbours(src, lw, k, ch)
                dst[ch, rows8(k + 1), :] = (1.0 - omega) * here + omega * (lsp[ch, rows8(k), :] + total)
            return carry

        lax.fori_loop(0, KL, body, 0, unroll=True)
        level_pads(dst)
        at = 1 - at
    return bufs[at]


def level_down(lsrc, li, ld, lw, lsp, fa, fb, lnat, lev, lpr, lpl, g):
    lane = lane_iota()

    def scale(k, carry):
        for ch in range(3):
            lsp[ch, rows8(k), :] = lsrc[ch, rows8(k), :] * li[rows8(k), :]
        return carry

    lax.fori_loop(0, KL, scale, 0, unroll=True)
    f = level_smooth(fa, fb, lsp, lw, True)

    def out(k, carry):
        at = pl.ds(LHALO - LPAD + k, 8, stride=KL)
        for ch in range(3):
            here, total = level_neighbours(f, lw, k, ch)
            lnat[8 + ch, at, :] = ld[rows8(k), :] * (lsp[ch, rows8(k), :] - here + total)
            lnat[ch, at, :] = here
            lnat[3 + ch, at, :] = lsrc[ch, rows8(k), :]
        return carry

    lax.fori_loop(0, KL, out, 0, unroll=True)

    def copy(i, carry):
        src = pl.ds(pl.multiple_of(LHALO + i * 8, 8), 8)
        right = left = jnp.zeros((8, 128), F32)
        for a in range(8):
            x = lnat[a, src, :]
            lev[a, rows8(i), :] = x
            here = (lane >= 16 * a) & (lane < 16 * a + 16)
            right = jnp.where(here, lroll(x, 16 * a - 64), right)
            left = jnp.where(here, lroll(x, 16 * a - 16), left)
        lpr[rows8(i), :] = right
        lpl[rows8(i), :] = left
        return carry

    lax.fori_loop(0, LROWS // 8, copy, 0)
    idx = (LHALO + 4 * lane) % 128
    parts = []
    for i in range(CROWS // 8):
        total = jnp.zeros((8, 128), F32)
        for ch in range(3):
            x = sum(lnat[8 + ch, pl.ds(LHALO + 32 * i + q, 8, stride=4), :] for q in range(4))
            x = x + lroll(x, 127)
            x = x + lroll(x, 126)
            x = jnp.where(lane < CCOLS, lanes_take(x, idx), 0.0) * 0.0625
            total = total + lroll(x, CCOLS * ch)
        parts.append(total)
    half = len(parts) // 2
    for i in range(half):
        g[i * 8 : i * 8 + 8, :] = parts[i] + lroll(parts[half + i], 64)


def level_halos(lev, lrows, lcols, lcorn, lnat, fx, fy, lw, ld, li, where):
    lane = lane_iota()

    def place(dst_row, count, own, left, right):
        def body(i, carry):
            dst = pl.ds(pl.multiple_of(dst_row + i * 8, 8), 8)
            l, r = left(rows8(i)), right(rows8(i))
            for a in range(8):
                x = jnp.where((lane >= 80) & (lane < 96), lroll(r, 80 - 16 * a), 0.0)
                x = jnp.where((lane >= 16) & (lane < 80), own(a, rows8(i)), x)
                lnat[a, dst, :] = jnp.where(lane < 16, lroll(l, -16 * a), x)
            return carry

        lax.fori_loop(0, count, body, 0)

    place(0, LHALO // 8, lambda a, r: lrows[0, a, r, :], lambda r: lcorn[0, r, :], lambda r: lcorn[1, r, :])
    place(LHALO, LROWS // 8, lambda a, r: lev[a, r, :], lambda r: lcols[0, r, :], lambda r: lcols[1, r, :])
    place(LHALO + LROWS, LHALO // 8, lambda a, r: lrows[1, a, r, :], lambda r: lcorn[2, r, :], lambda r: lcorn[3, r, :])
    def faces(k, carry):
        at = pl.ds(LHALO - LPAD + k, 8, stride=KL)
        fx[rows8(k), :] = lnat[6, at, :]
        fy[rows8(k), :] = lnat[7, at, :]
        return carry

    lax.fori_loop(0, KL, faces, 0)
    level_weights(fx, fy, lw, ld, li, where)


def level_up(corr, lnat, lnc, lw, li, lsp, fa, fb, where):
    lane, sub = lane_iota(), sub_iota()
    for ch in range(3):
        for h in range(LNAT // 32):
            x = corr[ch, 4 + 8 * h : 12 + 8 * h, :]
            for q in range(4):
                lnc[ch, pl.ds(32 * h + q, 8, stride=4), :] = x

    def fields(k, carry):
        at = pl.ds(LHALO - LPAD + k, 8, stride=KL)
        inside = level_inside(k, lane, sub, *where)
        inv = li[rows8(k), :]
        for ch in range(3):
            fa[ch, rows8(k + 1), :] = jnp.where(inside, lnat[ch, at, :] + lnc[ch, at, :], 0.0)
            lsp[ch, rows8(k), :] = lnat[3 + ch, at, :] * inv
        return carry

    lax.fori_loop(0, KL, fields, 0, unroll=True)
    level_pads(fa)
    return level_smooth(fa, fb, lsp, lw, False)


def fine_halos(vrows, vcols, vcorn, nat):
    unpack_field(nat, 8 + PAD, ROWS // 8, lambda ch, t, i, r: nat[ch, t, r, :], vcols.at[0], vcols.at[1])
    for slot, at in ((0, 8 + PAD - HALO), (1, 8 + PAD + ROWS)):
        own = lambda ch, t, i, r, slot=slot: vrows[slot, ch, t, rows8(i), :]
        unpack_field(nat, at, HALO // 8, own, vcorn.at[2 * slot], vcorn.at[2 * slot + 1])


def fine_up(field, nat, va, where):
    lane, sub = lane_iota(), sub_iota()

    def body(kl, carry):
        for t in range(3):
            idx = jnp.minimum((3 * lane + t) // 4, 127)
            inside = [fine_inside(kl * 4 + q, t, lane, sub, *where) for q in range(4)]
            for ch in range(3):
                add = lanes_take(field[ch, rows8(kl + 1), :], idx)
                for q in range(4):
                    x = nat[ch, t, pl.ds(8 + kl * 4 + q, 8, stride=K), :] + add
                    va[ch, t, rows8(kl * 4 + q + 1), :] = jnp.where(inside[q], x, 0.0)
        return carry

    lax.fori_loop(0, KL, body, 0)
    fine_pads(va)


def field_out(field, nat, vpr, vpl):
    def body(m, carry):
        for q in range(2):
            k = 2 * m + q
            for ch in range(3):
                for t in range(3):
                    nat[ch, t, pl.ds(8 + k, 8, stride=K), :] = field[ch, t, rows8(k + 1), :]
        return carry

    lax.fori_loop(0, K // 2, body, 0)
    pack_field(nat, vpr, vpl)


def positions(n_row, n_col):
    i, j = lax.axis_index("row"), lax.axis_index("col")
    fine = (i * ROWS, j * COLS, n_row * ROWS, n_col * COLS)
    level = (i * LROWS, j * LCOLS, n_row * LROWS, n_col * LCOLS)
    return fine, level


TOP, LOW = pl.ds(0, HALO), pl.ds(ROWS - HALO, HALO)
LTOP, LLOW = pl.ds(0, LHALO), pl.ds(LROWS - LHALO, LHALO)
MID = pl.ds(8 + PAD, ROWS)
FIRST, LAST = pl.ds(8 + PAD, HALO), pl.ds(8 + PAD + ROWS - HALO, HALO)
ABOVE, BELOW = pl.ds(8 + PAD - HALO, HALO), pl.ds(8 + PAD + ROWS, HALO)


class Sender:
    def __init__(self, send_sems, recv_sems):
        self.send_sems, self.recv_sems, self.count = send_sems, recv_sems, 0

    def __call__(self, src, dst, device):
        n = self.count
        self.count += 1
        copy = pltpu.make_async_remote_copy(
            src_ref=src, dst_ref=dst, send_sem=self.send_sems.at[n], recv_sem=self.recv_sems.at[n],
            device_id=device, device_id_type=MESH,
        )
        copy.start()
        return copy


def fine_operator(nat, dealt_src, fxp, fyp, sp, wt, dg, lfx, lfy, lnat, where):
    lane, sub = lane_iota(), sub_iota()

    def edge(code, a, b):
        return jnp.exp2(code * 0.25 - 2.0) * jnp.where(a != b, SEAM, 1.0)

    def faces(k, carry):
        at, above = pl.ds(8 + k, 8, stride=K), pl.ds(7 + k, 8, stride=K)
        code = left_of([nat[3, t, at, :] for t in range(3)], lane)
        label = [nat[5, t, at, :] for t in range(3)]
        beside = left_of(label, lane)
        fx, fy = [], []
        for t in range(3):
            row, col = natural_place(k, t, lane, sub, where[0], where[1])
            inner = edge(code[t], beside[t], label[t])
            fx.append(jnp.where((col >= 1) & (col < where[3]), inner, 1.0))
            inner = edge(nat[4, t, above, :], nat[5, t, above, :], label[t])
            fy.append(jnp.where((row >= 1) & (row < where[2]), inner, 1.0))
        for ref, tiles in zip((fxp, fyp), dealt([fx, fy], lane)):
            for t, x in enumerate(tiles):
                ref[t, rows8(k), :] = x
        return carry

    lax.fori_loop(0, K, faces, 0, unroll=2)
    for t in range(3):
        fyp[t, rows8(K), :] = pltpu.roll(fyp[t, rows8(0), :], 7, 0)

    def weights(k, carry):
        left = [fxp[t, rows8(k), :] for t in range(3)]
        right = [left[1], left[2], lroll(left[0], 127)]
        at = pl.ds(8 + k, 8, stride=K)
        scale = []
        for t in range(3):
            up, down = fyp[t, rows8(k), :], fyp[t, rows8(k + 1), :]
            diag = SCREEN + left[t] + right[t] + up + down
            inv = jnp.where(fine_inside(k, t, lane, sub, *where), 1.0 / diag, 0.0)
            scale.append(inv)
            dg[t, rows8(k), :] = diag
            for n, face in enumerate((left[t], right[t], up, down)):
                wt[n, t, rows8(k), :] = face * inv
        for ch in range(3):
            for t in range(3):
                sp[ch, t, rows8(k), :] = dealt_src[ch, t, at, :] * scale[t]
        return carry

    lax.fori_loop(0, K, weights, 0, unroll=2)

    def level_faces(kl, carry):
        rows = [sum(fxp[t, rows8(kl * 4 + q), :] for q in range(4)) for t in range(3)]
        x = pick(rows, lane) * 0.0625
        y = to_level([fyp[t, rows8(kl * 4), :] for t in range(3)], lane) * 0.0625
        at = pl.ds(LHALO - LPAD + kl, 8, stride=KL)
        lfx[rows8(kl), :] = x
        lfy[rows8(kl), :] = y
        lnat[6, at, :] = x
        lnat[7, at, :] = y
        return carry

    lax.fori_loop(0, KL, level_faces, 0)


def coarse_solve(
    n_row, n_col, place, send, g, s_cols, s_ext, t_back, row_eig, col_eig, nat, vpr, vpl, lev, lpr, lpl,
    vrows, vcols, vcorn, lrows, lcols, lcorn, one, two, three, mine, full, spec, back, corr,
    field_ready, with_halos,
):
    i, j, up, down, left, right = place
    n_modes = n_row * CROWS
    lane = lane_iota()

    first = [send(g, one.at[j], (i, lax.rem(j + d, n_col))) for d in range(1, n_col)]
    one[j] = g[...]
    halos = [
        send(lpr, lcols.at[0], (i, right)),
        send(lpl, lcols.at[1], (i, left)),
        send(lev.at[:, LTOP, :], lrows.at[1], (up, j)),
        send(lev.at[:, LLOW, :], lrows.at[0], (down, j)),
        send(lpr.at[LLOW, :], lcorn.at[0], (down, right)),
        send(lpl.at[LLOW, :], lcorn.at[1], (down, left)),
        send(lpr.at[LTOP, :], lcorn.at[2], (up, right)),
        send(lpl.at[LTOP, :], lcorn.at[3], (up, left)),
    ]
    field_ready()
    for copy in first:
        copy.wait()

    def placed(ref, n_rows):
        out = []
        for ch in range(3):
            parts = []
            for r in range(n_rows // 8):
                x = jnp.zeros((8, 128), F32)
                for p in range(n_col):
                    here = (lane >= CCOLS * p) & (lane < CCOLS * p + CCOLS)
                    low_half = r * 16 >= n_rows
                    row = r * 8 - n_rows // 2 if low_half else r * 8
                    y = lroll(ref[p, row : row + 8, :], CCOLS * (p - ch) - (64 if low_half else 0))
                    x = jnp.where(here, y, x)
                parts.append(x)
            out.append(jnp.concatenate(parts, axis=0))
        return out

    x = jnp.concatenate(placed(one, CROWS), axis=0)
    x = jnp.dot(x, s_cols[...], precision=HIGHEST, preferred_element_type=F32)
    total = lax.slice_in_dim(x, 0, CROWS)
    for ch in (1, 2):
        total = total + pltpu.roll(lax.slice_in_dim(x, CROWS * ch, CROWS * ch + CROWS), CCOLS * ch, 1)
    half = CROWS // 2
    total = lax.slice_in_dim(total, 0, half) + pltpu.roll(lax.slice_in_dim(total, half, CROWS), 64, 1)
    mine[...] = total
    second = [send(mine, two.at[i], (lax.rem(i + d, n_row), j)) for d in range(1, n_row)]
    two[i] = total
    halos += [
        send(vpr, vcols.at[0], (i, right)),
        send(vpl, vcols.at[1], (i, left)),
        send(vpr.at[LOW, :], vcorn.at[0], (down, right)),
        send(vpl.at[LOW, :], vcorn.at[1], (down, left)),
        send(vpr.at[TOP, :], vcorn.at[2], (up, right)),
        send(vpl.at[TOP, :], vcorn.at[3], (up, left)),
    ]
    halos += [
        send(nat.at[pl.ds(0, 3), :, FIRST, :], vrows.at[1], (up, j)),
        send(nat.at[pl.ds(0, 3), :, LAST, :], vrows.at[0], (down, j)),
    ]
    for copy in second:
        copy.wait()
    for p in range(n_row):
        for r in range(0, half, 8):
            x = two[p, r : r + 8, :]
            full[p * CROWS + r : p * CROWS + r + 8, :] = x
            full[p * CROWS + half + r : p * CROWS + half + r + 8, :] = lroll(x, 64)
    y = jnp.dot(s_ext[8 : 8 + n_modes, :], full[...], precision=HIGHEST, preferred_element_type=F32)
    eig = SCREEN + COARSE_SCALE * (row_eig[...] + col_eig[pl.ds(j, 1), :])
    spec[...] = y / eig
    rows = s_ext[pl.ds(pl.multiple_of(i * CROWS, CROWS), BROWS), :]
    z = jnp.dot(rows, spec[...], precision=HIGHEST, preferred_element_type=F32)
    half = BROWS // 2
    z = jnp.where(
        lax.broadcasted_iota(jnp.int32, (half, 128), 1) < 64,
        lax.slice_in_dim(z, 0, half), pltpu.roll(lax.slice_in_dim(z, half, BROWS), 64, 1),
    )
    back[...] = z
    third = [send(back, three.at[j], (i, lax.rem(j + d, n_col))) for d in range(1, n_col)]
    three[j] = z
    for copy in halos:
        copy.wait()
    with_halos()
    for copy in third:
        copy.wait()
    z = jnp.concatenate(placed(three, BROWS), axis=0)
    z = jnp.dot(z, t_back[...], precision=HIGHEST, preferred_element_type=F32)
    for ch in range(3):
        corr[ch] = lax.slice_in_dim(z, BROWS * ch, BROWS * ch + BROWS)


def kernel(n_row, n_col, src, codes, labels, *refs):
    tables_in, solution_out, residual_out = refs[:5], refs[5], refs[6]
    (
        codes_v, labels_v, right_pack, left_pack, srows, crows, labrows, cols, corners,
        nat, fxp, fyp, sp, wt, dg, va, vb, vpr, vpl,
        lsrc, lfx, lfy, lw, ld, li, lsp, fa, fb, lnat, lnc, lev, lpr, lpl, g,
        one, two, three, mine, full, spec, back, corr,
        vrows, vcols, vcorn, lrows, lcols, lcorn,
        s_cols, s_ext, t_back, row_eig, col_eig,
        copy_sems, table_sems, send_sems, recv_sems,
    ) = refs[7:]
    i, j = lax.axis_index("row"), lax.axis_index("col")
    up, down = lax.rem(i + n_row - 1, n_row), lax.rem(i + 1, n_row)
    left, right = lax.rem(j + n_col - 1, n_col), lax.rem(j + 1, n_col)
    where, lwhere = positions(n_row, n_col)
    lane = lane_iota()

    barrier = pltpu.get_barrier_semaphore()
    peers = [(i, lax.rem(j + d, n_col)) for d in range(1, n_col)]
    peers += [(lax.rem(i + d, n_row), j) for d in range(1, n_row)]
    peers += [(r, c) for r in (up, down) for c in (left, right)]
    for peer in peers:
        pl.semaphore_signal(barrier, inc=1, device_id=peer, device_id_type=MESH)

    loads = [pltpu.make_async_copy(codes, codes_v, copy_sems.at[0])]
    loads.append(pltpu.make_async_copy(labels, labels_v, copy_sems.at[1]))
    for a in range(3):
        for t in range(2):
            part = src.at[a, :, pl.ds(128 * t, 128)]
            loads.append(pltpu.make_async_copy(part, nat.at[a, t, MID, :], copy_sems.at[len(loads)]))
    for copy in loads:
        copy.start()
    table_loads = []
    for n, (table, ref) in enumerate(zip(tables_in, (s_cols, s_ext, t_back, row_eig, col_eig))):
        table_loads.append(pltpu.make_async_copy(table.at[j] if n in (0, 2) else table, ref, table_sems.at[n]))
        table_loads[-1].start()
    zero_ends(nat, 6)
    pl.semaphore_wait(barrier, n_col + n_row + 2)
    send = Sender(send_sems, recv_sems)
    copies = []
    for slot, rows, device in ((1, TOP, up), (0, LOW, down)):
        copies.append(send(src.at[:, rows, :], srows.at[slot], (device, j)))
        copies.append(send(codes.at[:, rows, :], crows.at[slot], (device, j)))
        copies.append(send(labels.at[rows, :], labrows.at[slot], (device, j)))
    for copy in loads:
        copy.wait()

    def convert(n, carry):
        r = rows8(n)
        at = pl.ds(pl.multiple_of(8 + PAD + 8 * n, 8), 8)
        for t in range(2):
            c = slice(128 * t, 128 * t + 128)
            nat[3, t, at, :] = codes_v[0, r, c].astype(F32)
            nat[4, t, at, :] = codes_v[1, r, c].astype(F32)
            nat[5, t, at, :] = labels_v[r, c].astype(F32)
        return carry

    lax.fori_loop(0, ROWS // 8, convert, 0, unroll=2)

    def natural(a, t, r):
        return nat[a, t, pl.ds(pl.multiple_of(8 + PAD + r.start, 8), 8), :]

    for tile, count in ((1, 2), (0, 4)):
        shifted = lambda a, t, r, tile=tile: natural(4 * tile + a, t, r)
        pack_fine(shifted, count, right_pack.at[pl.ds(tile, 1)], left_pack.at[pl.ds(tile, 1)], lane, ROWS)
        copies.append(send(right_pack.at[tile], cols.at[0, tile], (i, right)))
        copies.append(send(left_pack.at[tile], cols.at[1, tile], (i, left)))
    copies.append(send(right_pack.at[:, LOW, :], corners.at[0], (down, right)))
    copies.append(send(left_pack.at[:, LOW, :], corners.at[1], (down, left)))
    copies.append(send(right_pack.at[:, TOP, :], corners.at[2], (up, right)))
    copies.append(send(left_pack.at[:, TOP, :], corners.at[3], (up, left)))
    zero = jnp.zeros((8, 128), F32)
    for ch in range(3):
        for t in range(3):
            for r in (0, 8, 16, NAT - 24, NAT - 16, NAT - 8):
                va[ch, t, r : r + 8, :] = zero
    deal_sources(nat, va, 8 + PAD, ROWS // 8, (0, 1))
    for copy in copies:
        copy.wait()

    for t in range(2):
        c = slice(128 * t, 128 * t + 128)
        for slot, rows in ((0, ABOVE), (1, BELOW)):
            for a in range(3):
                nat[a, t, rows, :] = srows[slot, a, :, c]
            for a in range(2):
                nat[3 + a, t, rows, :] = crows[slot, a, :, c].astype(F32)
            nat[5, t, rows, :] = labrows[slot, :, c].astype(F32)
    unpack_columns(nat, 6, cols, corners, lane)
    deal_sources(nat, va, 8 + PAD - HALO, HALO // 8, (0, 1, 2))
    deal_sources(nat, va, 8 + PAD, ROWS // 8, (2,))
    deal_sources(nat, va, 8 + PAD + ROWS, HALO // 8, (0, 1, 2))
    fine_operator(nat, va, fxp, fyp, sp, wt, dg, lfx, lfy, lnat, where)
    level_weights(lfx, lfy, lw, ld, li, lwhere)

    field, other = fine_smooth(va, vb, sp, wt, True)
    for cycle in range(2):
        fine_residual_to_level(field, sp, wt, dg, lsrc)
        level_down(lsrc, li, ld, lw, lsp, fa, fb, lnat, lev, lpr, lpl, g)
        got = [ref.at[cycle] for ref in (vrows, vcols, vcorn, lrows, lcols, lcorn, one, two, three)]

        def field_ready(field=field, cycle=cycle):
            field_out(field, nat, vpr, vpl)
            if cycle == 0:
                for copy in table_loads:
                    copy.wait()

        def with_halos(got=got):
            level_halos(lev, got[3], got[4], got[5], lnat, lfx, lfy, lw, ld, li, lwhere)
            fine_halos(got[0], got[1], got[2], nat)

        coarse_solve(
            n_row, n_col, (i, j, up, down, left, right), send, g, s_cols, s_ext, t_back, row_eig, col_eig,
            nat, vpr, vpl, lev, lpr, lpl, *got, mine, full, spec, back, corr, field_ready, with_halos,
        )
        level = level_up(corr, lnat, lnc, lw, li, lsp, fa, fb, lwhere)
        fine_up(level, nat, va, where)
        field, other = fine_smooth(va, vb, sp, wt, False)
        if cycle == 0:
            field, other = fine_smooth(field, other, sp, wt, False)

    def solution_rows(m, carry):
        ks = (2 * m, 2 * m + 1)
        fields = [[field[ch, t, rows8(k + 1), :] for t in range(3)] for k in ks for ch in range(3)]
        for n, tiles in enumerate(undealt(fields, lane)):
            for t, x in enumerate(tiles):
                nat[n % 3, t, pl.ds(8 + ks[n // 3], 8, stride=K), :] = x
        return carry

    lax.fori_loop(0, K // 2, solution_rows, 0)
    stores = []

    def store(first, ref):
        for a in range(3):
            for t in range(2):
                out = ref.at[a, :, pl.ds(128 * t, 128)]
                copy = pltpu.make_async_copy(nat.at[first + a, t, MID, :], out, copy_sems.at[len(stores)])
                copy.start()
                stores.append(copy)

    store(0, solution_out)
    fields = []

    def emit(k, ch, here, total):
        fields.append(
            [dg[t, rows8(k), :] * (sp[ch, t, rows8(k), :] - here[t] + total[t]) for t in range(3)]
        )

    def finish(m):
        for n, tiles in enumerate(undealt(fields, lane)):
            for t, x in enumerate(tiles):
                nat[3 + n % 3, t, pl.ds(8 + 2 * m + n // 3, 8, stride=K), :] = x
        fields.clear()

    stencil_pass(field, wt, emit, 2, finish)
    store(3, residual_out)
    for copy in stores:
        copy.wait()


@functools.lru_cache(maxsize=None)
def tables(n_row, n_col):
    def sines(n):
        k = np.arange(1, n + 1)
        return math.sqrt(2.0 / (n + 1)) * np.sin(np.pi * ((k[:, None] * k[None, :]) % (2 * (n + 1))) / (n + 1))

    def eig(n):
        return 2.0 - 2.0 * np.cos(np.pi * np.arange(1, n + 1) / (n + 1))

    nr, nc = n_row * CROWS, n_col * CCOLS
    rows, cols = sines(nr), sines(nc)
    s_cols = np.zeros((n_col, 128, 128))
    t_back = np.zeros((n_col, 128, 128))
    col_eig = np.ones((n_col, 128))
    lane = np.arange(128)
    for j in range(n_col):
        own = slice(CCOLS * j, CCOLS * j + CCOLS)
        s_cols[j, :nc, :CCOLS] = cols[:, own]
        col_eig[j, : 3 * CCOLS] = np.tile(eig(nc)[own], 3)
        c = LCOLS * j + lane - LHALO
        ok = (c >= 0) & (c < n_col * LCOLS) & (lane < 96)
        t_back[j, :nc, ok] = cols[:, c[ok] // 4].T
    s_ext = np.zeros((nr + 16, nr))
    s_ext[8 : 8 + nr] = rows
    row_eig = np.repeat(eig(nr)[:, None], 128, axis=1)
    return tuple(x.astype(np.float32) for x in (s_cols, s_ext, t_back, row_eig, col_eig))


def shape(*dims, dtype=F32):
    return jax.ShapeDtypeStruct(dims, dtype)


IN_VMEM = pl.BlockSpec(memory_space=pltpu.VMEM)
IN_ANY = pl.BlockSpec(memory_space=pl.ANY)


def solution(mesh):
    n_row, n_col = mesh.shape["row"], mesh.shape["col"]

    def vmem(*dims, dtype=F32):
        return pltpu.VMEM(dims, dtype)

    n_copies = 14 + 2 * (2 * (n_col - 1) + (n_row - 1) + 16)
    scratch = [
        vmem(2, ROWS, COLS, dtype=jnp.int32), vmem(ROWS, COLS, dtype=jnp.int32),
        vmem(2, ROWS, 128), vmem(2, ROWS, 128),
        vmem(2, 3, HALO, COLS), vmem(2, 2, HALO, COLS, dtype=jnp.int32), vmem(2, HALO, COLS, dtype=jnp.int32),
        vmem(2, 2, ROWS, 128), vmem(4, 2, HALO, 128),
        vmem(6, 3, NAT, 128), vmem(3, K * 8, 128), vmem(3, (K + 1) * 8, 128),
        vmem(3, 3, K * 8, 128), vmem(4, 3, K * 8, 128), vmem(3, K * 8, 128),
        vmem(3, 3, (K + 2) * 8, 128), vmem(3, 3, (K + 2) * 8, 128),
        vmem(ROWS, 128), vmem(ROWS, 128),
        vmem(3, KL * 8, 128), vmem(KL * 8, 128), vmem((KL + 1) * 8, 128),
        vmem(4, KL * 8, 128), vmem(KL * 8, 128), vmem(KL * 8, 128), vmem(3, KL * 8, 128),
        vmem(3, (KL + 2) * 8, 128), vmem(3, (KL + 2) * 8, 128),
        vmem(11, LNAT, 128), vmem(3, LNAT, 128), vmem(8, LROWS, 128),
        vmem(LROWS, 128), vmem(LROWS, 128), vmem(CROWS // 2, 128),
        vmem(2, n_col, CROWS // 2, 128), vmem(2, n_row, CROWS // 2, 128), vmem(2, n_col, BROWS // 2, 128),
        vmem(CROWS // 2, 128), vmem(n_row * CROWS, 128), vmem(n_row * CROWS, 128),
        vmem(BROWS // 2, 128), vmem(3, BROWS, 128),
        vmem(2, 2, 3, 3, HALO, 128), vmem(2, 2, ROWS, 128), vmem(2, 4, HALO, 128),
        vmem(2, 2, 8, LHALO, 128), vmem(2, 2, LROWS, 128), vmem(2, 4, LHALO, 128),
        vmem(128, 128), vmem(n_row * CROWS + 16, n_row * CROWS), vmem(128, 128),
        vmem(n_row * CROWS, 128), vmem(n_col, 128),
        pltpu.SemaphoreType.DMA((12,)), pltpu.SemaphoreType.DMA((5,)),
        pltpu.SemaphoreType.DMA((n_copies,)), pltpu.SemaphoreType.DMA((n_copies,)),
    ]
    call = pl.pallas_call(
        functools.partial(kernel, n_row, n_col),
        out_shape=[shape(3, ROWS, COLS)] * 2,
        in_specs=[IN_ANY] * 8,
        out_specs=[IN_ANY] * 2,
        scratch_shapes=scratch,
        compiler_params=pltpu.CompilerParams(collective_id=0, has_side_effects=True, vmem_limit_bytes=VMEM_LIMIT),
    )
    consts = tables(n_row, n_col)

    def local(sources, edge_codes, seam_labels):
        return tuple(call(sources, edge_codes, seam_labels, *consts))

    spec = P(None, "row", "col")
    return jax.shard_map(
        local, mesh=mesh, in_specs=(spec, spec, P("row", "col")), out_specs=(spec, spec), check_vma=False
    )
```
